32 devices in a mesh: dp: 4 (over x, core), fsdp: 8 (over z, y).
Axes of the slice: x: 2, y: 2, z: 4, core: 2. Of those that a mesh axis runs over, the one named last changes fastest.
Arguments:
- patches_in: bfloat16 [32, 256, 1152], P(('dp', 'fsdp')), may hold values from -6 to 6
- condition: bfloat16 [32, 1152], P(('dp', 'fsdp')), may hold values from -6 to 6
- keep_count: int32 [32], P(('dp', 'fsdp')), may hold values from 48 to 192, as said below
- keep_index: int32 [32, 192], P(('dp', 'fsdp')), may hold values from 0 to 255, as said below
- w_ada: bfloat16 [1152, 6912], P('dp', 'fsdp'), may hold values from -0.1875 to 0.1875
- b_ada: bfloat16 [6912], P(('dp', 'fsdp')), may hold values from -3 to 3
- w_qkv: bfloat16 [1152, 3456], P('dp', 'fsdp'), may hold values from -0.1875 to 0.1875
- qv_bias: bfloat16 [2304], P(('dp', 'fsdp')), may hold values from -3 to 3
- w_proj: bfloat16 [1152, 1152], P('dp', 'fsdp'), may hold values from -1.5 to 1.5
- w_fc1: bfloat16 [1152, 4608], P('dp', 'fsdp'), may hold values from -0.1875 to 0.1875
- fc1_bias: bfloat16 [4608], P(('dp', 'fsdp')), may hold values from -3 to 3
- w_fc2: bfloat16 [4608, 1152], P('dp', 'fsdp'), may hold values from -0.1875 to 0.1875
- out_bias: bfloat16 [2304], P(('dp', 'fsdp')), may hold values from -3 to 3
- cotangent: bfloat16 [32, 192, 1152], P(('dp', 'fsdp')), may hold values from -6 to 6
Outputs:
- block_out: bfloat16 [32, 192, 1152], P(('dp', 'fsdp'))
- grad_patches: float32 [32, 256, 1152], P(('dp', 'fsdp'))
- grad_condition: float32 [32, 1152], P(('dp', 'fsdp'))
- grad_w_ada: float32 [1152, 6912], P('dp', 'fsdp')
- grad_b_ada: float32 [6912], P(('dp', 'fsdp'))
- grad_w_qkv: float32 [1152, 3456], P('dp', 'fsdp')
- grad_qv_bias: float32 [2304], P(('dp', 'fsdp'))
- grad_w_proj: float32 [1152, 1152], P('dp', 'fsdp')
- grad_w_fc1: float32 [1152, 4608], P('dp', 'fsdp')
- grad_fc1_bias: float32 [4608], P(('dp', 'fsdp'))
- grad_w_fc2: float32 [4608, 1152], P('dp', 'fsdp')
- grad_out_bias: float32 [2304], P(('dp', 'fsdp'))
The draws below stay inside these ranges and needn't reach their ends.
Inputs may be any that keep to these rules, and one draw needn't show every extreme that they name: `keep_count`: the first image keeps 192 tokens and the last 48. `keep_index`: the 192 entries of an image are distinct patch numbers.
All inputs are finite; a program needn't handle non-finite values.
Results may differ from the reference program's by a relative error of at most 0.017.
The reference program's roundings to bfloat16 on the way count: a program that leaves them out, or rounds other values in their place, can miss the bound.
Values may be sent and summed in bfloat16 or wider, within the bound.
A program may use at most 192 MiB of HBM per device.

```python
import math
import jax
import jax.numpy as jnp
from jax import lax

D = 1152
HEADS = 16
HEAD_DIM = 72
FF = 4608
PATCHES = 256
KEEP = 192
IMAGES = 32


def draw_keep_count(key, part):
    counts = jax.random.randint(jax.random.fold_in(key, 11), (IMAGES,), KEEP // 4, KEEP + 1)
    counts = counts.at[0].set(KEEP)
    counts = counts.at[IMAGES - 1].set(KEEP // 4)
    return counts.astype(jnp.int32)


def draw_keep_index(key, part):
    streams = jax.random.split(jax.random.fold_in(key, 23), IMAGES)

    def one_image(stream):
        return jax.random.permutation(stream, PATCHES)[:KEEP]
    return jax.vmap(one_image)(streams).astype(jnp.int32)


def spiked(values, own_key, source, target, blocks, factor):
    def block_of(axis_at):
        return (jnp.arange(values.shape[axis_at]) // (values.shape[axis_at] // blocks)).reshape((-1,) + (1,) * (values.ndim - 1 - axis_at))

    one_side = jax.random.permutation(own_key, blocks)[block_of(target)]
    second = (block_of(target) + blocks // 2) % blocks
    return jnp.where((block_of(source) == one_side) | (block_of(source) == second), factor * values, values)


def block_scale(key, extent, cuts, smallest, high):
    level, own = 1.0, jax.random.fold_in(key, 6)
    for axis_at, blocks in cuts:
        steps = jnp.exp(jax.random.uniform(jax.random.fold_in(own, axis_at), (blocks,), jnp.float32, smallest / len(cuts), high / len(cuts)))
        level = level * jnp.repeat(steps, extent[axis_at] // blocks).reshape([-1 if axis == axis_at else 1 for axis in range(len(extent))])
    return level


def noise(rng, dims, width, most, cuts=(), dtype=jnp.bfloat16):
    gain = block_scale(rng, dims, cuts, -0.22, 0.18) if cuts else 1.0
    values = jax.random.normal(rng, dims, jnp.float32) * width * gain
    return jnp.minimum(jnp.maximum(values, -most), most).astype(dtype)


def gaussian_with(stream_key, dims, width, bound, cuts, heavy, kind=jnp.bfloat16):
    values = width * jax.random.normal(stream_key, dims, jnp.float32)
    if cuts:
        values = values * block_scale(stream_key, dims, cuts, -0.22, 0.18)
    return jnp.clip(spiked(values, jax.random.fold_in(stream_key, 3), *heavy), -bound, bound).astype(kind)


def setup_inputs(seed: int = 0) -> dict:
    key_list = jax.random.split(jax.random.key(seed), 15)
    patches_in = noise(key_list[0], (IMAGES, PATCHES, D), 1.0, 6.0, ((0, 32),))
    condition = noise(key_list[1], (IMAGES, D), 1.0, 6.0, ((0, 32),))
    keep_count = draw_keep_count(jax.random.fold_in(key_list[14], 71), 0)
    keep_index = draw_keep_index(jax.random.fold_in(key_list[14], 71), 0)
    w_ada = noise(key_list[4], (D, 6 * D), D ** -0.5, 0.1875, ((0, 4), (1, 8)))
    b_ada = noise(key_list[5], (6 * D,), 0.5, 3.0, ((0, 32),))
    w_qkv = noise(key_list[6], (D, 3 * D), D ** -0.5, 0.1875, ((0, 4), (1, 8)))
    qv_bias = noise(key_list[7], (2 * D,), 0.5, 3.0, ((0, 32),))
    w_proj = noise(key_list[8], (D, D), (D // 64) ** -0.5, 1.5, ((0, 4), (1, 8)))
    w_fc1 = noise(key_list[9], (D, FF), D ** -0.5, 0.1875, ((0, 4), (1, 8)))
    fc1_bias = noise(key_list[10], (FF,), 0.5, 3.0, ((0, 32),))
    w_fc2 = noise(key_list[11], (FF, D), (FF // 4) ** -0.5, 0.1875, ((0, 4), (1, 8)))
    out_bias = noise(key_list[12], (2 * D,), 0.5, 3.0, ((0, 32),))
    cotangent = gaussian_with(key_list[13], (IMAGES, KEEP, D), 1.0, 6.0, ((0, 32),), (0, 2, 32, 2.75))
    return {"patches_in": patches_in, "condition": condition, "keep_count": keep_count, "keep_index": keep_index, "w_ada": w_ada, "b_ada": b_ada, "w_qkv": w_qkv, "qv_bias": qv_bias, "w_proj": w_proj, "w_fc1": w_fc1, "fc1_bias": fc1_bias, "w_fc2": w_fc2, "out_bias": out_bias, "cotangent": cotangent}


@jax.custom_vjp
def low(v):
    return lax.optimization_barrier(v.astype(jnp.bfloat16)).astype(jnp.float32)

@jax.custom_vjp
def low_back(v):
    return v

def low_keep(v):
    return (low(v), None)

def low_pass(kept, grad):
    return (grad,)

def back_keep(v):
    return (v, None)

def back_low(kept, grad):
    return (low(grad),)
low.defvjp(low_keep, low_pass)
low_back.defvjp(back_keep, back_low)
epsilon = 1e-06
negative = -1e+30

def layer_norm(inputs):
    centred = inputs - lax.optimization_barrier(jnp.mean(inputs, axis=-1, keepdims=True))
    return centred * lax.rsqrt(lax.optimization_barrier(jnp.mean(centred * centred, axis=-1, keepdims=True)) + epsilon)

def swish(inputs):
    return inputs / (1.0 + jnp.exp(-inputs))

def gelu_tanh(inputs):
    return 0.5 * inputs * (1.0 + jnp.tanh(0.7978845608028654 * (inputs + 0.044715 * inputs * inputs * inputs)))

def block_forward(pixels, cond_float, counts, indices, w_ada, b_ada, w_qkv, qv_bias, w_proj, w_fc1, fc1_bias, w_fc2, out_bias):
    highest = lax.Precision.HIGHEST
    features = pixels.shape[-1]
    kept_in = jnp.take_along_axis(pixels, indices[:, :, None], axis=1)
    allowed = jnp.arange(indices.shape[1])[None, :] < counts[:, None]
    signal = low(swish(cond_float))
    modulation = low_back(jnp.dot(signal, w_ada, precision=highest) + b_ada)
    shift_one, scale_one, gate_one, shift_two, scale_two, gate_two = [modulation[:, None, column * features:(column + 1) * features] for column in range(6)]
    hidden_one = low(layer_norm(kept_in) * (1.0 + scale_one) + shift_one)
    qkv_bias = jnp.concatenate([qv_bias[:features], jnp.zeros_like(qv_bias[:features]), qv_bias[features:]])
    projected = low(low_back(jnp.einsum('gtd,de->gte', hidden_one, w_qkv, precision=highest) + qkv_bias))
    head_shape = kept_in.shape[:2] + (HEADS, HEAD_DIM)
    queries = projected[..., :features].reshape(head_shape)
    key_rows = projected[..., features:2 * features].reshape(head_shape)
    values = projected[..., 2 * features:].reshape(head_shape)
    scores = low_back(jnp.einsum('gqhe,gkhe->ghqk', queries, key_rows, precision=highest) / math.sqrt(HEAD_DIM))
    scores = jnp.where(allowed[:, None, None, :], scores, negative)
    exponent = jnp.exp(scores - lax.optimization_barrier(jnp.max(scores, axis=-1, keepdims=True)))
    softmax_out = low(exponent / lax.optimization_barrier(jnp.sum(exponent, axis=-1, keepdims=True)))
    mixed = low(low_back(jnp.einsum('ghqk,gkhe->gqhe', softmax_out, values, precision=highest).reshape(kept_in.shape)))
    attended = low_back(jnp.einsum('gtd,de->gte', mixed, w_proj, precision=highest) + out_bias[:features])
    middle = kept_in + gate_one * attended
    hidden_two = low(layer_norm(middle) * (1.0 + scale_two) + shift_two)
    raised = low_back(jnp.einsum('gtd,de->gte', hidden_two, w_fc1, precision=highest) + fc1_bias)
    activated = low(gelu_tanh(raised))
    branch = low_back(jnp.einsum('gtf,fd->gtd', activated, w_fc2, precision=highest) + out_bias[features:])
    return middle + gate_two * branch

def reference(patches_in, condition, keep_count, keep_index, w_ada, b_ada, w_qkv, qv_bias, w_proj, w_fc1, fc1_bias, w_fc2, out_bias, cotangent):
    params = tuple((weight.astype(jnp.float32) for weight in (w_ada, b_ada, w_qkv, qv_bias, w_proj, w_fc1, fc1_bias, w_fc2, out_bias)))
    per_group = 16
    blocks = patches_in.shape[0] // per_group

    def split_groups(array):
        return array.reshape((blocks, per_group) + array.shape[1:])
    stacked = (split_groups(patches_in.astype(jnp.float32)), split_groups(condition.astype(jnp.float32)), split_groups(keep_count), split_groups(keep_index), split_groups(cotangent.astype(jnp.float32)))

    def group_step(totals, item):
        pixels, cond_group, counts, indices, upstream = item

        def forward(pixels_given, cond_given, *weights):
            return block_forward(pixels_given, cond_given, counts, indices, *weights)
        result, pullback = jax.vjp(forward, pixels, cond_group, *params)
        gradients = pullback(upstream)
        summed = tuple((before + gradient for before, gradient in zip(totals, gradients[2:])))
        return (summed, (result.astype(jnp.bfloat16), gradients[0], gradients[1]))
    initial = tuple((jnp.zeros_like(weight) for weight in params))
    totals, (outputs, grad_pixels, grad_conditions) = lax.scan(group_step, initial, stacked)
    return (outputs.reshape((patches_in.shape[0],) + outputs.shape[2:]), grad_pixels.reshape(patches_in.shape), grad_conditions.reshape(condition.shape), totals[0], totals[1], totals[2], totals[3], totals[4], totals[5], totals[6], totals[7], totals[8])
```

```python
import functools
import math

import jax
import jax.numpy as jnp
from jax import lax
from jax.experimental import pallas as pl
from jax.experimental.pallas import tpu as pltpu
from jax.sharding import PartitionSpec as P

HEADS = 16


epsilon = 1e-06
negative = -1e30


def layer_norm(inputs):
    centred = inputs - jnp.mean(inputs, axis=-1, keepdims=True)
    rstd = lax.rsqrt(jnp.mean(centred * centred, axis=-1, keepdims=True) + epsilon)
    return (centred * rstd, rstd)


def norm_back(upstream, normed, rstd):
    return rstd * (
        upstream
        - jnp.mean(upstream, axis=-1, keepdims=True)
        - normed * jnp.mean(upstream * normed, axis=-1, keepdims=True)
    )


def swish(inputs):
    return inputs / (1.0 + jnp.exp(-inputs))


def gelu_tanh(inputs):
    return (
        0.5
        * inputs
        * (1.0 + jnp.tanh(0.7978845608028654 * (inputs + 0.044715 * inputs * inputs * inputs)))
    )


def contract(left, right, left_dims, right_dims):
    return lax.dot_general(
        left, right, ((left_dims, right_dims), ((), ())), preferred_element_type=jnp.float32
    )


def rows_rows(left, right):
    return contract(left, right, (0,), (0,))


def times_transposed(left, right):
    return contract(left, right, (1,), (1,))


def swap(value, axis, mask):
    size = lax.axis_size(axis)
    return lax.ppermute(value, axis, [(index, index ^ mask) for index in range(size)])


def pick(pieces, index):
    return lax.dynamic_index_in_dim(pieces, index, 0, keepdims=False)


def put(pieces, value, index):
    return lax.dynamic_update_index_in_dim(pieces, value, index, 0)


def after(value, other):
    return lax.optimization_barrier((value, other))[0]


def ordered(parts, axis):
    here = lax.axis_index(axis)
    result = jnp.zeros((len(parts),) + parts[0].shape, parts[0].dtype)
    for mask, part in enumerate(parts):
        result = put(result, part, here ^ mask)
    return result


def trade(pieces, axis):
    size = lax.axis_size(axis)
    here = lax.axis_index(axis)
    parts = [pick(pieces, here)]
    for mask in range(1, size):
        parts.append(swap(pick(pieces, here ^ mask), axis, mask))
    return ordered(parts, axis)


def spread_small(value, axis):
    size = lax.axis_size(axis)
    return ordered([value] + [swap(value, axis, mask) for mask in range(1, size)], axis)


def fsdp_masks():
    size = lax.axis_size("fsdp")
    inner = size // 4
    return [inner * step for step in range(1, 4)], list(range(1, inner))


def collect(shard):
    outer, inner = fsdp_masks()
    parts = {0: shard}
    for mask in inner:
        parts[mask] = swap(shard, "fsdp", mask)
    for wide in outer:
        parts[wide] = swap(shard, "fsdp", wide)
    for wide in outer:
        for mask in inner:
            parts[wide ^ mask] = swap(parts[wide], "fsdp", mask)
    return [parts[mask] for mask in range(lax.axis_size("fsdp"))]


def reduce_blocks(blocks):
    outer, inner = fsdp_masks()
    here = lax.axis_index("fsdp")
    wide_all = [0] + outer
    kept = {wide: pick(blocks, here ^ wide).astype(jnp.float32) for wide in wide_all}
    for mask in inner:
        leaving = jnp.stack([pick(blocks, here ^ (wide ^ mask)) for wide in wide_all])
        arrived = swap(leaving, "fsdp", mask)
        for place, wide in enumerate(wide_all):
            kept[wide] = kept[wide] + arrived[place].astype(jnp.float32)
    total = kept[0]
    for wide in outer:
        total = total + swap(kept[wide].astype(jnp.bfloat16), "fsdp", wide).astype(jnp.float32)
    return total


def spread_dp(value):
    size = lax.axis_size("dp")
    slots = {0: value}
    mask = size // 2
    while mask:
        keys = sorted(slots)
        arrived = swap(jnp.stack([slots[key] for key in keys]), "dp", mask)
        for place, key in enumerate(keys):
            slots[key ^ mask] = arrived[place]
        mask //= 2
    return jnp.stack([slots[key] for key in range(size)])


def reduce_dp(slots):
    size = lax.axis_size("dp")
    held = {key: slots[key] for key in range(size)}
    mask = 1
    while mask < size:
        leaving = sorted(key for key in held if key & mask)
        arrived = swap(
            jnp.stack([held[key].astype(jnp.bfloat16) for key in leaving]), "dp", mask
        )
        for place, key in enumerate(leaving):
            held[key ^ mask] = held[key ^ mask] + arrived[place].astype(jnp.float32)
            del held[key]
        mask *= 2
    return held[0]


def inner_rows(left, right):
    return lax.dot_general(
        left, right, (((0,), (0,)), ((), ())), preferred_element_type=jnp.float32
    )


def flat_bias(collected):
    return collected.reshape(-1)


def gather_forward(w_ada, b_ada, w_qkv, qv_bias, w_proj, w_fc1, fc1_bias, w_fc2, out_bias):
    part_ada, part_qkv, part_proj, part_one, part_two, bias_ada, bias_qv, bias_one, bias_out = (
        lax.all_gather(w_ada, "fsdp", axis=1, tiled=True),
        lax.all_gather(w_qkv, "fsdp", axis=1, tiled=True),
        lax.all_gather(w_proj, "fsdp", axis=1, tiled=True),
        lax.all_gather(w_fc1, "fsdp", axis=1, tiled=True),
        lax.all_gather(w_fc2, "fsdp", axis=1, tiled=True),
        lax.all_gather(b_ada.reshape(1, 1, -1), "fsdp", axis=1, tiled=True),
        lax.all_gather(qv_bias.reshape(1, 1, -1), "fsdp", axis=1, tiled=True),
        lax.all_gather(fc1_bias.reshape(1, 1, -1), "fsdp", axis=1, tiled=True),
        lax.all_gather(out_bias.reshape(1, 1, -1), "fsdp", axis=1, tiled=True),
    )
    gathered = (
        lax.all_gather(part_ada, "dp", axis=0, tiled=True),
        lax.all_gather(part_qkv, "dp", axis=0, tiled=True),
        lax.all_gather(part_proj, "dp", axis=0, tiled=True),
        lax.all_gather(part_one, "dp", axis=0, tiled=True),
        lax.all_gather(part_two, "dp", axis=0, tiled=True),
        lax.all_gather(bias_ada, "dp", axis=0, tiled=True),
        lax.all_gather(bias_qv, "dp", axis=0, tiled=True),
        lax.all_gather(bias_one, "dp", axis=0, tiled=True),
        lax.all_gather(bias_out, "dp", axis=0, tiled=True),
    )
    return (
        gathered[0],
        flat_bias(gathered[5]),
        gathered[1],
        flat_bias(gathered[6]),
        gathered[2],
        gathered[3],
        flat_bias(gathered[7]),
        gathered[4],
        flat_bias(gathered[8]),
    )


def gather_backward(w_ada, w_qkv, w_proj, w_fc1, w_fc2):
    part_ada, part_qkv, part_proj, part_one, part_two = (
        lax.all_gather(w_ada, "fsdp", axis=1, tiled=True),
        lax.all_gather(w_qkv, "fsdp", axis=1, tiled=True),
        lax.all_gather(w_proj, "fsdp", axis=1, tiled=True),
        lax.all_gather(w_fc1, "fsdp", axis=1, tiled=True),
        lax.all_gather(w_fc2, "fsdp", axis=1, tiled=True),
    )
    return (
        lax.all_gather(part_ada, "dp", axis=0, tiled=True),
        lax.all_gather(part_qkv, "dp", axis=0, tiled=True),
        lax.all_gather(part_proj, "dp", axis=0, tiled=True),
        lax.all_gather(part_one, "dp", axis=0, tiled=True),
        lax.all_gather(part_two, "dp", axis=0, tiled=True),
    )


def split_bias(term):
    return term.reshape(lax.axis_size("dp"), lax.axis_size("fsdp"), -1)


def own_bias(summed):
    return lax.dynamic_index_in_dim(summed, lax.axis_index("dp"), 0, keepdims=False).reshape(-1)


def owned_columns(matrix, width):
    return lax.dynamic_slice_in_dim(matrix, lax.axis_index("dp") * width, width, 1)


def column_totals(matrix):
    return jnp.sum(matrix.astype(jnp.float32), axis=0)


def plain_shards(
    patches_in,
    condition,
    keep_count,
    keep_index,
    w_ada,
    b_ada,
    w_qkv,
    qv_bias,
    w_proj,
    w_fc1,
    fc1_bias,
    w_fc2,
    out_bias,
    cotangent,
):
    images, kept_slots = keep_index.shape
    features = patches_in.shape[2]
    hidden_units = w_fc2.shape[0] * lax.axis_size("dp")
    all_rows = images * kept_slots
    head_size = features // HEADS
    factor = 1.0 / math.sqrt(head_size)
    head_shape = (images, kept_slots, HEADS, head_size)
    row_width = features // lax.axis_size("dp")
    unit_width = hidden_units // lax.axis_size("dp")
    ada_full, ada_bias, qkv_full, qv_full, proj_full, one_full, one_bias, two_full, out_full = (
        gather_forward(w_ada, b_ada, w_qkv, qv_bias, w_proj, w_fc1, fc1_bias, w_fc2, out_bias)
    )
    inputs = patches_in.astype(jnp.float32)
    kept_in = jnp.take_along_axis(inputs, keep_index[:, :, None], axis=1)
    allowed = (jnp.arange(kept_slots)[None, :] < keep_count[:, None])[:, None, None, :]
    cond_float = condition.astype(jnp.float32)
    signal = swish(cond_float).astype(jnp.bfloat16)
    modulation = jnp.dot(signal, ada_full, preferred_element_type=jnp.float32) + ada_bias.astype(
        jnp.float32
    )
    shift_one, scale_one, gate_one, shift_two, scale_two, gate_two = [
        modulation[:, None, column * features : (column + 1) * features] for column in range(6)
    ]
    normed_one, rstd_one = layer_norm(kept_in)
    hidden_one = (
        (normed_one * (1.0 + scale_one) + shift_one)
        .astype(jnp.bfloat16)
        .reshape(all_rows, features)
    )
    qv_float = qv_full.astype(jnp.float32)
    qkv_bias = jnp.concatenate(
        [qv_float[:features], jnp.zeros((features,), jnp.float32), qv_float[features:]]
    )
    projected = (
        jnp.dot(hidden_one, qkv_full, preferred_element_type=jnp.float32) + qkv_bias
    ).astype(jnp.bfloat16)
    queries = projected[:, :features].reshape(head_shape)
    key_rows = projected[:, features : 2 * features].reshape(head_shape)
    values = projected[:, 2 * features :].reshape(head_shape)
    scores = (
        jnp.einsum("iqhe,ikhe->ihqk", queries, key_rows, preferred_element_type=jnp.float32)
        * factor
    )
    scores = jnp.where(allowed, scores, negative)
    top_score = jnp.max(scores, axis=-1, keepdims=True)
    exponent = jnp.exp(scores - top_score)
    row_total = jnp.sum(exponent, axis=-1, keepdims=True)
    log_total = top_score + jnp.log(row_total)
    softmax_low = (exponent / row_total).astype(jnp.bfloat16)
    mixed = jnp.einsum("ihqk,ikhe->iqhe", softmax_low, values, preferred_element_type=jnp.float32)
    mixed_low = mixed.reshape(all_rows, features).astype(jnp.bfloat16)
    out_float = out_full.astype(jnp.float32)
    attended = (
        jnp.dot(mixed_low, proj_full, preferred_element_type=jnp.float32) + out_float[:features]
    ).reshape(images, kept_slots, features)
    middle = kept_in + gate_one * attended
    normed_two, rstd_two = layer_norm(middle)
    hidden_two = (
        (normed_two * (1.0 + scale_two) + shift_two)
        .astype(jnp.bfloat16)
        .reshape(all_rows, features)
    )
    raised = jnp.dot(hidden_two, one_full, preferred_element_type=jnp.float32) + one_bias.astype(
        jnp.float32
    )
    activated = gelu_tanh(raised).astype(jnp.bfloat16)
    branch = (
        jnp.dot(activated, two_full, preferred_element_type=jnp.float32) + out_float[features:]
    ).reshape(images, kept_slots, features)
    block_out = (middle + gate_two * branch).astype(jnp.bfloat16)
    ada_back, qkv_back, proj_back, one_back, two_back = gather_backward(
        w_ada, w_qkv, w_proj, w_fc1, w_fc2
    )
    upstream = cotangent.astype(jnp.float32)
    d_gate_two = jnp.sum(upstream * branch, axis=1)
    d_branch = (gate_two * upstream).reshape(all_rows, features).astype(jnp.bfloat16)
    d_activated = times_transposed(d_branch, two_back)
    unused, gelu_pull = jax.vjp(gelu_tanh, raised)
    d_raised = gelu_pull(d_activated)[0].astype(jnp.bfloat16)
    d_hidden_two = times_transposed(d_raised, one_back).reshape(images, kept_slots, features)
    d_shift_two = jnp.sum(d_hidden_two, axis=1)
    d_scale_two = jnp.sum(d_hidden_two * normed_two, axis=1)
    d_middle = upstream + norm_back(d_hidden_two * (1.0 + scale_two), normed_two, rstd_two)
    d_gate_one = jnp.sum(d_middle * attended, axis=1)
    d_attended = (gate_one * d_middle).reshape(all_rows, features).astype(jnp.bfloat16)
    d_mixed = times_transposed(d_attended, proj_back).astype(jnp.bfloat16).reshape(head_shape)
    scores_again = (
        jnp.einsum("iqhe,ikhe->ihqk", queries, key_rows, preferred_element_type=jnp.float32)
        * factor
    )
    scores_again = jnp.where(allowed, scores_again, negative)
    softmax_again = jnp.exp(scores_again - log_total)
    d_softmax = jnp.einsum("iqhe,ikhe->ihqk", d_mixed, values, preferred_element_type=jnp.float32)
    row_delta = jnp.sum(d_softmax * softmax_again, axis=-1, keepdims=True)
    d_scores = (softmax_again * (d_softmax - row_delta)).astype(jnp.bfloat16)
    d_queries = (
        jnp.einsum("ihqk,ikhe->iqhe", d_scores, key_rows, preferred_element_type=jnp.float32)
        * factor
    )
    d_keys = (
        jnp.einsum("ihqk,iqhe->ikhe", d_scores, queries, preferred_element_type=jnp.float32)
        * factor
    )
    d_values = jnp.einsum(
        "ihqk,iqhe->ikhe",
        softmax_again.astype(jnp.bfloat16),
        d_mixed,
        preferred_element_type=jnp.float32,
    )
    d_projected = jnp.concatenate(
        [
            d_queries.reshape(all_rows, features),
            d_keys.reshape(all_rows, features),
            d_values.reshape(all_rows, features),
        ],
        axis=1,
    ).astype(jnp.bfloat16)
    d_hidden_one = times_transposed(d_projected, qkv_back).reshape(images, kept_slots, features)
    d_shift_one = jnp.sum(d_hidden_one, axis=1)
    d_scale_one = jnp.sum(d_hidden_one * normed_one, axis=1)
    d_kept = d_middle + norm_back(d_hidden_one * (1.0 + scale_one), normed_one, rstd_one)
    grad_patches = jnp.zeros_like(inputs).at[jnp.arange(images)[:, None], keep_index].add(d_kept)
    d_modulation = jnp.concatenate(
        [d_shift_one, d_scale_one, d_gate_one, d_shift_two, d_scale_two, d_gate_two], axis=1
    ).astype(jnp.bfloat16)
    d_signal = times_transposed(d_modulation, ada_back)
    unused_too, swish_pull = jax.vjp(swish, cond_float)
    grad_condition = swish_pull(d_signal)[0]
    piece_one = lax.all_gather(hidden_one, "dp", axis=0, tiled=True)
    piece_proj_d = lax.all_gather(d_projected, "dp", axis=0, tiled=True)
    piece_mixed = lax.all_gather(mixed_low, "dp", axis=0, tiled=True)
    piece_att_d = lax.all_gather(d_attended, "dp", axis=0, tiled=True)
    piece_two = lax.all_gather(hidden_two, "dp", axis=0, tiled=True)
    piece_raised_d = lax.all_gather(d_raised, "dp", axis=0, tiled=True)
    piece_act = lax.all_gather(activated, "dp", axis=0, tiled=True)
    piece_branch_d = lax.all_gather(d_branch, "dp", axis=0, tiled=True)
    grad_qkv = inner_rows(owned_columns(piece_one, row_width), piece_proj_d)
    grad_proj = inner_rows(owned_columns(piece_mixed, row_width), piece_att_d)
    grad_one = inner_rows(owned_columns(piece_two, row_width), piece_raised_d)
    grad_two = inner_rows(owned_columns(piece_act, unit_width), piece_branch_d)
    qkv_sums = column_totals(piece_proj_d)
    proj_sums = column_totals(piece_att_d)
    one_sums = column_totals(piece_raised_d)
    two_sums = column_totals(piece_branch_d)
    piece_signal = lax.all_gather(signal, "dp", axis=0, tiled=True)
    piece_mod_d = lax.all_gather(d_modulation, "dp", axis=0, tiled=True)
    grad_ada = inner_rows(owned_columns(piece_signal, row_width), piece_mod_d)
    ada_sums = column_totals(piece_mod_d)
    grad_qv = jnp.concatenate([qkv_sums[:features], qkv_sums[2 * features :]])
    grad_out = jnp.concatenate([proj_sums, two_sums])
    terms = (
        grad_ada,
        grad_qkv,
        grad_proj,
        grad_one,
        grad_two,
        split_bias(ada_sums),
        split_bias(grad_qv),
        split_bias(one_sums),
        split_bias(grad_out),
    )
    (
        final_ada,
        final_qkv,
        final_proj,
        final_one,
        final_two,
        final_ada_bias,
        final_qv,
        final_bias,
        final_out,
    ) = (
        lax.psum_scatter(
            terms[0].astype(jnp.bfloat16), "fsdp", scatter_dimension=1, tiled=True
        ).astype(jnp.float32),
        lax.psum_scatter(
            terms[1].astype(jnp.bfloat16), "fsdp", scatter_dimension=1, tiled=True
        ).astype(jnp.float32),
        lax.psum_scatter(
            terms[2].astype(jnp.bfloat16), "fsdp", scatter_dimension=1, tiled=True
        ).astype(jnp.float32),
        lax.psum_scatter(
            terms[3].astype(jnp.bfloat16), "fsdp", scatter_dimension=1, tiled=True
        ).astype(jnp.float32),
        lax.psum_scatter(
            terms[4].astype(jnp.bfloat16), "fsdp", scatter_dimension=1, tiled=True
        ).astype(jnp.float32),
        lax.psum_scatter(
            terms[5].astype(jnp.bfloat16), "fsdp", scatter_dimension=1, tiled=True
        ).astype(jnp.float32),
        lax.psum_scatter(
            terms[6].astype(jnp.bfloat16), "fsdp", scatter_dimension=1, tiled=True
        ).astype(jnp.float32),
        lax.psum_scatter(
            terms[7].astype(jnp.bfloat16), "fsdp", scatter_dimension=1, tiled=True
        ).astype(jnp.float32),
        lax.psum_scatter(
            terms[8].astype(jnp.bfloat16), "fsdp", scatter_dimension=1, tiled=True
        ).astype(jnp.float32),
    )
    return (
        block_out,
        grad_patches,
        grad_condition,
        final_ada,
        own_bias(final_ada_bias),
        final_qkv,
        own_bias(final_qv),
        final_proj,
        final_one,
        own_bias(final_bias),
        final_two,
        own_bias(final_out),
    )


MESH = pl.DeviceIdType.MESH


def remote(source, target, send, recv, device):
    return pltpu.make_async_remote_copy(
        src_ref=source,
        dst_ref=target,
        send_sem=send,
        recv_sem=recv,
        device_id=device,
        device_id_type=MESH,
    )


def greet(devices):
    barrier = pltpu.get_barrier_semaphore()
    for device in devices:
        pl.semaphore_signal(barrier, 1, device_id=device, device_id_type=MESH)
    pl.semaphore_wait(barrier, len(devices))


def everyone_body(n_dp, n_fs, source, target, send, recv, local):
    d_at, f_at = lax.axis_index("dp"), lax.axis_index("fsdp")
    own = d_at * n_fs + f_at
    others = [(a, b) for a in range(n_dp) for b in range(n_fs) if a or b]
    greet([(d_at ^ a, f_at ^ b) for a, b in others])
    copies = []
    for place, (a, b) in enumerate(others):
        there = (d_at ^ a) * n_fs + (f_at ^ b)
        copies.append(
            remote(
                source.at[there],
                target.at[own],
                send.at[place],
                recv.at[place],
                (d_at ^ a, f_at ^ b),
            )
        )
    for copy in copies:
        copy.start()
    stay = pltpu.make_async_copy(source.at[own], target.at[own], local)
    stay.start()
    stay.wait()
    for copy in copies:
        copy.wait()


def exchange_everyone(pieces, ident):
    n_dp, n_fs = lax.axis_size("dp"), lax.axis_size("fsdp")
    count = n_dp * n_fs - 1
    return pl.pallas_call(
        functools.partial(everyone_body, n_dp, n_fs),
        out_shape=jax.ShapeDtypeStruct(pieces.shape, pieces.dtype),
        in_specs=[pl.BlockSpec(memory_space=pltpu.VMEM)],
        out_specs=pl.BlockSpec(memory_space=pltpu.VMEM),
        scratch_shapes=[
            pltpu.SemaphoreType.DMA((count,)),
            pltpu.SemaphoreType.DMA((count,)),
            pltpu.SemaphoreType.DMA,
        ],
        compiler_params=pltpu.CompilerParams(collective_id=ident, has_side_effects=True),
        name="exchange_everyone",
    )(pieces)


def tiles(rows, height):
    width = height * 128
    return jnp.pad(rows, ((0, 0), (0, width - rows.shape[1]))).reshape(-1, height, 128)


def untiles(pieces, width):
    return pieces.reshape(pieces.shape[0], -1)[:, :width]


def normed(value):
    centred = value - jnp.mean(value, axis=-1, keepdims=True)
    rstd = lax.rsqrt(jnp.mean(centred * centred, axis=-1, keepdims=True) + epsilon)
    return centred * rstd, rstd


def head_place(block, per_shard):
    return block // per_shard, block % per_shard


def forward_body(
    sizes,
    att_ref,
    one_ref,
    two_ref,
    kept_ref,
    mod_ref,
    bias_ref,
    out_bias_ref,
    cot_ref,
    count_ref,
    att_all,
    one_all,
    two_all,
    hidden_one_ref,
    projected_ref,
    mixed_ref,
    attended_ref,
    hidden_all,
    branch_all,
    proj_dense,
    send_z,
    send_y,
    send_x,
    recv_w,
    send_e,
    recv_e,
    local,
):
    n_dp, n_fs, heads, size, cols = sizes
    d_at, f_at = lax.axis_index("dp"), lax.axis_index("fsdp")
    slots, features = kept_ref.shape
    row_width = att_ref.shape[0]
    unit = one_ref.shape[0]
    inner = n_fs // 4
    wide_masks = [inner * step for step in range(1, 4)]
    near_masks = list(range(1, inner))
    dp_masks = []
    mask = n_dp // 2
    while mask:
        dp_masks.append(mask)
        mask //= 2
    low = jnp.bfloat16
    full = jnp.float32
    greet(
        [(d_at, f_at ^ b) for b in wide_masks + near_masks] + [(d_at ^ a, f_at) for a in dp_masks]
    )

    def slot(array, a, b):
        if array == 0:
            start = pl.multiple_of((d_at ^ a) * row_width, 16)
            return att_all.at[f_at ^ b, pl.ds(start, row_width), :]
        start = pl.multiple_of((f_at ^ b) * unit, 16)
        return (one_all if array == 1 else two_all).at[pl.ds(start, unit), :]

    def block(array, a, b):
        if a == 0 and b == 0:
            return (att_ref, one_ref, two_ref)[array]
        return slot(array, a, b)

    started = []

    def send(array, a, b, axis, mask, sem):
        device = (d_at ^ mask, f_at) if axis == 0 else (d_at, f_at ^ mask)
        to_a, to_b = (a ^ mask, b) if axis == 0 else (a, b ^ mask)
        copy = remote(
            block(array, a, b), slot(array, a, b), sem, recv_w.at[array, to_a, to_b], device
        )
        copy.start()
        started.append(copy)

    def arrive(array, a, b):
        place = slot(array, a, b)
        pltpu.make_async_copy(place, place, recv_w.at[array, a, b]).wait()

    def send_wide(array):
        for place, mask in enumerate(wide_masks):
            send(array, 0, 0, 1, mask, send_z.at[array, place])

    def send_near(array, wide, place):
        for step, mask in enumerate(near_masks):
            send(array, 0, wide, 1, mask, send_y.at[array, place, step])

    send_wide(0)
    send_near(0, 0, 0)
    send_wide(1)
    send_wide(2)

    def onward(a, b):
        for step, mask in enumerate(dp_masks):
            if a & (mask | (mask - 1)) == 0:
                send(0, a, b, 0, mask, send_x.at[a, b, step])

    onward(0, 0)
    keep_own = pltpu.make_async_copy(att_ref, slot(0, 0, 0), local.at[1])
    keep_own.start()
    keep_one = pltpu.make_async_copy(one_ref, slot(1, 0, 0), local.at[2])
    keep_one.start()
    keep_two = pltpu.make_async_copy(two_ref, slot(2, 0, 0), local.at[3])
    keep_two.start()

    kept = kept_ref[...]
    mods = [mod_ref[row : row + 1, :] for row in range(6)]
    normed_one, _ = normed(kept)
    hidden_one = (normed_one * (1.0 + mods[1]) + mods[0]).astype(low)
    hidden_one_ref[...] = hidden_one
    branch_all[0] = (mods[5] * cot_ref[...].astype(full)).astype(low)

    for mask in near_masks:
        arrive(0, 0, mask)
        onward(0, mask)
    for place, wide in enumerate(wide_masks):
        arrive(0, 0, wide)
        send_near(0, wide, place + 1)
        onward(0, wide)
    send_near(1, 0, 0)
    send_near(2, 0, 0)
    for wide in wide_masks:
        for mask in near_masks:
            arrive(0, 0, wide ^ mask)
            onward(0, wide ^ mask)
    order = sorted(range(1, n_dp), key=lambda a: (-(a & -a), a))
    for a in order:
        for b in range(n_fs):
            arrive(0, a, b)
            onward(a, b)
    keep_own.wait()

    def spread(buffer, kind):
        held = [0]
        for step, mask in enumerate(dp_masks):
            copies = []
            for key in held:
                copies.append(
                    remote(
                        buffer.at[key],
                        buffer.at[key ^ mask],
                        send_e.at[kind, key ^ mask],
                        recv_e.at[kind, key ^ mask],
                        (d_at ^ mask, f_at),
                    )
                )
                copies[-1].start()
            yield copies
            held = sorted(held + [key ^ mask for key in held])

    for copies in spread(branch_all, 0):
        for copy in copies:
            copy.wait()

    per_shard = cols // size
    for f in range(n_fs):
        out = jnp.dot(hidden_one, att_all[f, :, :cols], preferred_element_type=full)
        projected_ref[f] = (out + bias_ref[f]).astype(low)

    allowed = lax.broadcasted_iota(jnp.int32, (slots, slots), 1) < count_ref[0]
    factor = 1.0 / math.sqrt(size)
    for h in range(heads):
        parts = []
        for kind in range(3):
            f, j = head_place(kind * heads + h, per_shard)
            parts.append(projected_ref[f, :, j * size : (j + 1) * size])
        scores = contract(parts[0], parts[1], (1,), (1,)) * factor
        scores = jnp.where(allowed, scores, negative)
        top = jnp.max(scores, axis=-1, keepdims=True)
        exponent = jnp.exp(scores - top)
        softmax = exponent / jnp.sum(exponent, axis=-1, keepdims=True)
        mix = jnp.dot(softmax.astype(low), parts[2], preferred_element_type=full)
        mixed_ref[:, h * size : (h + 1) * size] = mix.astype(low)

    width = proj_dense.shape[1] // n_fs
    for f in range(n_fs):
        proj_dense[:, f * width : (f + 1) * width] = att_all[f, :, cols : cols + width]
    attended = (
        jnp.dot(mixed_ref[...], proj_dense[...], preferred_element_type=full) + out_bias_ref[...]
    )
    attended_ref[...] = attended
    middle = kept + mods[2] * attended
    normed_two, _ = normed(middle)
    hidden_all[0] = (normed_two * (1.0 + mods[4]) + mods[3]).astype(low)
    for copies in spread(hidden_all, 1):
        for copy in copies:
            copy.wait()

    for array in (1, 2):
        for place, wide in enumerate(wide_masks):
            arrive(array, 0, wide)
            send_near(array, wide, place + 1)
    for array in (1, 2):
        for wide in [0] + wide_masks:
            for mask in near_masks:
                arrive(array, 0, wide ^ mask)
    keep_one.wait()
    keep_two.wait()
    for copy in started:
        copy.wait_send()


def forward_kernel(att, one_block, two_block, kept, mods, bias, out_bias, cot, count, cols):
    n_dp, n_fs = lax.axis_size("dp"), lax.axis_size("fsdp")
    slots, features = kept.shape
    unit = one_block.shape[0]
    size = features // HEADS
    inner = n_fs // 4
    low, full = jnp.bfloat16, jnp.float32
    vmem = pl.BlockSpec(memory_space=pltpu.VMEM)
    shapes = [
        ((n_fs, features, att.shape[1]), low),
        ((n_fs * unit, features), low),
        ((n_fs * two_block.shape[0], two_block.shape[1]), low),
        ((slots, features), low),
        ((n_fs, slots, cols), low),
        ((slots, features), low),
        ((slots, features), full),
        ((n_dp, slots, features), low),
        ((n_dp, slots, features), low),
        ((features, features), low),
    ]
    return pl.pallas_call(
        functools.partial(forward_body, (n_dp, n_fs, HEADS, size, cols)),
        out_shape=[jax.ShapeDtypeStruct(shape, kind) for shape, kind in shapes],
        in_specs=[vmem] * 8 + [pl.BlockSpec(memory_space=pltpu.SMEM)],
        out_specs=[vmem] * len(shapes),
        scratch_shapes=[
            pltpu.SemaphoreType.DMA((3, 3)),
            pltpu.SemaphoreType.DMA((3, 4, max(inner - 1, 1))),
            pltpu.SemaphoreType.DMA((n_dp, n_fs, n_dp.bit_length() - 1)),
            pltpu.SemaphoreType.DMA((3, n_dp, n_fs)),
            pltpu.SemaphoreType.DMA((2, n_dp)),
            pltpu.SemaphoreType.DMA((2, n_dp)),
            pltpu.SemaphoreType.DMA((4,)),
        ],
        compiler_params=pltpu.CompilerParams(
            collective_id=5, has_side_effects=True, vmem_limit_bytes=64 * 1024 * 1024 - 65536
        ),
        name="forward",
    )(att, one_block, two_block, kept, mods, bias, out_bias, cot, count)


def shards(
    patches_in,
    condition,
    keep_count,
    keep_index,
    w_ada,
    b_ada,
    w_qkv,
    qv_bias,
    w_proj,
    w_fc1,
    fc1_bias,
    w_fc2,
    out_bias,
    cotangent,
):
    n_dp, n_fs = lax.axis_size("dp"), lax.axis_size("fsdp")
    n_all = n_dp * n_fs
    d_at, f_at = lax.axis_index("dp"), lax.axis_index("fsdp")
    kept_slots = keep_index.shape[1]
    features = patches_in.shape[2]
    hidden_units = w_fc2.shape[0] * n_dp
    head_size = features // HEADS
    factor = 1.0 / math.sqrt(head_size)
    head_shape = (kept_slots, HEADS, head_size)
    row_width = features // n_dp
    low = jnp.bfloat16
    full = jnp.float32

    unit_width = w_fc1.shape[1] // n_dp
    one_pieces = w_fc1.reshape(row_width, n_dp, unit_width).transpose(1, 2, 0)
    two_pieces = (
        w_fc2.reshape(n_fs // n_dp, n_dp, unit_width, w_fc2.shape[1])
        .transpose(1, 3, 0, 2)
        .reshape(n_dp, w_fc2.shape[1], -1)
    )
    both_pieces = jnp.concatenate([one_pieces, two_pieces], axis=2)
    cond_float = condition.astype(full)
    signal = swish(cond_float).astype(low)
    message = jnp.concatenate(
        [signal, b_ada[None], qv_bias[None], fc1_bias[None], out_bias[None]], axis=1
    )
    sizes = [features, b_ada.shape[0], qv_bias.shape[0], fc1_bias.shape[0], out_bias.shape[0]]
    ends = [sum(sizes[: place + 1]) for place in range(len(sizes))]
    shared = exchange_everyone(
        jnp.broadcast_to(tiles(message, 16), (n_all, 16, 128)), 1
    )
    shared = untiles(shared, ends[-1])
    both = trade(both_pieces, "dp")
    one_block = both[:, :, :row_width].transpose(1, 0, 2).reshape(unit_width, features)
    two_block = (
        both[:, :, row_width:].transpose(1, 0, 2).reshape(w_fc2.shape[1], hidden_units // n_dp)
    )
    signals = lax.dynamic_slice_in_dim(shared[:, :features], d_at * row_width, row_width, 1)
    ada_bias, qv_full, one_bias, out_full = [
        shared[:, ends[place] : ends[place + 1]].reshape(-1).astype(full) for place in range(4)
    ]

    partial_mod = jnp.dot(signals, w_ada, preferred_element_type=full)
    rows_mod = untiles(exchange_everyone(tiles(partial_mod, 8), 2), partial_mod.shape[1])
    modulation = jnp.sum(rows_mod.reshape(n_dp, n_fs, -1), axis=0).reshape(1, -1) + ada_bias
    mods = modulation.reshape(6, features)
    shift_one, scale_one, gate_one, shift_two, scale_two, gate_two = [
        mods[row : row + 1] for row in range(6)
    ]
    own_one_bias = pick(
        one_bias.reshape(n_fs, n_dp, unit_width).transpose(1, 0, 2), d_at
    ).reshape(-1)

    indices = keep_index[0]
    inputs = patches_in[0]
    kept_in = jnp.take(inputs, indices, axis=0).astype(full)
    qkv_bias = jnp.concatenate(
        [qv_full[:features], jnp.zeros((features,), full), qv_full[features:]]
    )
    qkv_cols = w_qkv.shape[1]
    (
        att_all,
        one_full,
        two_full,
        hidden_one,
        projected_all,
        mixed_low,
        attended,
        hidden_two_all,
        d_branch_all,
        proj_full,
    ) = forward_kernel(
        jnp.concatenate([w_qkv, w_proj], axis=1),
        one_block,
        two_block,
        kept_in,
        mods,
        qkv_bias.reshape(n_fs, 1, qkv_cols),
        out_full[None, :features],
        cotangent[0],
        keep_count,
        qkv_cols,
    )
    hidden_two_all = hidden_two_all.reshape(n_dp * kept_slots, features)
    d_branch_all = d_branch_all.reshape(n_dp * kept_slots, features)
    d_branch = d_branch_all[:kept_slots]
    qkv_full = att_all[:, :, :qkv_cols].transpose(1, 0, 2).reshape(features, -1)
    projected = projected_all.transpose(1, 0, 2).reshape(kept_slots, -1)
    allowed = (jnp.arange(kept_slots) < keep_count[0])[None, None, :]
    normed_one, rstd_one = layer_norm(kept_in)
    middle = kept_in + gate_one * attended
    normed_two, rstd_two = layer_norm(middle)
    upstream = cotangent[0].astype(full)
    queries = projected[:, :features].reshape(head_shape)
    key_rows = projected[:, features : 2 * features].reshape(head_shape)
    values = projected[:, 2 * features :].reshape(head_shape)
    scores = jnp.einsum("qhe,khe->hqk", queries, key_rows, preferred_element_type=full) * factor
    scores = jnp.where(allowed, scores, negative)
    top_score = jnp.max(scores, axis=-1, keepdims=True)
    exponent = jnp.exp(scores - top_score)
    softmax = exponent / jnp.sum(exponent, axis=-1, keepdims=True)
    softmax_low = softmax.astype(low)

    raised = times_transposed(hidden_two_all, one_full) + own_one_bias
    activated = gelu_tanh(raised).astype(low)
    grad_two = rows_rows(d_branch_all, activated).astype(low)
    branch_part = times_transposed(activated, two_full)
    branch = (
        reduce_dp(branch_part.reshape(n_dp, kept_slots, features)) + out_full[features:]
    )
    block_out = (middle + gate_two * branch).astype(low)
    d_gate_two = jnp.sum(upstream * branch, axis=0)
    d_activated = jnp.dot(d_branch_all, two_full, preferred_element_type=full)
    unused, gelu_pull = jax.vjp(gelu_tanh, raised)
    d_raised = gelu_pull(d_activated)[0].astype(low)
    d_hidden_part = jnp.dot(d_raised, one_full, preferred_element_type=full)
    d_hidden_two = reduce_dp(d_hidden_part.reshape(n_dp, kept_slots, features))
    grad_one = rows_rows(d_raised, hidden_two_all).astype(low)
    one_sums = jnp.sum(d_raised.astype(full), axis=0)
    final_two = reduce_blocks(grad_two.reshape(n_fs, -1, hidden_units // n_dp)).astype(low)
    final_one = reduce_blocks(grad_one.reshape(n_fs, unit_width, features)).astype(low)
    one_out = trade(final_one.reshape(unit_width, n_dp, row_width).transpose(1, 0, 2), "dp")
    one_out = one_out.reshape(-1, row_width).T.astype(full)
    two_out = trade(
        final_two.reshape(final_two.shape[0], n_dp, -1).transpose(1, 0, 2), "dp"
    )
    two_out = (
        two_out.reshape(n_dp, final_two.shape[0], n_fs // n_dp, unit_width)
        .transpose(2, 0, 3, 1)
        .reshape(w_fc2.shape)
        .astype(full)
    )

    d_shift_two = jnp.sum(d_hidden_two, axis=0)
    d_scale_two = jnp.sum(d_hidden_two * normed_two, axis=0)
    d_middle = upstream + norm_back(d_hidden_two * (1.0 + scale_two), normed_two, rstd_two)
    d_gate_one = jnp.sum(d_middle * attended, axis=0)
    d_attended = (gate_one * d_middle).astype(low)
    d_mixed = times_transposed(d_attended, proj_full).astype(low).reshape(head_shape)
    d_softmax = jnp.einsum("qhe,khe->hqk", d_mixed, values, preferred_element_type=full)
    row_delta = jnp.sum(d_softmax * softmax, axis=-1, keepdims=True)
    d_scores = (softmax * (d_softmax - row_delta)).astype(low)
    d_queries = jnp.einsum("hqk,khe->qhe", d_scores, key_rows, preferred_element_type=full)
    d_keys = jnp.einsum("hqk,qhe->khe", d_scores, queries, preferred_element_type=full)
    d_values = jnp.einsum("hqk,qhe->khe", softmax_low, d_mixed, preferred_element_type=full)
    d_projected = jnp.concatenate(
        [
            (d_queries * factor).reshape(kept_slots, features),
            (d_keys * factor).reshape(kept_slots, features),
            d_values.reshape(kept_slots, features),
        ],
        axis=1,
    ).astype(low)
    d_hidden_one = times_transposed(d_projected, qkv_full)
    d_shift_one = jnp.sum(d_hidden_one, axis=0)
    d_scale_one = jnp.sum(d_hidden_one * normed_one, axis=0)
    d_kept = d_middle + norm_back(d_hidden_one * (1.0 + scale_one), normed_one, rstd_one)
    grad_patches = jnp.zeros(inputs.shape, full).at[indices].set(d_kept, unique_indices=True)[None]

    def own_rows(rows):
        return trade(rows.reshape(kept_slots, n_dp, row_width).transpose(1, 0, 2), "dp").reshape(
            n_dp * kept_slots, row_width
        )

    def by_index(rows):
        here = lax.axis_index("dp")
        slots = spread_dp(rows)
        return ordered([slots[mask] for mask in range(n_dp)], "dp").reshape(
            n_dp * kept_slots, -1
        )

    grad_proj = rows_rows(own_rows(mixed_low), by_index(d_attended)).astype(low)
    grad_qkv = rows_rows(own_rows(hidden_one), by_index(d_projected)).astype(low)
    proj_out = reduce_blocks(grad_proj.reshape(row_width, n_fs, -1).transpose(1, 0, 2))
    qkv_out = reduce_blocks(grad_qkv.reshape(row_width, n_fs, -1).transpose(1, 0, 2))

    d_modulation = jnp.concatenate(
        [d_shift_one, d_scale_one, d_gate_one, d_shift_two, d_scale_two, d_gate_two]
    ).astype(low)
    group_d = trade(d_modulation.reshape(n_fs, -1), "fsdp")
    all_d = spread_small(group_d, "dp").reshape(n_all, -1)
    grad_ada = rows_rows(signals, all_d)
    part_signal = times_transposed(all_d, w_ada).reshape(n_dp, n_fs, row_width)
    group_signal = jnp.sum(trade(part_signal.transpose(1, 0, 2), "fsdp"), axis=0)
    d_signal = trade(group_signal, "dp").reshape(1, features)
    unused_too, swish_pull = jax.vjp(swish, cond_float)
    grad_condition = swish_pull(d_signal)[0]

    sums = jnp.sum(d_projected.astype(full), axis=0)
    one_spread = jnp.zeros((n_fs, n_dp, unit_width), full)
    one_spread = lax.dynamic_update_index_in_dim(
        one_spread, one_sums.reshape(n_fs, unit_width), d_at, 1
    )
    bias_parts = [
        d_modulation.astype(full),
        jnp.concatenate([sums[:features], sums[2 * features :]]),
        one_spread.reshape(-1),
        jnp.concatenate(
            [
                jnp.sum(d_attended.astype(full), axis=0),
                jnp.sum(d_branch.astype(full), axis=0),
            ]
        ),
    ]
    bias_all = jnp.concatenate([part.reshape(n_all, -1) for part in bias_parts], axis=1)
    bias_all = bias_all.reshape(n_dp, n_fs, -1)
    bias_group = jnp.sum(trade(bias_all.transpose(1, 0, 2), "fsdp"), axis=0)
    bias_own = jnp.sum(trade(bias_group, "dp"), axis=0)
    starts = [end - features for end in ends]
    ada_out, qv_out, bias_out, out_out = [
        bias_own[starts[place] : starts[place + 1]] for place in range(4)
    ]
    return (
        block_out[None],
        grad_patches,
        grad_condition,
        grad_ada,
        ada_out,
        qkv_out,
        qv_out,
        proj_out,
        one_out,
        bias_out,
        two_out,
        out_out,
    )


def kernels_fit(*arrays):
    w_qkv, w_fc1 = arrays[6], arrays[9]
    features = arrays[0].shape[2]
    unit_width = w_fc1.shape[1] // lax.axis_size("dp")
    return (
        w_qkv.shape[1] % (features // HEADS) == 0
        and w_qkv.shape[0] % 16 == 0
        and unit_width % 16 == 0
        and unit_width == arrays[11].shape[1]
        and lax.axis_size("fsdp") % 4 == 0
    )


def solution(mesh):
    both = ("dp", "fsdp")
    weight = P("dp", "fsdp")
    flat = P(both)
    placed = (
        P(both, None, None),
        P(both, None),
        flat,
        P(both, None),
        weight,
        flat,
        weight,
        flat,
        weight,
        weight,
        flat,
        weight,
        flat,
        P(both, None, None),
    )

    def chosen(*arrays):
        return (shards if kernels_fit(*arrays) else plain_shards)(*arrays)

    return jax.shard_map(
        chosen,
        mesh=mesh,
        in_specs=placed,
        out_specs=(
            P(both, None, None),
            P(both, None, None),
            P(both, None),
            weight,
            flat,
            weight,
            flat,
            weight,
            weight,
            flat,
            weight,
            flat,
        ),
        check_vma=False,
    )
```

```python
import functools
import math

import jax
import jax.numpy as jnp
from jax import lax
from jax.experimental import pallas as pl
from jax.experimental.pallas import tpu as pltpu
from jax.sharding import PartitionSpec as P

HEADS = 16


epsilon = 1e-06
negative = -1e30


def layer_norm(inputs):
    centred = inputs - jnp.mean(inputs, axis=-1, keepdims=True)
    rstd = lax.rsqrt(jnp.mean(centred * centred, axis=-1, keepdims=True) + epsilon)
    return (centred * rstd, rstd)


def norm_back(upstream, normed, rstd):
    return rstd * (
        upstream
        - jnp.mean(upstream, axis=-1, keepdims=True)
        - normed * jnp.mean(upstream * normed, axis=-1, keepdims=True)
    )


def swish(inputs):
    return inputs / (1.0 + jnp.exp(-inputs))


def gelu_tanh(inputs):
    return (
        0.5
        * inputs
        * (1.0 + jnp.tanh(0.7978845608028654 * (inputs + 0.044715 * inputs * inputs * inputs)))
    )


def contract(left, right, left_dims, right_dims):
    return lax.dot_general(
        left, right, ((left_dims, right_dims), ((), ())), preferred_element_type=jnp.float32
    )


def rows_rows(left, right):
    return contract(left, right, (0,), (0,))


def times_transposed(left, right):
    return contract(left, right, (1,), (1,))


def swap(value, axis, mask):
    size = lax.axis_size(axis)
    return lax.ppermute(value, axis, [(index, index ^ mask) for index in range(size)])


def pick(pieces, index):
    return lax.dynamic_index_in_dim(pieces, index, 0, keepdims=False)


def put(pieces, value, index):
    return lax.dynamic_update_index_in_dim(pieces, value, index, 0)


def after(value, other):
    return lax.optimization_barrier((value, other))[0]


def ordered(parts, axis):
    here = lax.axis_index(axis)
    result = jnp.zeros((len(parts),) + parts[0].shape, parts[0].dtype)
    for mask, part in enumerate(parts):
        result = put(result, part, here ^ mask)
    return result


def trade(pieces, axis):
    size = lax.axis_size(axis)
    here = lax.axis_index(axis)
    parts = [pick(pieces, here)]
    for mask in range(1, size):
        parts.append(swap(pick(pieces, here ^ mask), axis, mask))
    return ordered(parts, axis)


def spread_small(value, axis):
    size = lax.axis_size(axis)
    return ordered([value] + [swap(value, axis, mask) for mask in range(1, size)], axis)


def fsdp_masks():
    size = lax.axis_size("fsdp")
    inner = size // 4
    return [inner * step for step in range(1, 4)], list(range(1, inner))


def collect(shard):
    outer, inner = fsdp_masks()
    parts = {0: shard}
    for mask in inner:
        parts[mask] = swap(shard, "fsdp", mask)
    for wide in outer:
        parts[wide] = swap(shard, "fsdp", wide)
    for wide in outer:
        for mask in inner:
            parts[wide ^ mask] = swap(parts[wide], "fsdp", mask)
    return [parts[mask] for mask in range(lax.axis_size("fsdp"))]


def reduce_blocks(blocks):
    outer, inner = fsdp_masks()
    here = lax.axis_index("fsdp")
    wide_all = [0] + outer
    kept = {wide: pick(blocks, here ^ wide).astype(jnp.float32) for wide in wide_all}
    for mask in inner:
        leaving = jnp.stack([pick(blocks, here ^ (wide ^ mask)) for wide in wide_all])
        arrived = swap(leaving, "fsdp", mask)
        for place, wide in enumerate(wide_all):
            kept[wide] = kept[wide] + arrived[place].astype(jnp.float32)
    total = kept[0]
    for wide in outer:
        total = total + swap(kept[wide].astype(jnp.bfloat16), "fsdp", wide).astype(jnp.float32)
    return total


def spread_dp(value):
    size = lax.axis_size("dp")
    slots = {0: value}
    mask = size // 2
    while mask:
        keys = sorted(slots)
        arrived = swap(jnp.stack([slots[key] for key in keys]), "dp", mask)
        for place, key in enumerate(keys):
            slots[key ^ mask] = arrived[place]
        mask //= 2
    return jnp.stack([slots[key] for key in range(size)])


def reduce_dp(slots):
    size = lax.axis_size("dp")
    held = {key: slots[key] for key in range(size)}
    mask = 1
    while mask < size:
        leaving = sorted(key for key in held if key & mask)
        arrived = swap(
            jnp.stack([held[key].astype(jnp.bfloat16) for key in leaving]), "dp", mask
        )
        for place, key in enumerate(leaving):
            held[key ^ mask] = held[key ^ mask] + arrived[place].astype(jnp.float32)
            del held[key]
        mask *= 2
    return held[0]


def inner_rows(left, right):
    return lax.dot_general(
        left, right, (((0,), (0,)), ((), ())), preferred_element_type=jnp.float32
    )


def flat_bias(collected):
    return collected.reshape(-1)


def gather_forward(w_ada, b_ada, w_qkv, qv_bias, w_proj, w_fc1, fc1_bias, w_fc2, out_bias):
    part_ada, part_qkv, part_proj, part_one, part_two, bias_ada, bias_qv, bias_one, bias_out = (
        lax.all_gather(w_ada, "fsdp", axis=1, tiled=True),
        lax.all_gather(w_qkv, "fsdp", axis=1, tiled=True),
        lax.all_gather(w_proj, "fsdp", axis=1, tiled=True),
        lax.all_gather(w_fc1, "fsdp", axis=1, tiled=True),
        lax.all_gather(w_fc2, "fsdp", axis=1, tiled=True),
        lax.all_gather(b_ada.reshape(1, 1, -1), "fsdp", axis=1, tiled=True),
        lax.all_gather(qv_bias.reshape(1, 1, -1), "fsdp", axis=1, tiled=True),
        lax.all_gather(fc1_bias.reshape(1, 1, -1), "fsdp", axis=1, tiled=True),
        lax.all_gather(out_bias.reshape(1, 1, -1), "fsdp", axis=1, tiled=True),
    )
    gathered = (
        lax.all_gather(part_ada, "dp", axis=0, tiled=True),
        lax.all_gather(part_qkv, "dp", axis=0, tiled=True),
        lax.all_gather(part_proj, "dp", axis=0, tiled=True),
        lax.all_gather(part_one, "dp", axis=0, tiled=True),
        lax.all_gather(part_two, "dp", axis=0, tiled=True),
        lax.all_gather(bias_ada, "dp", axis=0, tiled=True),
        lax.all_gather(bias_qv, "dp", axis=0, tiled=True),
        lax.all_gather(bias_one, "dp", axis=0, tiled=True),
        lax.all_gather(bias_out, "dp", axis=0, tiled=True),
    )
    return (
        gathered[0],
        flat_bias(gathered[5]),
        gathered[1],
        flat_bias(gathered[6]),
        gathered[2],
        gathered[3],
        flat_bias(gathered[7]),
        gathered[4],
        flat_bias(gathered[8]),
    )


def gather_backward(w_ada, w_qkv, w_proj, w_fc1, w_fc2):
    part_ada, part_qkv, part_proj, part_one, part_two = (
        lax.all_gather(w_ada, "fsdp", axis=1, tiled=True),
        lax.all_gather(w_qkv, "fsdp", axis=1, tiled=True),
        lax.all_gather(w_proj, "fsdp", axis=1, tiled=True),
        lax.all_gather(w_fc1, "fsdp", axis=1, tiled=True),
        lax.all_gather(w_fc2, "fsdp", axis=1, tiled=True),
    )
    return (
        lax.all_gather(part_ada, "dp", axis=0, tiled=True),
        lax.all_gather(part_qkv, "dp", axis=0, tiled=True),
        lax.all_gather(part_proj, "dp", axis=0, tiled=True),
        lax.all_gather(part_one, "dp", axis=0, tiled=True),
        lax.all_gather(part_two, "dp", axis=0, tiled=True),
    )


def split_bias(term):
    return term.reshape(lax.axis_size("dp"), lax.axis_size("fsdp"), -1)


def own_bias(summed):
    return lax.dynamic_index_in_dim(summed, lax.axis_index("dp"), 0, keepdims=False).reshape(-1)


def owned_columns(matrix, width):
    return lax.dynamic_slice_in_dim(matrix, lax.axis_index("dp") * width, width, 1)


def column_totals(matrix):
    return jnp.sum(matrix.astype(jnp.float32), axis=0)


def plain_shards(
    patches_in,
    condition,
    keep_count,
    keep_index,
    w_ada,
    b_ada,
    w_qkv,
    qv_bias,
    w_proj,
    w_fc1,
    fc1_bias,
    w_fc2,
    out_bias,
    cotangent,
):
    images, kept_slots = keep_index.shape
    features = patches_in.shape[2]
    hidden_units = w_fc2.shape[0] * lax.axis_size("dp")
    all_rows = images * kept_slots
    head_size = features // HEADS
    factor = 1.0 / math.sqrt(head_size)
    head_shape = (images, kept_slots, HEADS, head_size)
    row_width = features // lax.axis_size("dp")
    unit_width = hidden_units // lax.axis_size("dp")
    ada_full, ada_bias, qkv_full, qv_full, proj_full, one_full, one_bias, two_full, out_full = (
        gather_forward(w_ada, b_ada, w_qkv, qv_bias, w_proj, w_fc1, fc1_bias, w_fc2, out_bias)
    )
    inputs = patches_in.astype(jnp.float32)
    kept_in = jnp.take_along_axis(inputs, keep_index[:, :, None], axis=1)
    allowed = (jnp.arange(kept_slots)[None, :] < keep_count[:, None])[:, None, None, :]
    cond_float = condition.astype(jnp.float32)
    signal = swish(cond_float).astype(jnp.bfloat16)
    modulation = jnp.dot(signal, ada_full, preferred_element_type=jnp.float32) + ada_bias.astype(
        jnp.float32
    )
    shift_one, scale_one, gate_one, shift_two, scale_two, gate_two = [
        modulation[:, None, column * features : (column + 1) * features] for column in range(6)
    ]
    normed_one, rstd_one = layer_norm(kept_in)
    hidden_one = (
        (normed_one * (1.0 + scale_one) + shift_one)
        .astype(jnp.bfloat16)
        .reshape(all_rows, features)
    )
    qv_float = qv_full.astype(jnp.float32)
    qkv_bias = jnp.concatenate(
        [qv_float[:features], jnp.zeros((features,), jnp.float32), qv_float[features:]]
    )
    projected = (
        jnp.dot(hidden_one, qkv_full, preferred_element_type=jnp.float32) + qkv_bias
    ).astype(jnp.bfloat16)
    queries = projected[:, :features].reshape(head_shape)
    key_rows = projected[:, features : 2 * features].reshape(head_shape)
    values = projected[:, 2 * features :].reshape(head_shape)
    scores = (
        jnp.einsum("iqhe,ikhe->ihqk", queries, key_rows, preferred_element_type=jnp.float32)
        * factor
    )
    scores = jnp.where(allowed, scores, negative)
    top_score = jnp.max(scores, axis=-1, keepdims=True)
    exponent = jnp.exp(scores - top_score)
    row_total = jnp.sum(exponent, axis=-1, keepdims=True)
    log_total = top_score + jnp.log(row_total)
    softmax_low = (exponent / row_total).astype(jnp.bfloat16)
    mixed = jnp.einsum("ihqk,ikhe->iqhe", softmax_low, values, preferred_element_type=jnp.float32)
    mixed_low = mixed.reshape(all_rows, features).astype(jnp.bfloat16)
    out_float = out_full.astype(jnp.float32)
    attended = (
        jnp.dot(mixed_low, proj_full, preferred_element_type=jnp.float32) + out_float[:features]
    ).reshape(images, kept_slots, features)
    middle = kept_in + gate_one * attended
    normed_two, rstd_two = layer_norm(middle)
    hidden_two = (
        (normed_two * (1.0 + scale_two) + shift_two)
        .astype(jnp.bfloat16)
        .reshape(all_rows, features)
    )
    raised = jnp.dot(hidden_two, one_full, preferred_element_type=jnp.float32) + one_bias.astype(
        jnp.float32
    )
    activated = gelu_tanh(raised).astype(jnp.bfloat16)
    branch = (
        jnp.dot(activated, two_full, preferred_element_type=jnp.float32) + out_float[features:]
    ).reshape(images, kept_slots, features)
    block_out = (middle + gate_two * branch).astype(jnp.bfloat16)
    ada_back, qkv_back, proj_back, one_back, two_back = gather_backward(
        w_ada, w_qkv, w_proj, w_fc1, w_fc2
    )
    upstream = cotangent.astype(jnp.float32)
    d_gate_two = jnp.sum(upstream * branch, axis=1)
    d_branch = (gate_two * upstream).reshape(all_rows, features).astype(jnp.bfloat16)
    d_activated = times_transposed(d_branch, two_back)
    unused, gelu_pull = jax.vjp(gelu_tanh, raised)
    d_raised = gelu_pull(d_activated)[0].astype(jnp.bfloat16)
    d_hidden_two = times_transposed(d_raised, one_back).reshape(images, kept_slots, features)
    d_shift_two = jnp.sum(d_hidden_two, axis=1)
    d_scale_two = jnp.sum(d_hidden_two * normed_two, axis=1)
    d_middle = upstream + norm_back(d_hidden_two * (1.0 + scale_two), normed_two, rstd_two)
    d_gate_one = jnp.sum(d_middle * attended, axis=1)
    d_attended = (gate_one * d_middle).reshape(all_rows, features).astype(jnp.bfloat16)
    d_mixed = times_transposed(d_attended, proj_back).astype(jnp.bfloat16).reshape(head_shape)
    scores_again = (
        jnp.einsum("iqhe,ikhe->ihqk", queries, key_rows, preferred_element_type=jnp.float32)
        * factor
    )
    scores_again = jnp.where(allowed, scores_again, negative)
    softmax_again = jnp.exp(scores_again - log_total)
    d_softmax = jnp.einsum("iqhe,ikhe->ihqk", d_mixed, values, preferred_element_type=jnp.float32)
    row_delta = jnp.sum(d_softmax * softmax_again, axis=-1, keepdims=True)
    d_scores = (softmax_again * (d_softmax - row_delta)).astype(jnp.bfloat16)
    d_queries = (
        jnp.einsum("ihqk,ikhe->iqhe", d_scores, key_rows, preferred_element_type=jnp.float32)
        * factor
    )
    d_keys = (
        jnp.einsum("ihqk,iqhe->ikhe", d_scores, queries, preferred_element_type=jnp.float32)
        * factor
    )
    d_values = jnp.einsum(
        "ihqk,iqhe->ikhe",
        softmax_again.astype(jnp.bfloat16),
        d_mixed,
        preferred_element_type=jnp.float32,
    )
    d_projected = jnp.concatenate(
        [
            d_queries.reshape(all_rows, features),
            d_keys.reshape(all_rows, features),
            d_values.reshape(all_rows, features),
        ],
        axis=1,
    ).astype(jnp.bfloat16)
    d_hidden_one = times_transposed(d_projected, qkv_back).reshape(images, kept_slots, features)
    d_shift_one = jnp.sum(d_hidden_one, axis=1)
    d_scale_one = jnp.sum(d_hidden_one * normed_one, axis=1)
    d_kept = d_middle + norm_back(d_hidden_one * (1.0 + scale_one), normed_one, rstd_one)
    grad_patches = jnp.zeros_like(inputs).at[jnp.arange(images)[:, None], keep_index].add(d_kept)
    d_modulation = jnp.concatenate(
        [d_shift_one, d_scale_one, d_gate_one, d_shift_two, d_scale_two, d_gate_two], axis=1
    ).astype(jnp.bfloat16)
    d_signal = times_transposed(d_modulation, ada_back)
    unused_too, swish_pull = jax.vjp(swish, cond_float)
    grad_condition = swish_pull(d_signal)[0]
    piece_one = lax.all_gather(hidden_one, "dp", axis=0, tiled=True)
    piece_proj_d = lax.all_gather(d_projected, "dp", axis=0, tiled=True)
    piece_mixed = lax.all_gather(mixed_low, "dp", axis=0, tiled=True)
    piece_att_d = lax.all_gather(d_attended, "dp", axis=0, tiled=True)
    piece_two = lax.all_gather(hidden_two, "dp", axis=0, tiled=True)
    piece_raised_d = lax.all_gather(d_raised, "dp", axis=0, tiled=True)
    piece_act = lax.all_gather(activated, "dp", axis=0, tiled=True)
    piece_branch_d = lax.all_gather(d_branch, "dp", axis=0, tiled=True)
    grad_qkv = inner_rows(owned_columns(piece_one, row_width), piece_proj_d)
    grad_proj = inner_rows(owned_columns(piece_mixed, row_width), piece_att_d)
    grad_one = inner_rows(owned_columns(piece_two, row_width), piece_raised_d)
    grad_two = inner_rows(owned_columns(piece_act, unit_width), piece_branch_d)
    qkv_sums = column_totals(piece_proj_d)
    proj_sums = column_totals(piece_att_d)
    one_sums = column_totals(piece_raised_d)
    two_sums = column_totals(piece_branch_d)
    piece_signal = lax.all_gather(signal, "dp", axis=0, tiled=True)
    piece_mod_d = lax.all_gather(d_modulation, "dp", axis=0, tiled=True)
    grad_ada = inner_rows(owned_columns(piece_signal, row_width), piece_mod_d)
    ada_sums = column_totals(piece_mod_d)
    grad_qv = jnp.concatenate([qkv_sums[:features], qkv_sums[2 * features :]])
    grad_out = jnp.concatenate([proj_sums, two_sums])
    terms = (
        grad_ada,
        grad_qkv,
        grad_proj,
        grad_one,
        grad_two,
        split_bias(ada_sums),
        split_bias(grad_qv),
        split_bias(one_sums),
        split_bias(grad_out),
    )
    (
        final_ada,
        final_qkv,
        final_proj,
        final_one,
        final_two,
        final_ada_bias,
        final_qv,
        final_bias,
        final_out,
    ) = (
        lax.psum_scatter(
            terms[0].astype(jnp.bfloat16), "fsdp", scatter_dimension=1, tiled=True
        ).astype(jnp.float32),
        lax.psum_scatter(
            terms[1].astype(jnp.bfloat16), "fsdp", scatter_dimension=1, tiled=True
        ).astype(jnp.float32),
        lax.psum_scatter(
            terms[2].astype(jnp.bfloat16), "fsdp", scatter_dimension=1, tiled=True
        ).astype(jnp.float32),
        lax.psum_scatter(
            terms[3].astype(jnp.bfloat16), "fsdp", scatter_dimension=1, tiled=True
        ).astype(jnp.float32),
        lax.psum_scatter(
            terms[4].astype(jnp.bfloat16), "fsdp", scatter_dimension=1, tiled=True
        ).astype(jnp.float32),
        lax.psum_scatter(
            terms[5].astype(jnp.bfloat16), "fsdp", scatter_dimension=1, tiled=True
        ).astype(jnp.float32),
        lax.psum_scatter(
            terms[6].astype(jnp.bfloat16), "fsdp", scatter_dimension=1, tiled=True
        ).astype(jnp.float32),
        lax.psum_scatter(
            terms[7].astype(jnp.bfloat16), "fsdp", scatter_dimension=1, tiled=True
        ).astype(jnp.float32),
        lax.psum_scatter(
            terms[8].astype(jnp.bfloat16), "fsdp", scatter_dimension=1, tiled=True
        ).astype(jnp.float32),
    )
    return (
        block_out,
        grad_patches,
        grad_condition,
        final_ada,
        own_bias(final_ada_bias),
        final_qkv,
        own_bias(final_qv),
        final_proj,
        final_one,
        own_bias(final_bias),
        final_two,
        own_bias(final_out),
    )


MESH = pl.DeviceIdType.MESH


def remote(source, target, send, recv, device):
    return pltpu.make_async_remote_copy(
        src_ref=source,
        dst_ref=target,
        send_sem=send,
        recv_sem=recv,
        device_id=device,
        device_id_type=MESH,
    )


def greet(devices):
    barrier = pltpu.get_barrier_semaphore()
    for device in devices:
        pl.semaphore_signal(barrier, 1, device_id=device, device_id_type=MESH)
    pl.semaphore_wait(barrier, len(devices))


def everyone_body(n_dp, n_fs, source, target, send, recv, local):
    d_at, f_at = lax.axis_index("dp"), lax.axis_index("fsdp")
    own = d_at * n_fs + f_at
    others = [(a, b) for a in range(n_dp) for b in range(n_fs) if a or b]
    greet([(d_at ^ a, f_at ^ b) for a, b in others])
    copies = []
    for place, (a, b) in enumerate(others):
        there = (d_at ^ a) * n_fs + (f_at ^ b)
        copies.append(
            remote(
                source.at[there],
                target.at[own],
                send.at[place],
                recv.at[place],
                (d_at ^ a, f_at ^ b),
            )
        )
    for copy in copies:
        copy.start()
    stay = pltpu.make_async_copy(source.at[own], target.at[own], local)
    stay.start()
    stay.wait()
    for copy in copies:
        copy.wait()


def exchange_everyone(pieces, ident):
    n_dp, n_fs = lax.axis_size("dp"), lax.axis_size("fsdp")
    count = n_dp * n_fs - 1
    return pl.pallas_call(
        functools.partial(everyone_body, n_dp, n_fs),
        out_shape=jax.ShapeDtypeStruct(pieces.shape, pieces.dtype),
        in_specs=[pl.BlockSpec(memory_space=pltpu.VMEM)],
        out_specs=pl.BlockSpec(memory_space=pltpu.VMEM),
        scratch_shapes=[
            pltpu.SemaphoreType.DMA((count,)),
            pltpu.SemaphoreType.DMA((count,)),
            pltpu.SemaphoreType.DMA,
        ],
        compiler_params=pltpu.CompilerParams(collective_id=ident, has_side_effects=True),
        name="exchange_everyone",
    )(pieces)


def tiles(rows, height):
    width = height * 128
    return jnp.pad(rows, ((0, 0), (0, width - rows.shape[1]))).reshape(-1, height, 128)


def untiles(pieces, width):
    return pieces.reshape(pieces.shape[0], -1)[:, :width]


def normed(value):
    centred = value - jnp.mean(value, axis=-1, keepdims=True)
    rstd = lax.rsqrt(jnp.mean(centred * centred, axis=-1, keepdims=True) + epsilon)
    return centred * rstd, rstd


def head_place(block, per_shard):
    return block // per_shard, block % per_shard


def forward_body(
    sizes,
    att_ref,
    one_ref,
    two_ref,
    kept_ref,
    mod_ref,
    bias_ref,
    out_bias_ref,
    cot_ref,
    count_ref,
    att_all,
    one_all,
    two_all,
    hidden_one_ref,
    projected_ref,
    mixed_ref,
    attended_ref,
    hidden_all,
    branch_all,
    proj_dense,
    send_z,
    send_y,
    send_x,
    recv_w,
    send_e,
    recv_e,
    local,
):
    n_dp, n_fs, heads, size, cols = sizes
    d_at, f_at = lax.axis_index("dp"), lax.axis_index("fsdp")
    slots, features = kept_ref.shape
    row_width = att_ref.shape[0]
    unit = one_ref.shape[0]
    inner = n_fs // 4
    wide_masks = [inner * step for step in range(1, 4)]
    near_masks = list(range(1, inner))
    dp_masks = []
    mask = n_dp // 2
    while mask:
        dp_masks.append(mask)
        mask //= 2
    low = jnp.bfloat16
    full = jnp.float32
    greet(
        [(d_at, f_at ^ b) for b in wide_masks + near_masks] + [(d_at ^ a, f_at) for a in dp_masks]
    )

    def slot(array, a, b):
        if array == 0:
            start = pl.multiple_of((d_at ^ a) * row_width, 16)
            return att_all.at[f_at ^ b, pl.ds(start, row_width), :]
        start = pl.multiple_of((f_at ^ b) * unit, 16)
        return (one_all if array == 1 else two_all).at[pl.ds(start, unit), :]

    def block(array, a, b):
        if a == 0 and b == 0:
            return (att_ref, one_ref, two_ref)[array]
        return slot(array, a, b)

    started = []

    def send(array, a, b, axis, mask, sem):
        device = (d_at ^ mask, f_at) if axis == 0 else (d_at, f_at ^ mask)
        to_a, to_b = (a ^ mask, b) if axis == 0 else (a, b ^ mask)
        copy = remote(
            block(array, a, b), slot(array, a, b), sem, recv_w.at[array, to_a, to_b], device
        )
        copy.start()
        started.append(copy)

    def arrive(array, a, b):
        place = slot(array, a, b)
        pltpu.make_async_copy(place, place, recv_w.at[array, a, b]).wait()

    def send_wide(array):
        for place, mask in enumerate(wide_masks):
            send(array, 0, 0, 1, mask, send_z.at[array, place])

    def send_near(array, wide, place):
        for step, mask in enumerate(near_masks):
            send(array, 0, wide, 1, mask, send_y.at[array, place, step])

    send_wide(0)
    send_near(0, 0, 0)
    send_wide(1)
    send_wide(2)

    def onward(a, b):
        for step, mask in enumerate(dp_masks):
            if a & (mask | (mask - 1)) == 0:
                send(0, a, b, 0, mask, send_x.at[a, b, step])

    onward(0, 0)
    keep_own = pltpu.make_async_copy(att_ref, slot(0, 0, 0), local.at[1])
    keep_own.start()
    keep_one = pltpu.make_async_copy(one_ref, slot(1, 0, 0), local.at[2])
    keep_one.start()
    keep_two = pltpu.make_async_copy(two_ref, slot(2, 0, 0), local.at[3])
    keep_two.start()

    kept = kept_ref[...]
    mods = [mod_ref[row : row + 1, :] for row in range(6)]
    normed_one, _ = normed(kept)
    hidden_one = (normed_one * (1.0 + mods[1]) + mods[0]).astype(low)
    hidden_one_ref[...] = hidden_one
    branch_all[0] = (mods[5] * cot_ref[...].astype(full)).astype(low)

    for mask in near_masks:
        arrive(0, 0, mask)
        onward(0, mask)
    for place, wide in enumerate(wide_masks):
        arrive(0, 0, wide)
        send_near(0, wide, place + 1)
        onward(0, wide)
    send_near(1, 0, 0)
    send_near(2, 0, 0)
    for wide in wide_masks:
        for mask in near_masks:
            arrive(0, 0, wide ^ mask)
            onward(0, wide ^ mask)
    order = sorted(range(1, n_dp), key=lambda a: (-(a & -a), a))
    for a in order:
        for b in range(n_fs):
            arrive(0, a, b)
            onward(a, b)
    keep_own.wait()

    def spread(buffer, kind):
        held = [0]
        for step, mask in enumerate(dp_masks):
            copies = []
            for key in held:
                copies.append(
                    remote(
                        buffer.at[key],
                        buffer.at[key ^ mask],
                        send_e.at[kind, key ^ mask],
                        recv_e.at[kind, key ^ mask],
                        (d_at ^ mask, f_at),
                    )
                )
                copies[-1].start()
            yield copies
            held = sorted(held + [key ^ mask for key in held])

    for copies in spread(branch_all, 0):
        for copy in copies:
            copy.wait()

    per_shard = cols // size
    for f in range(n_fs):
        out = jnp.dot(hidden_one, att_all[f, :, :cols], preferred_element_type=full)
        projected_ref[f] = (out + bias_ref[f]).astype(low)

    allowed = lax.broadcasted_iota(jnp.int32, (slots, slots), 1) < count_ref[0]
    factor = 1.0 / math.sqrt(size)
    for h in range(heads):
        parts = []
        for kind in range(3):
            f, j = head_place(kind * heads + h, per_shard)
            parts.append(projected_ref[f, :, j * size : (j + 1) * size])
        scores = contract(parts[0], parts[1], (1,), (1,)) * factor
        scores = jnp.where(allowed, scores, negative)
        top = jnp.max(scores, axis=-1, keepdims=True)
        exponent = jnp.exp(scores - top)
        softmax = exponent / jnp.sum(exponent, axis=-1, keepdims=True)
        mix = jnp.dot(softmax.astype(low), parts[2], preferred_element_type=full)
        mixed_ref[:, h * size : (h + 1) * size] = mix.astype(low)

    width = proj_dense.shape[1] // n_fs
    for f in range(n_fs):
        proj_dense[:, f * width : (f + 1) * width] = att_all[f, :, cols : cols + width]
    attended = (
        jnp.dot(mixed_ref[...], proj_dense[...], preferred_element_type=full) + out_bias_ref[...]
    )
    attended_ref[...] = attended
    middle = kept + mods[2] * attended
    normed_two, _ = normed(middle)
    hidden_all[0] = (normed_two * (1.0 + mods[4]) + mods[3]).astype(low)
    for copies in spread(hidden_all, 1):
        for copy in copies:
            copy.wait()

    for array in (1, 2):
        for place, wide in enumerate(wide_masks):
            arrive(array, 0, wide)
            send_near(array, wide, place + 1)
    for array in (1, 2):
        for wide in [0] + wide_masks:
            for mask in near_masks:
                arrive(array, 0, wide ^ mask)
    keep_one.wait()
    keep_two.wait()
    for copy in started:
        copy.wait_send()


def forward_kernel(att, one_block, two_block, kept, mods, bias, out_bias, cot, count, cols):
    n_dp, n_fs = lax.axis_size("dp"), lax.axis_size("fsdp")
    slots, features = kept.shape
    unit = one_block.shape[0]
    size = features // HEADS
    inner = n_fs // 4
    low, full = jnp.bfloat16, jnp.float32
    vmem = pl.BlockSpec(memory_space=pltpu.VMEM)
    shapes = [
        ((n_fs, features, att.shape[1]), low),
        ((n_fs * unit, features), low),
        ((n_fs * two_block.shape[0], two_block.shape[1]), low),
        ((slots, features), low),
        ((n_fs, slots, cols), low),
        ((slots, features), low),
        ((slots, features), full),
        ((n_dp, slots, features), low),
        ((n_dp, slots, features), low),
        ((features, features), low),
    ]
    return pl.pallas_call(
        functools.partial(forward_body, (n_dp, n_fs, HEADS, size, cols)),
        out_shape=[jax.ShapeDtypeStruct(shape, kind) for shape, kind in shapes],
        in_specs=[vmem] * 8 + [pl.BlockSpec(memory_space=pltpu.SMEM)],
        out_specs=[vmem] * len(shapes),
        scratch_shapes=[
            pltpu.SemaphoreType.DMA((3, 3)),
            pltpu.SemaphoreType.DMA((3, 4, max(inner - 1, 1))),
            pltpu.SemaphoreType.DMA((n_dp, n_fs, n_dp.bit_length() - 1)),
            pltpu.SemaphoreType.DMA((3, n_dp, n_fs)),
            pltpu.SemaphoreType.DMA((2, n_dp)),
            pltpu.SemaphoreType.DMA((2, n_dp)),
            pltpu.SemaphoreType.DMA((4,)),
        ],
        compiler_params=pltpu.CompilerParams(
            collective_id=5, has_side_effects=True, vmem_limit_bytes=64 * 1024 * 1024 - 65536
        ),
        name="forward",
    )(att, one_block, two_block, kept, mods, bias, out_bias, cot, count)


def gelu_parts(raised):
    square = raised * raised
    inner = 0.7978845608028654 * raised * (1.0 + 0.044715 * square)
    bend = jnp.tanh(inner)
    slope = 0.7978845608028654 * (1.0 + 3.0 * 0.044715 * square)
    half = 0.5 * (1.0 + bend)
    return raised * half, half + 0.5 * raised * (1.0 - bend * bend) * slope


def column_sums(value):
    return jnp.sum(value, axis=0, keepdims=True)


def backward_body(
    sizes,
    att_hbm,
    proj_ref,
    one_ref,
    two_ref,
    hidden_one_ref,
    projected_ref,
    mixed_ref,
    attended_ref,
    hidden_all,
    branch_all,
    kept_ref,
    mod_ref,
    one_bias_ref,
    out_bias_ref,
    cot_ref,
    count_ref,
    block_ref,
    d_kept_ref,
    d_mod_ref,
    one_out,
    two_out,
    att_out,
    qkv_sums,
    wide_sums,
    act_ref,
    d_raised_ref,
    part_ref,
    core_got,
    cross_put,
    cross_got,
    grad_one,
    grad_two,
    grad_att,
    mlp_y,
    mlp_z,
    att_y,
    att_z,
    rows_put,
    rows_got,
    d_att_all,
    d_mixed_ref,
    d_proj_all,
    weight_ring,
    send_m,
    recv_m,
    send_d,
    recv_d,
    send_e,
    recv_e,
    send_p,
    recv_p,
    local,
):
    heads, size, cols = sizes
    n_dp, n_fs = 4, 8
    d_at, f_at = lax.axis_index("dp"), lax.axis_index("fsdp")
    slots, features = kept_ref.shape
    row_width = features // n_dp
    unit = one_out.shape[0]
    width = features // n_fs
    wide_masks = [2, 4, 6]
    low = jnp.bfloat16
    full = jnp.float32
    core, cross, near = (d_at ^ 1, f_at), (d_at ^ 2, f_at), (d_at, f_at ^ 1)
    greet([core, cross, (d_at ^ 3, f_at), near] + [(d_at, f_at ^ b) for b in wide_masks])
    sent = []

    def push(source, target, send, recv, device):
        copy = remote(source, target, send, recv, device)
        copy.start()
        sent.append(copy)
        return copy

    def arrive(place, recv):
        pltpu.make_async_copy(place, place, recv).wait()

    for kind, source in enumerate((hidden_one_ref, mixed_ref)):
        for piece in range(n_dp):
            rows_put[kind, piece] = source[:, piece * row_width : (piece + 1) * row_width]

    def image_step(image, carry):
        raised = contract(hidden_all[image], one_ref[...], (1,), (1,)) + one_bias_ref[...]
        active, slope = gelu_parts(raised)
        act_ref[image] = active.astype(low)
        d_active = jnp.dot(branch_all[image], two_ref[...], preferred_element_type=full)
        d_raised_ref[image] = (d_active * slope).astype(low)
        return carry

    lax.fori_loop(0, n_dp, image_step, 0)

    def flat(ref, start, count):
        return ref[:, :, pl.ds(start, count)].reshape(n_dp * slots, count)

    def weight_grad(target, left, right):
        step = features // 3
        for part in range(3):
            target[part * step : (part + 1) * step, :] = rows_rows(
                flat(left, part * step, step), flat(right, 0, features)
            ).astype(low)

    def block_rows(index):
        return pl.ds(pl.multiple_of(index * unit, 16), unit)

    def send_blocks(kind, grad):
        for place, wide in enumerate([0] + wide_masks):
            push(
                grad.at[block_rows(f_at ^ wide ^ 1), :],
                mlp_y.at[kind, place],
                send_m.at[kind, place],
                recv_m.at[kind, place],
                near,
            )

    def fold_blocks(kind, grad):
        for place, wide in enumerate([0] + wide_masks):
            arrive(mlp_y.at[kind, place], recv_m.at[kind, place])
            rows = block_rows(f_at ^ wide)
            grad[rows, :] = (
                grad[rows, :].astype(full) + mlp_y[kind, place].astype(full)
            ).astype(low)
            if wide:
                push(
                    grad.at[rows, :],
                    mlp_z.at[kind, place - 1],
                    send_m.at[kind, 3 + place],
                    recv_m.at[kind, 3 + place],
                    (d_at, f_at ^ wide),
                )

    def finish_blocks(kind, grad, target):
        total = grad[block_rows(f_at), :].astype(full)
        for place in range(3):
            arrive(mlp_z.at[kind, place], recv_m.at[kind, 4 + place])
            total = total + mlp_z[kind, place].astype(full)
        target[...] = total

    weight_grad(grad_two, branch_all, act_ref)
    send_blocks(1, grad_two)

    for kind in range(2):
        for mask in (2, 3, 1):
            push(
                rows_put.at[kind, d_at ^ mask],
                rows_got.at[kind, mask],
                send_p.at[kind, mask],
                recv_p.at[kind, mask],
                (d_at ^ mask, f_at),
            )
        keep = pltpu.make_async_copy(rows_put.at[kind, d_at], rows_got.at[kind, 0], local.at[0])
        keep.start()
        keep.wait()

    def part_step(left, right, dims):
        def step(image, carry):
            part_ref[image] = contract(left[image], right[...], (1,), dims).astype(low)
            return carry

        lax.fori_loop(0, n_dp, step, 0)

    def core_send(kind):
        return [
            push(
                part_ref.at[image],
                core_got.at[kind, place],
                send_d.at[kind, place],
                recv_d.at[kind, place],
                core,
            )
            for place, image in enumerate((3, 1))
        ]

    def cross_send(kind):
        arrive(core_got.at[kind, 0], recv_d.at[kind, 0])
        cross_put[kind] = (
            part_ref[2].astype(full) + core_got[kind, 0].astype(full)
        ).astype(low)
        push(
            cross_put.at[kind], cross_got.at[kind], send_d.at[kind, 2], recv_d.at[kind, 2], cross
        )
        arrive(core_got.at[kind, 1], recv_d.at[kind, 1])

    part_step(d_raised_ref, one_ref, (0,))
    leaving = core_send(0)
    cross_send(0)
    own_part = part_ref[0].astype(full) + core_got[0, 1].astype(full)
    weight_grad(grad_one, d_raised_ref, hidden_all)
    send_blocks(0, grad_one)
    fold_blocks(1, grad_two)
    one_sum = jnp.zeros((1, features), full)
    for image in range(n_dp):
        one_sum = one_sum + column_sums(d_raised_ref[image].astype(full))
    wide_sums[0:1, :] = one_sum
    wide_sums[1:2, :] = column_sums(branch_all[0].astype(full))

    mods = [mod_ref[row : row + 1, :] for row in range(6)]
    kept = kept_ref[...]
    attended = attended_ref[...]
    middle = kept + mods[2] * attended
    normed_two, rstd_two = normed(middle)
    upstream = cot_ref[...].astype(full)
    arrive(cross_got.at[0], recv_d.at[0, 2])
    d_hidden_two = own_part + cross_got[0].astype(full)
    d_mod_ref[3:4, :] = column_sums(d_hidden_two)
    d_mod_ref[4:5, :] = column_sums(d_hidden_two * normed_two)
    d_middle = upstream + norm_back(d_hidden_two * (1.0 + mods[4]), normed_two, rstd_two)
    d_mod_ref[2:3, :] = column_sums(d_middle * attended)
    d_attended = (mods[2] * d_middle).astype(low)
    d_att_all[0] = d_attended
    d_kept_ref[...] = d_middle
    wide_sums[2:3, :] = column_sums(d_attended.astype(full))
    d_mixed_ref[...] = contract(d_attended, proj_ref[...], (1,), (1,)).astype(low)
    push(d_att_all.at[0], d_att_all.at[2], send_e.at[2], recv_e.at[2], cross)
    push(d_att_all.at[0], d_att_all.at[1], send_e.at[1], recv_e.at[1], core)

    for copy in leaving:
        copy.wait_send()
    part_step(act_ref, two_ref, (1,))
    core_send(1)
    cross_send(1)
    fold_blocks(0, grad_one)

    per_shard = cols // size
    allowed = lax.broadcasted_iota(jnp.int32, (slots, slots), 1) < count_ref[0]
    factor = 1.0 / math.sqrt(size)
    for h in range(heads):
        places = [head_place(kind * heads + h, per_shard) for kind in range(3)]
        q, k, v = [projected_ref[f, :, j * size : (j + 1) * size] for f, j in places]
        d_mix = d_mixed_ref[:, h * size : (h + 1) * size]
        scores = contract(q, k, (1,), (1,)) * factor
        scores = jnp.where(allowed, scores, negative)
        exponent = jnp.exp(scores - jnp.max(scores, axis=-1, keepdims=True))
        softmax = exponent / jnp.sum(exponent, axis=-1, keepdims=True)
        d_softmax = contract(d_mix, v, (1,), (1,))
        delta = jnp.sum(d_softmax * softmax, axis=-1, keepdims=True)
        d_scores = (softmax * (d_softmax - delta)).astype(low)
        results = [
            jnp.dot(d_scores, k, preferred_element_type=full) * factor,
            rows_rows(d_scores, q) * factor,
            rows_rows(softmax.astype(low), d_mix),
        ]
        for (f, j), result in zip(places, results):
            d_proj_all[0, f, :, j * size : (j + 1) * size] = result.astype(low)

    for f in range(n_fs):
        push(
            d_proj_all.at[0, f], d_proj_all.at[2, f], send_p.at[2 + f, 2], recv_p.at[2 + f, 2], cross
        )
        push(
            d_proj_all.at[0, f], d_proj_all.at[1, f], send_p.at[2 + f, 1], recv_p.at[2 + f, 1], core
        )
    arrive(d_att_all.at[2], recv_e.at[2])
    push(d_att_all.at[2], d_att_all.at[3], send_e.at[3], recv_e.at[3], core)

    loads = [
        pltpu.make_async_copy(att_hbm.at[f], weight_ring.at[f % 2], local.at[1 + f % 2])
        for f in range(n_fs)
    ]
    loads[0].start()
    d_hidden_one = jnp.zeros((slots, features), full)
    for f in range(n_fs):
        if f + 1 < n_fs:
            loads[f + 1].start()
        loads[f].wait()
        own = d_proj_all[0, f]
        d_hidden_one = d_hidden_one + contract(
            own, weight_ring[f % 2, :, :cols], (1,), (1,)
        )
        qkv_sums[f] = column_sums(own.astype(full))
        arrive(d_proj_all.at[2, f], recv_p.at[2 + f, 2])
        push(
            d_proj_all.at[2, f], d_proj_all.at[3, f], send_p.at[2 + f, 3], recv_p.at[2 + f, 3], core
        )
    normed_one, rstd_one = normed(kept)
    d_mod_ref[0:1, :] = column_sums(d_hidden_one)
    d_mod_ref[1:2, :] = column_sums(d_hidden_one * normed_one)
    d_kept_ref[...] = d_kept_ref[...] + norm_back(
        d_hidden_one * (1.0 + mods[1]), normed_one, rstd_one
    )

    for kind in range(2):
        for mask in (2, 3, 1):
            arrive(rows_got.at[kind, mask], recv_p.at[kind, mask])
    for mask in (1, 3):
        arrive(d_att_all.at[mask], recv_e.at[mask])
    grad_proj = rows_rows(
        rows_got[1].reshape(n_dp * slots, row_width),
        d_att_all[...].reshape(n_dp * slots, features),
    ).astype(low)
    for f in range(n_fs):
        grad_att[f, :, cols : cols + width] = grad_proj[:, f * width : (f + 1) * width]
    for f in range(n_fs):
        for mask in (1, 3):
            arrive(d_proj_all.at[mask, f], recv_p.at[2 + f, mask])

    def qkv_grad(f):
        grad_att[f, :, :cols] = rows_rows(
            rows_got[0].reshape(n_dp * slots, row_width),
            d_proj_all[:, f].reshape(n_dp * slots, cols),
        ).astype(low)

    for place, wide in enumerate([0] + wide_masks):
        qkv_grad(f_at ^ wide ^ 1)
        push(
            grad_att.at[f_at ^ wide ^ 1],
            att_y.at[place],
            send_m.at[2, place],
            recv_m.at[2, place],
            near,
        )
    for wide in [0] + wide_masks:
        qkv_grad(f_at ^ wide)
    for place, wide in enumerate([0] + wide_masks):
        arrive(att_y.at[place], recv_m.at[2, place])
        index = f_at ^ wide
        grad_att[index] = (grad_att[index].astype(full) + att_y[place].astype(full)).astype(low)
        if wide:
            push(
                grad_att.at[index],
                att_z.at[place - 1],
                send_m.at[2, 3 + place],
                recv_m.at[2, 3 + place],
                (d_at, index),
            )

    arrive(cross_got.at[1], recv_d.at[1, 2])
    branch = (
        part_ref[0].astype(full)
        + core_got[1, 1].astype(full)
        + cross_got[1].astype(full)
        + out_bias_ref[...]
    )
    d_mod_ref[5:6, :] = column_sums(upstream * branch)
    block_ref[...] = (middle + mods[5] * branch).astype(low)
    finish_blocks(1, grad_two, two_out)
    finish_blocks(0, grad_one, one_out)
    total = grad_att[f_at].astype(full)
    for place in range(3):
        arrive(att_z.at[place], recv_m.at[2, 4 + place])
        total = total + att_z[place].astype(full)
    att_out[...] = total
    for copy in sent:
        if not any(copy is gone for gone in leaving):
            copy.wait_send()


def backward_kernel(
    att_all, proj, one_full, two_full, forward, kept, mods, one_bias, out_bias, cot, count, cols
):
    hidden_one, projected, mixed, attended, hidden_all, branch_all = forward
    n_dp, n_fs = lax.axis_size("dp"), lax.axis_size("fsdp")
    slots, features = kept.shape
    row_width = features // n_dp
    unit = features // n_fs
    att_cols = att_all.shape[2]
    low, full = jnp.bfloat16, jnp.float32
    vmem = pl.BlockSpec(memory_space=pltpu.VMEM)
    shapes = [
        ((slots, features), low),
        ((slots, features), full),
        ((8, features), full),
        ((unit, features), full),
        ((unit, features), full),
        ((row_width, att_cols), full),
        ((n_fs, 1, cols), full),
        ((8, features), full),
    ]
    image = (slots, features)
    scratch = [
        (n_dp,) + image,
        (n_dp,) + image,
        (n_dp,) + image,
        (2, 2) + image,
        (2,) + image,
        (2,) + image,
        (features, features),
        (features, features),
        (n_fs, row_width, att_cols),
        (2, 4, unit, features),
        (2, 3, unit, features),
        (4, row_width, att_cols),
        (3, row_width, att_cols),
        (2, n_dp, slots, row_width),
        (2, n_dp, slots, row_width),
        (n_dp,) + image,
        image,
        (n_dp, n_fs, slots, cols),
        (2, features, att_cols),
    ]
    dma = pltpu.SemaphoreType.DMA
    return pl.pallas_call(
        functools.partial(backward_body, (HEADS, features // HEADS, cols)),
        out_shape=[jax.ShapeDtypeStruct(shape, kind) for shape, kind in shapes],
        in_specs=[pl.BlockSpec(memory_space=pl.ANY)]
        + [vmem] * 14
        + [pl.BlockSpec(memory_space=pltpu.SMEM)],
        out_specs=[vmem] * len(shapes),
        scratch_shapes=[pltpu.VMEM(shape, low) for shape in scratch]
        + [dma((3, 7)), dma((3, 7)), dma((2, 3)), dma((2, 3)), dma((4,)), dma((4,))]
        + [dma((2 + n_fs, 4)), dma((2 + n_fs, 4)), dma((3,))],
        compiler_params=pltpu.CompilerParams(
            collective_id=6, has_side_effects=True, vmem_limit_bytes=64 * 1024 * 1024 - 65536
        ),
        name="backward",
    )(
        att_all,
        proj,
        one_full,
        two_full,
        hidden_one,
        projected,
        mixed,
        attended,
        hidden_all,
        branch_all,
        kept,
        mods,
        one_bias,
        out_bias,
        cot,
        count,
    )


def shards(
    patches_in,
    condition,
    keep_count,
    keep_index,
    w_ada,
    b_ada,
    w_qkv,
    qv_bias,
    w_proj,
    w_fc1,
    fc1_bias,
    w_fc2,
    out_bias,
    cotangent,
):
    n_dp, n_fs = lax.axis_size("dp"), lax.axis_size("fsdp")
    n_all = n_dp * n_fs
    d_at, f_at = lax.axis_index("dp"), lax.axis_index("fsdp")
    kept_slots = keep_index.shape[1]
    features = patches_in.shape[2]
    hidden_units = w_fc2.shape[0] * n_dp
    head_size = features // HEADS
    factor = 1.0 / math.sqrt(head_size)
    head_shape = (kept_slots, HEADS, head_size)
    row_width = features // n_dp
    low = jnp.bfloat16
    full = jnp.float32

    unit_width = w_fc1.shape[1] // n_dp
    one_pieces = w_fc1.reshape(row_width, n_dp, unit_width).transpose(1, 2, 0)
    two_pieces = (
        w_fc2.reshape(n_fs // n_dp, n_dp, unit_width, w_fc2.shape[1])
        .transpose(1, 3, 0, 2)
        .reshape(n_dp, w_fc2.shape[1], -1)
    )
    both_pieces = jnp.concatenate([one_pieces, two_pieces], axis=2)
    cond_float = condition.astype(full)
    signal = swish(cond_float).astype(low)
    message = jnp.concatenate(
        [signal, b_ada[None], qv_bias[None], fc1_bias[None], out_bias[None]], axis=1
    )
    sizes = [features, b_ada.shape[0], qv_bias.shape[0], fc1_bias.shape[0], out_bias.shape[0]]
    ends = [sum(sizes[: place + 1]) for place in range(len(sizes))]
    shared = exchange_everyone(
        jnp.broadcast_to(tiles(message, 16), (n_all, 16, 128)), 1
    )
    shared = untiles(shared, ends[-1])
    both = trade(both_pieces, "dp")
    one_block = both[:, :, :row_width].transpose(1, 0, 2).reshape(unit_width, features)
    two_block = (
        both[:, :, row_width:].transpose(1, 0, 2).reshape(w_fc2.shape[1], hidden_units // n_dp)
    )
    signals = lax.dynamic_slice_in_dim(shared[:, :features], d_at * row_width, row_width, 1)
    ada_bias, qv_full, one_bias, out_full = [
        shared[:, ends[place] : ends[place + 1]].reshape(-1).astype(full) for place in range(4)
    ]

    partial_mod = jnp.dot(signals, w_ada, preferred_element_type=full)
    rows_mod = untiles(exchange_everyone(tiles(partial_mod, 8), 2), partial_mod.shape[1])
    modulation = jnp.sum(rows_mod.reshape(n_dp, n_fs, -1), axis=0).reshape(1, -1) + ada_bias
    mods = modulation.reshape(6, features)
    shift_one, scale_one, gate_one, shift_two, scale_two, gate_two = [
        mods[row : row + 1] for row in range(6)
    ]
    own_one_bias = pick(
        one_bias.reshape(n_fs, n_dp, unit_width).transpose(1, 0, 2), d_at
    ).reshape(-1)

    indices = keep_index[0]
    inputs = patches_in[0]
    kept_in = jnp.take(inputs, indices, axis=0).astype(full)
    qkv_bias = jnp.concatenate(
        [qv_full[:features], jnp.zeros((features,), full), qv_full[features:]]
    )
    qkv_cols = w_qkv.shape[1]
    (
        att_all,
        one_full,
        two_full,
        hidden_one,
        projected_all,
        mixed_low,
        attended,
        hidden_two_all,
        d_branch_all,
        proj_full,
    ) = forward_kernel(
        jnp.concatenate([w_qkv, w_proj], axis=1),
        one_block,
        two_block,
        kept_in,
        mods,
        qkv_bias.reshape(n_fs, 1, qkv_cols),
        out_full[None, :features],
        cotangent[0],
        keep_count,
        qkv_cols,
    )
    (
        block_out,
        d_kept,
        d_mods,
        final_one,
        final_two,
        att_out,
        qkv_sums,
        wide_sums,
    ) = backward_kernel(
        att_all,
        proj_full,
        one_full,
        two_full,
        (hidden_one, projected_all, mixed_low, attended, hidden_two_all, d_branch_all),
        kept_in,
        mods,
        own_one_bias[None],
        out_full[None, features:],
        cotangent[0],
        keep_count,
        qkv_cols,
    )
    qkv_out = att_out[:, :qkv_cols]
    proj_out = att_out[:, qkv_cols:]
    grad_patches = jnp.zeros(inputs.shape, full).at[indices].set(d_kept, unique_indices=True)[None]
    one_out = trade(
        final_one.astype(low).reshape(unit_width, n_dp, row_width).transpose(1, 0, 2), "dp"
    )
    one_out = one_out.reshape(-1, row_width).T.astype(full)
    two_out = trade(
        final_two.astype(low).reshape(final_two.shape[0], n_dp, -1).transpose(1, 0, 2), "dp"
    )
    two_out = (
        two_out.reshape(n_dp, final_two.shape[0], n_fs // n_dp, unit_width)
        .transpose(2, 0, 3, 1)
        .reshape(w_fc2.shape)
        .astype(full)
    )

    d_modulation = d_mods[:6].reshape(-1).astype(low)
    group_d = trade(d_modulation.reshape(n_fs, -1), "fsdp")
    all_d = spread_small(group_d, "dp").reshape(n_all, -1)
    grad_ada = rows_rows(signals, all_d)
    part_signal = times_transposed(all_d, w_ada).reshape(n_dp, n_fs, row_width)
    group_signal = jnp.sum(trade(part_signal.transpose(1, 0, 2), "fsdp"), axis=0)
    d_signal = trade(group_signal, "dp").reshape(1, features)
    unused_too, swish_pull = jax.vjp(swish, cond_float)
    grad_condition = swish_pull(d_signal)[0]

    sums = qkv_sums.reshape(-1)
    one_spread = jnp.zeros((n_fs, n_dp, unit_width), full)
    one_spread = lax.dynamic_update_index_in_dim(
        one_spread, wide_sums[0].reshape(n_fs, unit_width), d_at, 1
    )
    bias_parts = [
        d_modulation.astype(full),
        jnp.concatenate([sums[:features], sums[2 * features :]]),
        one_spread.reshape(-1),
        jnp.concatenate([wide_sums[2], wide_sums[1]]),
    ]
    bias_all = jnp.concatenate([part.reshape(n_all, -1) for part in bias_parts], axis=1)
    bias_all = bias_all.reshape(n_dp, n_fs, -1)
    bias_group = jnp.sum(trade(bias_all.transpose(1, 0, 2), "fsdp"), axis=0)
    bias_own = jnp.sum(trade(bias_group, "dp"), axis=0)
    starts = [end - features for end in ends]
    ada_out, qv_out, bias_out, out_out = [
        bias_own[starts[place] : starts[place + 1]] for place in range(4)
    ]
    return (
        block_out[None],
        grad_patches,
        grad_condition,
        grad_ada,
        ada_out,
        qkv_out,
        qv_out,
        proj_out,
        one_out,
        bias_out,
        two_out,
        out_out,
    )


def kernels_fit(*arrays):
    w_qkv, w_fc1 = arrays[6], arrays[9]
    features = arrays[0].shape[2]
    unit_width = w_fc1.shape[1] // lax.axis_size("dp")
    return (
        w_qkv.shape[1] % (features // HEADS) == 0
        and w_qkv.shape[0] % 16 == 0
        and unit_width % 16 == 0
        and unit_width == arrays[11].shape[1]
        and lax.axis_size("dp") == 4
        and lax.axis_size("fsdp") == 8
    )


def solution(mesh):
    both = ("dp", "fsdp")
    weight = P("dp", "fsdp")
    flat = P(both)
    placed = (
        P(both, None, None),
        P(both, None),
        flat,
        P(both, None),
        weight,
        flat,
        weight,
        flat,
        weight,
        weight,
        flat,
        weight,
        flat,
        P(both, None, None),
    )

    def chosen(*arrays):
        return (shards if kernels_fit(*arrays) else plain_shards)(*arrays)

    return jax.shard_map(
        chosen,
        mesh=mesh,
        in_specs=placed,
        out_specs=(
            P(both, None, None),
            P(both, None, None),
            P(both, None),
            weight,
            flat,
            weight,
            flat,
            weight,
            weight,
            flat,
            weight,
            flat,
        ),
        check_vma=False,
    )
```

```python
import functools
import math

import jax
import jax.numpy as jnp
from jax import lax
from jax.experimental import pallas as pl
from jax.experimental.pallas import tpu as pltpu
from jax.sharding import PartitionSpec as P

HEADS = 16


epsilon = 1e-06
negative = -1e30


def layer_norm(inputs):
    centred = inputs - jnp.mean(inputs, axis=-1, keepdims=True)
    rstd = lax.rsqrt(jnp.mean(centred * centred, axis=-1, keepdims=True) + epsilon)
    return (centred * rstd, rstd)


def norm_back(upstream, normed, rstd):
    return rstd * (
        upstream
        - jnp.mean(upstream, axis=-1, keepdims=True)
        - normed * jnp.mean(upstream * normed, axis=-1, keepdims=True)
    )


def swish(inputs):
    return inputs / (1.0 + jnp.exp(-inputs))


def gelu_tanh(inputs):
    return (
        0.5
        * inputs
        * (1.0 + jnp.tanh(0.7978845608028654 * (inputs + 0.044715 * inputs * inputs * inputs)))
    )


def contract(left, right, left_dims, right_dims):
    return lax.dot_general(
        left, right, ((left_dims, right_dims), ((), ())), preferred_element_type=jnp.float32
    )


def rows_rows(left, right):
    return contract(left, right, (0,), (0,))


def times_transposed(left, right):
    return contract(left, right, (1,), (1,))


def inner_rows(left, right):
    return lax.dot_general(
        left, right, (((0,), (0,)), ((), ())), preferred_element_type=jnp.float32
    )


def flat_bias(collected):
    return collected.reshape(-1)


def gather_forward(w_ada, b_ada, w_qkv, qv_bias, w_proj, w_fc1, fc1_bias, w_fc2, out_bias):
    part_ada, part_qkv, part_proj, part_one, part_two, bias_ada, bias_qv, bias_one, bias_out = (
        lax.all_gather(w_ada, "fsdp", axis=1, tiled=True),
        lax.all_gather(w_qkv, "fsdp", axis=1, tiled=True),
        lax.all_gather(w_proj, "fsdp", axis=1, tiled=True),
        lax.all_gather(w_fc1, "fsdp", axis=1, tiled=True),
        lax.all_gather(w_fc2, "fsdp", axis=1, tiled=True),
        lax.all_gather(b_ada.reshape(1, 1, -1), "fsdp", axis=1, tiled=True),
        lax.all_gather(qv_bias.reshape(1, 1, -1), "fsdp", axis=1, tiled=True),
        lax.all_gather(fc1_bias.reshape(1, 1, -1), "fsdp", axis=1, tiled=True),
        lax.all_gather(out_bias.reshape(1, 1, -1), "fsdp", axis=1, tiled=True),
    )
    gathered = (
        lax.all_gather(part_ada, "dp", axis=0, tiled=True),
        lax.all_gather(part_qkv, "dp", axis=0, tiled=True),
        lax.all_gather(part_proj, "dp", axis=0, tiled=True),
        lax.all_gather(part_one, "dp", axis=0, tiled=True),
        lax.all_gather(part_two, "dp", axis=0, tiled=True),
        lax.all_gather(bias_ada, "dp", axis=0, tiled=True),
        lax.all_gather(bias_qv, "dp", axis=0, tiled=True),
        lax.all_gather(bias_one, "dp", axis=0, tiled=True),
        lax.all_gather(bias_out, "dp", axis=0, tiled=True),
    )
    return (
        gathered[0],
        flat_bias(gathered[5]),
        gathered[1],
        flat_bias(gathered[6]),
        gathered[2],
        gathered[3],
        flat_bias(gathered[7]),
        gathered[4],
        flat_bias(gathered[8]),
    )


def gather_backward(w_ada, w_qkv, w_proj, w_fc1, w_fc2):
    part_ada, part_qkv, part_proj, part_one, part_two = (
        lax.all_gather(w_ada, "fsdp", axis=1, tiled=True),
        lax.all_gather(w_qkv, "fsdp", axis=1, tiled=True),
        lax.all_gather(w_proj, "fsdp", axis=1, tiled=True),
        lax.all_gather(w_fc1, "fsdp", axis=1, tiled=True),
        lax.all_gather(w_fc2, "fsdp", axis=1, tiled=True),
    )
    return (
        lax.all_gather(part_ada, "dp", axis=0, tiled=True),
        lax.all_gather(part_qkv, "dp", axis=0, tiled=True),
        lax.all_gather(part_proj, "dp", axis=0, tiled=True),
        lax.all_gather(part_one, "dp", axis=0, tiled=True),
        lax.all_gather(part_two, "dp", axis=0, tiled=True),
    )


def split_bias(term):
    return term.reshape(lax.axis_size("dp"), lax.axis_size("fsdp"), -1)


def own_bias(summed):
    return lax.dynamic_index_in_dim(summed, lax.axis_index("dp"), 0, keepdims=False).reshape(-1)


def owned_columns(matrix, width):
    return lax.dynamic_slice_in_dim(matrix, lax.axis_index("dp") * width, width, 1)


def column_totals(matrix):
    return jnp.sum(matrix.astype(jnp.float32), axis=0)


def plain_shards(
    patches_in,
    condition,
    keep_count,
    keep_index,
    w_ada,
    b_ada,
    w_qkv,
    qv_bias,
    w_proj,
    w_fc1,
    fc1_bias,
    w_fc2,
    out_bias,
    cotangent,
):
    images, kept_slots = keep_index.shape
    features = patches_in.shape[2]
    hidden_units = w_fc2.shape[0] * lax.axis_size("dp")
    all_rows = images * kept_slots
    head_size = features // HEADS
    factor = 1.0 / math.sqrt(head_size)
    head_shape = (images, kept_slots, HEADS, head_size)
    row_width = features // lax.axis_size("dp")
    unit_width = hidden_units // lax.axis_size("dp")
    ada_full, ada_bias, qkv_full, qv_full, proj_full, one_full, one_bias, two_full, out_full = (
        gather_forward(w_ada, b_ada, w_qkv, qv_bias, w_proj, w_fc1, fc1_bias, w_fc2, out_bias)
    )
    inputs = patches_in.astype(jnp.float32)
    kept_in = jnp.take_along_axis(inputs, keep_index[:, :, None], axis=1)
    allowed = (jnp.arange(kept_slots)[None, :] < keep_count[:, None])[:, None, None, :]
    cond_float = condition.astype(jnp.float32)
    signal = swish(cond_float).astype(jnp.bfloat16)
    modulation = jnp.dot(signal, ada_full, preferred_element_type=jnp.float32) + ada_bias.astype(
        jnp.float32
    )
    shift_one, scale_one, gate_one, shift_two, scale_two, gate_two = [
        modulation[:, None, column * features : (column + 1) * features] for column in range(6)
    ]
    normed_one, rstd_one = layer_norm(kept_in)
    hidden_one = (
        (normed_one * (1.0 + scale_one) + shift_one)
        .astype(jnp.bfloat16)
        .reshape(all_rows, features)
    )
    qv_float = qv_full.astype(jnp.float32)
    qkv_bias = jnp.concatenate(
        [qv_float[:features], jnp.zeros((features,), jnp.float32), qv_float[features:]]
    )
    projected = (
        jnp.dot(hidden_one, qkv_full, preferred_element_type=jnp.float32) + qkv_bias
    ).astype(jnp.bfloat16)
    queries = projected[:, :features].reshape(head_shape)
    key_rows = projected[:, features : 2 * features].reshape(head_shape)
    values = projected[:, 2 * features :].reshape(head_shape)
    scores = (
        jnp.einsum("iqhe,ikhe->ihqk", queries, key_rows, preferred_element_type=jnp.float32)
        * factor
    )
    scores = jnp.where(allowed, scores, negative)
    top_score = jnp.max(scores, axis=-1, keepdims=True)
    exponent = jnp.exp(scores - top_score)
    row_total = jnp.sum(exponent, axis=-1, keepdims=True)
    log_total = top_score + jnp.log(row_total)
    softmax_low = (exponent / row_total).astype(jnp.bfloat16)
    mixed = jnp.einsum("ihqk,ikhe->iqhe", softmax_low, values, preferred_element_type=jnp.float32)
    mixed_low = mixed.reshape(all_rows, features).astype(jnp.bfloat16)
    out_float = out_full.astype(jnp.float32)
    attended = (
        jnp.dot(mixed_low, proj_full, preferred_element_type=jnp.float32) + out_float[:features]
    ).reshape(images, kept_slots, features)
    middle = kept_in + gate_one * attended
    normed_two, rstd_two = layer_norm(middle)
    hidden_two = (
        (normed_two * (1.0 + scale_two) + shift_two)
        .astype(jnp.bfloat16)
        .reshape(all_rows, features)
    )
    raised = jnp.dot(hidden_two, one_full, preferred_element_type=jnp.float32) + one_bias.astype(
        jnp.float32
    )
    activated = gelu_tanh(raised).astype(jnp.bfloat16)
    branch = (
        jnp.dot(activated, two_full, preferred_element_type=jnp.float32) + out_float[features:]
    ).reshape(images, kept_slots, features)
    block_out = (middle + gate_two * branch).astype(jnp.bfloat16)
    ada_back, qkv_back, proj_back, one_back, two_back = gather_backward(
        w_ada, w_qkv, w_proj, w_fc1, w_fc2
    )
    upstream = cotangent.astype(jnp.float32)
    d_gate_two = jnp.sum(upstream * branch, axis=1)
    d_branch = (gate_two * upstream).reshape(all_rows, features).astype(jnp.bfloat16)
    d_activated = times_transposed(d_branch, two_back)
    unused, gelu_pull = jax.vjp(gelu_tanh, raised)
    d_raised = gelu_pull(d_activated)[0].astype(jnp.bfloat16)
    d_hidden_two = times_transposed(d_raised, one_back).reshape(images, kept_slots, features)
    d_shift_two = jnp.sum(d_hidden_two, axis=1)
    d_scale_two = jnp.sum(d_hidden_two * normed_two, axis=1)
    d_middle = upstream + norm_back(d_hidden_two * (1.0 + scale_two), normed_two, rstd_two)
    d_gate_one = jnp.sum(d_middle * attended, axis=1)
    d_attended = (gate_one * d_middle).reshape(all_rows, features).astype(jnp.bfloat16)
    d_mixed = times_transposed(d_attended, proj_back).astype(jnp.bfloat16).reshape(head_shape)
    scores_again = (
        jnp.einsum("iqhe,ikhe->ihqk", queries, key_rows, preferred_element_type=jnp.float32)
        * factor
    )
    scores_again = jnp.where(allowed, scores_again, negative)
    softmax_again = jnp.exp(scores_again - log_total)
    d_softmax = jnp.einsum("iqhe,ikhe->ihqk", d_mixed, values, preferred_element_type=jnp.float32)
    row_delta = jnp.sum(d_softmax * softmax_again, axis=-1, keepdims=True)
    d_scores = (softmax_again * (d_softmax - row_delta)).astype(jnp.bfloat16)
    d_queries = (
        jnp.einsum("ihqk,ikhe->iqhe", d_scores, key_rows, preferred_element_type=jnp.float32)
        * factor
    )
    d_keys = (
        jnp.einsum("ihqk,iqhe->ikhe", d_scores, queries, preferred_element_type=jnp.float32)
        * factor
    )
    d_values = jnp.einsum(
        "ihqk,iqhe->ikhe",
        softmax_again.astype(jnp.bfloat16),
        d_mixed,
        preferred_element_type=jnp.float32,
    )
    d_projected = jnp.concatenate(
        [
            d_queries.reshape(all_rows, features),
            d_keys.reshape(all_rows, features),
            d_values.reshape(all_rows, features),
        ],
        axis=1,
    ).astype(jnp.bfloat16)
    d_hidden_one = times_transposed(d_projected, qkv_back).reshape(images, kept_slots, features)
    d_shift_one = jnp.sum(d_hidden_one, axis=1)
    d_scale_one = jnp.sum(d_hidden_one * normed_one, axis=1)
    d_kept = d_middle + norm_back(d_hidden_one * (1.0 + scale_one), normed_one, rstd_one)
    grad_patches = jnp.zeros_like(inputs).at[jnp.arange(images)[:, None], keep_index].add(d_kept)
    d_modulation = jnp.concatenate(
        [d_shift_one, d_scale_one, d_gate_one, d_shift_two, d_scale_two, d_gate_two], axis=1
    ).astype(jnp.bfloat16)
    d_signal = times_transposed(d_modulation, ada_back)
    unused_too, swish_pull = jax.vjp(swish, cond_float)
    grad_condition = swish_pull(d_signal)[0]
    piece_one = lax.all_gather(hidden_one, "dp", axis=0, tiled=True)
    piece_proj_d = lax.all_gather(d_projected, "dp", axis=0, tiled=True)
    piece_mixed = lax.all_gather(mixed_low, "dp", axis=0, tiled=True)
    piece_att_d = lax.all_gather(d_attended, "dp", axis=0, tiled=True)
    piece_two = lax.all_gather(hidden_two, "dp", axis=0, tiled=True)
    piece_raised_d = lax.all_gather(d_raised, "dp", axis=0, tiled=True)
    piece_act = lax.all_gather(activated, "dp", axis=0, tiled=True)
    piece_branch_d = lax.all_gather(d_branch, "dp", axis=0, tiled=True)
    grad_qkv = inner_rows(owned_columns(piece_one, row_width), piece_proj_d)
    grad_proj = inner_rows(owned_columns(piece_mixed, row_width), piece_att_d)
    grad_one = inner_rows(owned_columns(piece_two, row_width), piece_raised_d)
    grad_two = inner_rows(owned_columns(piece_act, unit_width), piece_branch_d)
    qkv_sums = column_totals(piece_proj_d)
    proj_sums = column_totals(piece_att_d)
    one_sums = column_totals(piece_raised_d)
    two_sums = column_totals(piece_branch_d)
    piece_signal = lax.all_gather(signal, "dp", axis=0, tiled=True)
    piece_mod_d = lax.all_gather(d_modulation, "dp", axis=0, tiled=True)
    grad_ada = inner_rows(owned_columns(piece_signal, row_width), piece_mod_d)
    ada_sums = column_totals(piece_mod_d)
    grad_qv = jnp.concatenate([qkv_sums[:features], qkv_sums[2 * features :]])
    grad_out = jnp.concatenate([proj_sums, two_sums])
    terms = (
        grad_ada,
        grad_qkv,
        grad_proj,
        grad_one,
        grad_two,
        split_bias(ada_sums),
        split_bias(grad_qv),
        split_bias(one_sums),
        split_bias(grad_out),
    )
    (
        final_ada,
        final_qkv,
        final_proj,
        final_one,
        final_two,
        final_ada_bias,
        final_qv,
        final_bias,
        final_out,
    ) = (
        lax.psum_scatter(
            terms[0].astype(jnp.bfloat16), "fsdp", scatter_dimension=1, tiled=True
        ).astype(jnp.float32),
        lax.psum_scatter(
            terms[1].astype(jnp.bfloat16), "fsdp", scatter_dimension=1, tiled=True
        ).astype(jnp.float32),
        lax.psum_scatter(
            terms[2].astype(jnp.bfloat16), "fsdp", scatter_dimension=1, tiled=True
        ).astype(jnp.float32),
        lax.psum_scatter(
            terms[3].astype(jnp.bfloat16), "fsdp", scatter_dimension=1, tiled=True
        ).astype(jnp.float32),
        lax.psum_scatter(
            terms[4].astype(jnp.bfloat16), "fsdp", scatter_dimension=1, tiled=True
        ).astype(jnp.float32),
        lax.psum_scatter(
            terms[5].astype(jnp.bfloat16), "fsdp", scatter_dimension=1, tiled=True
        ).astype(jnp.float32),
        lax.psum_scatter(
            terms[6].astype(jnp.bfloat16), "fsdp", scatter_dimension=1, tiled=True
        ).astype(jnp.float32),
        lax.psum_scatter(
            terms[7].astype(jnp.bfloat16), "fsdp", scatter_dimension=1, tiled=True
        ).astype(jnp.float32),
        lax.psum_scatter(
            terms[8].astype(jnp.bfloat16), "fsdp", scatter_dimension=1, tiled=True
        ).astype(jnp.float32),
    )
    return (
        block_out,
        grad_patches,
        grad_condition,
        final_ada,
        own_bias(final_ada_bias),
        final_qkv,
        own_bias(final_qv),
        final_proj,
        final_one,
        own_bias(final_bias),
        final_two,
        own_bias(final_out),
    )


MESH = pl.DeviceIdType.MESH


def remote(source, target, send, recv, device):
    return pltpu.make_async_remote_copy(
        src_ref=source,
        dst_ref=target,
        send_sem=send,
        recv_sem=recv,
        device_id=device,
        device_id_type=MESH,
    )


def greet(devices):
    barrier = pltpu.get_barrier_semaphore()
    for device in devices:
        pl.semaphore_signal(barrier, 1, device_id=device, device_id_type=MESH)
    pl.semaphore_wait(barrier, len(devices))


def normed(value):
    centred = value - jnp.mean(value, axis=-1, keepdims=True)
    rstd = lax.rsqrt(jnp.mean(centred * centred, axis=-1, keepdims=True) + epsilon)
    return centred * rstd, rstd


def forward_body(
    sizes,
    note_ref,
    ada_ref,
    piece_ref,
    qkv_ref,
    proj_ref,
    kept_ref,
    cot_ref,
    count_ref,
    qkv_all,
    one_all,
    two_all,
    projected_ref,
    attended_ref,
    hidden_all,
    branch_all,
    proj_dense,
    hidden_rows,
    mixed_rows,
    mod_ref,
    bias_ref,
    signal_ref,
    proj_all,
    mixed_ref,
    piece_got,
    one_block,
    two_block,
    note_got,
    row_put,
    row_got,
    send_n,
    recv_n,
    send_z,
    send_y,
    send_x,
    recv_w,
    send_e,
    recv_e,
    local,
):
    heads, size, widths = sizes
    n_dp, n_fs = 4, 8
    d_at, f_at = lax.axis_index("dp"), lax.axis_index("fsdp")
    own_at = d_at * n_fs + f_at
    slots, features = kept_ref.shape
    half_rows, cols = qkv_ref.shape[0], qkv_ref.shape[1] // 2
    unit = one_block.shape[0]
    row_width = 2 * half_rows
    width = proj_ref.shape[1] // 2
    low = jnp.bfloat16
    full = jnp.float32
    others = [(a, b) for a in range(n_dp) for b in range(n_fs) if a or b]
    greet([(d_at ^ a, f_at ^ b) for a, b in others])

    own_blocks = (qkv_ref, proj_ref, one_block, two_block)
    gathered = (qkv_all, proj_all, one_all, two_all)
    started = []

    def slot(array, a, b):
        if array < 2:
            start = pl.multiple_of((d_at ^ a) * half_rows, 16)
            return gathered[array].at[f_at ^ b, pl.ds(start, half_rows), :]
        start = pl.multiple_of((f_at ^ b) * unit, 16)
        return gathered[array].at[pl.ds(start, unit), :]

    def push(source, target, send, recv, device):
        copy = remote(source, target, send, recv, device)
        copy.start()
        started.append(copy)

    def pass_on(array, a, b, axis, mask, sem):
        device = (d_at ^ mask, f_at) if axis == 0 else (d_at, f_at ^ mask)
        to_a, to_b = (a ^ mask, b) if axis == 0 else (a, b ^ mask)
        source = own_blocks[array] if a == 0 and b == 0 else slot(array, a, b)
        push(source, slot(array, a, b), sem, recv_w.at[array, to_a, to_b], device)

    def arrive(array, a, b):
        place = slot(array, a, b)
        pltpu.make_async_copy(place, place, recv_w.at[array, a, b]).wait()

    def wide(array):
        for mask in (2, 4, 6):
            pass_on(array, 0, 0, 1, mask, send_z.at[array, mask // 2 - 1])

    def near(array, b):
        pass_on(array, 0, b, 1, 1, send_y.at[array, b // 2])

    def onward(array, a, b):
        if a == 0:
            pass_on(array, a, b, 0, 2, send_x.at[array, 0, b])
        if a in (0, 2):
            pass_on(array, a, b, 0, 1, send_x.at[array, 1 + a // 2, b])

    near(0, 0)
    wide(0)
    onward(0, 0, 0)
    for place, (a, b) in enumerate(others):
        push(
            note_ref.at[d_at ^ a],
            note_got.at[own_at],
            send_n.at[0, place],
            recv_n.at[0, place],
            (d_at ^ a, f_at ^ b),
        )
    stays = [
        pltpu.make_async_copy(note_ref.at[d_at], note_got.at[own_at], local.at[0]),
        pltpu.make_async_copy(qkv_ref, slot(0, 0, 0), local.at[1]),
        pltpu.make_async_copy(proj_ref, slot(1, 0, 0), local.at[2]),
        pltpu.make_async_copy(piece_ref.at[d_at], piece_got.at[d_at], local.at[3]),
    ]
    for stay in stays:
        stay.start()
    wide(1)
    for mask in (1, 2, 3):
        push(
            piece_ref.at[d_at ^ mask],
            piece_got.at[d_at],
            send_e.at[2, mask],
            recv_e.at[2, mask],
            (d_at ^ mask, f_at),
        )

    kept = kept_ref[...]
    normed_one, _ = normed(kept)

    stays[0].wait()
    for place, (a, b) in enumerate(others):
        at = (d_at ^ a) * n_fs + (f_at ^ b)
        pltpu.make_async_copy(note_got.at[at], note_got.at[at], recv_n.at[0, place]).wait()
    notes = note_got[...]
    signals = jnp.concatenate([notes[:, row, :] for row in range(3)], axis=1).astype(low)
    signal_ref[...] = signals
    terms = jnp.dot(signals, ada_ref[...], preferred_element_type=full)
    ada_width = widths[0]
    ada_piece = ada_width * n_fs // (n_dp * n_fs)

    def bias_piece(index, start, count):
        row = note_got[index]
        line = jnp.concatenate([row[3 + step : 4 + step, :] for step in range(5)], axis=1)
        return line[:, start : start + count]

    block_bias = jnp.concatenate(
        [bias_piece(f_at * n_dp + step, 0, ada_piece) for step in range(n_dp)], axis=1
    )
    first = (d_at == 0).astype(full)
    for row in range(7):
        piece = terms[:, row * 128 : (row + 1) * 128]
        count = min(128, ada_width - row * 128)
        add = block_bias[:, row * 128 : row * 128 + count] * first
        if count < 128:
            add = jnp.concatenate([add, jnp.zeros((1, 128 - count), full)], axis=1)
        row_put[:, row, :] = piece + add
    for place, (a, b) in enumerate(others):
        push(
            row_put.at[(d_at ^ a) * n_fs + (f_at ^ b)],
            row_got.at[own_at],
            send_n.at[1, place],
            recv_n.at[1, place],
            (d_at ^ a, f_at ^ b),
        )
    keep_row = pltpu.make_async_copy(row_put.at[own_at], row_got.at[own_at], local.at[0])
    keep_row.start()

    arrive(0, 0, 1)
    onward(0, 0, 1)
    arrive(0, 0, 2)
    near(0, 2)
    onward(0, 0, 2)

    qv_width, one_width, out_width = widths[1:]
    starts = [ada_piece, ada_piece + qv_width, ada_piece + qv_width + one_width]
    lines = []
    for index in range(n_dp * n_fs):
        lines.append(
            (
                bias_piece(index, starts[0], qv_width),
                bias_piece(index, starts[2], out_width),
            )
        )
    heads_per = cols // size
    for f in range(n_fs):
        parts = []
        for j in range(heads_per):
            head = f * heads_per + j
            if head < heads:
                parts.append(lines[head][0])
            elif head < 2 * heads:
                parts.append(jnp.zeros((1, size), full))
            else:
                parts.append(lines[head - heads][0])
        bias_ref[f : f + 1, :cols] = jnp.concatenate(parts, axis=1)
    bias_ref[8:9, :] = jnp.concatenate([line[1] for line in lines[:heads]], axis=1)
    bias_ref[9:10, :] = jnp.concatenate([line[1] for line in lines[heads:]], axis=1)
    bias_ref[10:11, :] = jnp.concatenate(
        [bias_piece(f * n_dp + d_at, starts[1], one_width) for f in range(n_fs)], axis=1
    )

    arrive(0, 0, 4)
    near(0, 4)
    onward(0, 0, 4)
    arrive(0, 0, 3)
    onward(0, 0, 3)

    keep_row.wait()
    for place, (a, b) in enumerate(others):
        at = (d_at ^ a) * n_fs + (f_at ^ b)
        pltpu.make_async_copy(row_got.at[at], row_got.at[at], recv_n.at[1, place]).wait()
    sums = row_got[0:n_fs]
    for d in range(1, n_dp):
        sums = sums + row_got[d * n_fs : (d + 1) * n_fs]
    sums = jnp.concatenate([sums[:, row, :] for row in range(7)], axis=1)
    pieces = []
    for index in range(6 * n_dp):
        f, third = index // 3, index % 3
        pieces.append(sums[f : f + 1, third * row_width : (third + 1) * row_width])
    mods = []
    for row in range(6):
        mods.append(jnp.concatenate(pieces[row * n_dp : (row + 1) * n_dp], axis=1))
        mod_ref[row : row + 1, :] = mods[row]
    hidden_one = (normed_one * (1.0 + mods[1]) + mods[0]).astype(low)
    branch_all[0] = (mods[5] * cot_ref[...].astype(full)).astype(low)
    chunks = [
        hidden_one[:, place * half_rows : (place + 1) * half_rows] for place in range(2 * n_dp)
    ]
    for d in range(n_dp):
        hidden_rows[d] = jnp.concatenate(chunks[2 * d : 2 * d + 2], axis=1)
    halves = [jnp.concatenate(chunks[part::2], axis=1) for part in range(2)]

    stays[3].wait()
    for mask in (1, 2, 3):
        place = piece_got.at[d_at ^ mask]
        pltpu.make_async_copy(place, place, recv_e.at[2, mask]).wait()
    one_block[...] = jnp.concatenate([piece_got[d, :, :row_width] for d in range(n_dp)], axis=1)
    two_block[...] = jnp.concatenate([piece_got[d, :, row_width:] for d in range(n_dp)], axis=1)

    arrive(0, 0, 6)
    near(0, 6)
    onward(0, 0, 6)
    near(1, 0)
    arrive(0, 0, 5)
    onward(0, 0, 5)
    arrive(0, 0, 7)
    onward(0, 0, 7)
    onward(1, 0, 0)
    arrive(1, 0, 1)
    onward(1, 0, 1)
    arrive(1, 0, 2)
    near(1, 2)
    onward(1, 0, 2)
    wide(2)
    wide(3)
    keep_one = pltpu.make_async_copy(one_block, slot(2, 0, 0), local.at[0])
    keep_one.start()
    keep_two = pltpu.make_async_copy(two_block, slot(3, 0, 0), local.at[3])
    keep_two.start()
    arrive(1, 0, 4)
    near(1, 4)
    onward(1, 0, 4)
    arrive(1, 0, 3)
    onward(1, 0, 3)
    arrive(1, 0, 6)
    near(1, 6)
    onward(1, 0, 6)
    near(2, 0)
    arrive(1, 0, 5)
    onward(1, 0, 5)
    arrive(1, 0, 7)
    onward(1, 0, 7)

    def spread_step(buffer, kind, mask):
        for key in [0] if mask == 2 else [0, 2]:
            push(
                buffer.at[key],
                buffer.at[key ^ mask],
                send_e.at[kind, key ^ mask],
                recv_e.at[kind, key ^ mask],
                (d_at ^ mask, f_at),
            )

    def spread_wait(buffer, kind, keys):
        for key in keys:
            place = buffer.at[key]
            pltpu.make_async_copy(place, place, recv_e.at[kind, key]).wait()

    stays[1].wait()
    order = [0, 1, 2, 4, 3, 6, 5, 7]
    for place, b in enumerate(order):
        arrive(0, 2, b)
        onward(0, 2, b)
        arrive(0, 1, b)
        arrive(0, 3, b)
        f = f_at ^ b
        out = jnp.dot(halves[0], qkv_all[f, :, :cols], preferred_element_type=full)
        out = out + jnp.dot(halves[1], qkv_all[f, :, cols:], preferred_element_type=full)
        projected_ref[f] = (out + bias_ref[pl.ds(f, 1), :cols]).astype(low)
    spread_step(branch_all, 0, 2)

    relays = []
    for array in (2, 3):
        for mask in (2, 4, 6):
            relays.append((array, mask))

    def relay():
        array, mask = relays.pop(0)
        arrive(array, 0, mask)
        near(array, mask)
        if (array, mask) == (2, 6):
            near(3, 0)

    allowed = lax.broadcasted_iota(jnp.int32, (slots, slots), 1) < count_ref[0]
    factor = 1.0 / math.sqrt(size)
    for h in range(heads):
        q, k, v = [
            projected_ref[f, :, j * size : (j + 1) * size]
            for f, j in (
                ((kind * heads + h) // heads_per, (kind * heads + h) % heads_per)
                for kind in range(3)
            )
        ]
        scores = contract(q, k, (1,), (1,)) * factor
        scores = jnp.where(allowed, scores, negative)
        exponent = jnp.exp(scores - jnp.max(scores, axis=-1, keepdims=True))
        softmax = exponent / jnp.sum(exponent, axis=-1, keepdims=True)
        mix = jnp.dot(softmax.astype(low), v, preferred_element_type=full).astype(low)
        pair, side = h // 2, h % 2
        start = ((pair % 2) * n_dp + pair // 2) * half_rows + side * size
        mixed_ref[:, start : start + size] = mix
        start = (pair % 2) * half_rows + side * size
        mixed_rows[pair // 2, :, start : start + size] = mix
        if h in (3, 7, 11):
            relay()
        if h == 8:
            spread_wait(branch_all, 0, [2])
            spread_step(branch_all, 0, 1)

    for b in order:
        arrive(1, 2, b)
        onward(1, 2, b)
    stays[2].wait()
    for b in order:
        arrive(1, 1, b)
        arrive(1, 3, b)
    for f in range(n_fs):
        for part in range(2):
            proj_dense[
                part * n_dp * half_rows : (part + 1) * n_dp * half_rows,
                f * width : (f + 1) * width,
            ] = proj_all[f, :, part * width : (part + 1) * width]
    attended = (
        jnp.dot(mixed_ref[...], proj_dense[...], preferred_element_type=full) + bias_ref[8:9, :]
    )
    attended_ref[...] = attended
    middle = kept + mods[2] * attended
    normed_two, _ = normed(middle)
    hidden_all[0] = (normed_two * (1.0 + mods[4]) + mods[3]).astype(low)
    spread_step(hidden_all, 1, 2)
    relay()
    spread_wait(hidden_all, 1, [2])
    spread_step(hidden_all, 1, 1)
    relay()
    relay()
    spread_wait(hidden_all, 1, [1, 3])
    spread_wait(branch_all, 0, [1, 3])
    for array in (2, 3):
        for b in (1, 3, 5, 7):
            arrive(array, 0, b)
    keep_one.wait()
    keep_two.wait()
    for copy in started:
        copy.wait_send()


def forward_kernel(notes, ada, pieces, qkv, proj, kept, cot, count, widths):
    n_dp, n_fs = lax.axis_size("dp"), lax.axis_size("fsdp")
    slots, features = kept.shape
    unit = pieces.shape[1]
    size = features // HEADS
    half_rows = qkv.shape[0]
    cols = qkv.shape[1] // 2
    n_all = n_dp * n_fs
    low, full = jnp.bfloat16, jnp.float32
    vmem = pl.BlockSpec(memory_space=pltpu.VMEM)
    shapes = [
        ((n_fs, n_dp * half_rows, 2 * cols), low),
        ((n_fs * unit, features), low),
        ((features, n_fs * unit), low),
        ((n_fs, slots, cols), low),
        ((slots, features), full),
        ((n_dp, slots, features), low),
        ((n_dp, slots, features), low),
        ((features, features), low),
        ((n_dp, slots, 2 * half_rows), low),
        ((n_dp, slots, 2 * half_rows), low),
        ((8, features), full),
        ((16, features), full),
        ((n_all, 384), low),
    ]
    scratch = [
        ((n_fs, n_dp * half_rows, proj.shape[1]), low),
        ((slots, features), low),
        (pieces.shape, low),
        ((unit, features), low),
        ((unit, features), low),
        ((n_all, 8, 128), full),
        ((n_all, 8, 128), full),
        ((n_all, 8, 128), full),
    ]
    dma = pltpu.SemaphoreType.DMA
    return pl.pallas_call(
        functools.partial(forward_body, (HEADS, size, widths)),
        out_shape=[jax.ShapeDtypeStruct(shape, kind) for shape, kind in shapes],
        in_specs=[vmem] * 7 + [pl.BlockSpec(memory_space=pltpu.SMEM)],
        out_specs=[vmem] * len(shapes),
        scratch_shapes=[pltpu.VMEM(shape, kind) for shape, kind in scratch]
        + [dma((2, n_all - 1)), dma((2, n_all - 1)), dma((4, 3)), dma((4, 4))]
        + [dma((2, 3, n_fs)), dma((4, n_dp, n_fs)), dma((3, 4)), dma((3, 4)), dma((4,))],
        compiler_params=pltpu.CompilerParams(
            collective_id=5, has_side_effects=True, vmem_limit_bytes=64 * 1024 * 1024 - 65536
        ),
        name="forward",
    )(notes, ada, pieces, qkv, proj, kept, cot, count)


def gelu_parts(raised):
    square = raised * raised
    inner = 0.7978845608028654 * raised * (1.0 + 0.044715 * square)
    bend = jnp.tanh(inner)
    slope = 0.7978845608028654 * (1.0 + 3.0 * 0.044715 * square)
    half = 0.5 * (1.0 + bend)
    return raised * half, half + 0.5 * raised * (1.0 - bend * bend) * slope


def column_sums(value):
    return jnp.sum(value, axis=0, keepdims=True)


def store_tile(ref, index, line):
    for row in range(8):
        piece = line[:, row * 128 : (row + 1) * 128]
        if piece.shape[1] == 0:
            break
        if piece.shape[1] < 128:
            rest = jnp.zeros((1, 128 - piece.shape[1]), line.dtype)
            piece = jnp.concatenate([piece, rest], axis=1)
        ref[index, row : row + 1, :] = piece


def backward_body(
    sizes,
    qkv_hbm,
    ada_ref,
    signal_ref,
    proj_ref,
    one_ref,
    two_ref,
    projected_ref,
    attended_ref,
    hidden_all,
    branch_all,
    hidden_rows,
    mixed_rows,
    kept_ref,
    mod_ref,
    bias_ref,
    cot_ref,
    count_ref,
    block_ref,
    d_kept_ref,
    mlp_out,
    att_out,
    ada_out,
    last_got,
    act_ref,
    d_raised_ref,
    part_ref,
    core_got,
    cross_put,
    cross_got,
    grads,
    got_y,
    got_z,
    rows_got,
    d_att_all,
    d_mixed_ref,
    d_proj_all,
    weight_ring,
    mlp_put,
    d_mod_ref,
    sum_put,
    sum_got,
    note_put,
    note_got,
    last_put,
    send_m,
    recv_m,
    send_d,
    recv_d,
    send_e,
    recv_e,
    send_p,
    recv_p,
    send_n,
    recv_n,
    send_s,
    recv_s,
    send_b,
    recv_b,
    local,
):
    heads, size, ada_width = sizes
    n_dp, n_fs = 4, 8
    d_at, f_at = lax.axis_index("dp"), lax.axis_index("fsdp")
    own_at = d_at * n_fs + f_at
    slots, features = kept_ref.shape
    cols = projected_ref.shape[2]
    heads_per = cols // size
    row_width = features // n_dp
    half_rows = row_width // 2
    unit = features // n_fs
    low = jnp.bfloat16
    full = jnp.float32
    core, cross, near = (d_at ^ 1, f_at), (d_at ^ 2, f_at), (d_at, f_at ^ 1)
    others = [(a, b) for a in range(n_dp) for b in range(n_fs) if a or b]
    greet([(d_at ^ a, f_at ^ b) for a, b in others])
    sent = []

    def push(source, target, send, recv, device):
        copy = remote(source, target, send, recv, device)
        copy.start()
        sent.append(copy)
        return copy

    def arrive(place, recv):
        pltpu.make_async_copy(place, place, recv).wait()

    stays = []
    for kind, source in enumerate((hidden_rows, mixed_rows)):
        for mask in (2, 3, 1):
            push(
                source.at[d_at ^ mask],
                rows_got.at[kind, mask],
                send_p.at[kind, mask],
                recv_p.at[kind, mask],
                (d_at ^ mask, f_at),
            )
        stays.append(
            pltpu.make_async_copy(source.at[d_at], rows_got.at[kind, 0], local.at[kind])
        )
        stays[kind].start()

    def image_step(image, carry):
        raised = contract(hidden_all[image], one_ref[...], (1,), (1,)) + bias_ref[10:11, :]
        active, slope = gelu_parts(raised)
        act_ref[image] = active.astype(low)
        d_active = jnp.dot(branch_all[image], two_ref[...], preferred_element_type=full)
        d_raised_ref[image] = (d_active * slope).astype(low)
        return carry

    lax.fori_loop(0, n_dp, image_step, 0)

    def flat(ref, start, count):
        return ref[:, :, pl.ds(start, count)].reshape(n_dp * slots, count)

    def weight_grad(kind, left, right):
        step = features // 3
        for part in range(3):
            grads[kind, part * step : (part + 1) * step, :] = rows_rows(
                flat(left, part * step, step), flat(right, 0, features)
            ).astype(low)

    def block_rows(index):
        return pl.ds(pl.multiple_of(index * unit, 16), unit)

    def send_block(kind, place, index):
        push(
            grads.at[kind, block_rows(index), :],
            got_y.at[kind, place],
            send_m.at[kind, place],
            recv_m.at[kind, place],
            near,
        )

    def fold_block(kind, place, index):
        arrive(got_y.at[kind, place], recv_m.at[kind, place])
        rows = block_rows(index)
        grads[kind, rows, :] = (
            grads[kind, rows, :].astype(full) + got_y[kind, place].astype(full)
        ).astype(low)

    def send_wide(kind, index, mask):
        place = mask // 2 - 1
        return remote(
            grads.at[kind, block_rows(index), :],
            got_z.at[kind, place],
            send_m.at[kind, 4 + place],
            recv_m.at[kind, 4 + place],
            (d_at, index),
        )

    def fold_all(kind):
        for place, wide in enumerate((2, 4, 6, 0)):
            fold_block(kind, place, f_at ^ wide)
            if wide:
                copy = send_wide(kind, f_at ^ wide, wide)
                copy.start()
                sent.append(copy)

    def finish(kind):
        total = grads[kind, block_rows(f_at), :].astype(full)
        for place in range(3):
            arrive(got_z.at[kind, place], recv_m.at[kind, 4 + place])
            total = total + got_z[kind, place].astype(full)
        return total

    weight_grad(1, branch_all, act_ref)
    for place, wide in enumerate((2, 4, 6, 0)):
        send_block(1, place, f_at ^ wide ^ 1)

    def part_step(left, right, dims):
        def step(image, carry):
            part_ref[image] = contract(left[image], right[...], (1,), dims).astype(low)
            return carry

        lax.fori_loop(0, n_dp, step, 0)

    def core_send(kind):
        return [
            push(
                part_ref.at[image],
                core_got.at[kind, place],
                send_d.at[kind, place],
                recv_d.at[kind, place],
                core,
            )
            for place, image in enumerate((3, 1))
        ]

    def cross_send(kind):
        arrive(core_got.at[kind, 0], recv_d.at[kind, 0])
        cross_put[kind] = (
            part_ref[2].astype(full) + core_got[kind, 0].astype(full)
        ).astype(low)
        push(
            cross_put.at[kind], cross_got.at[kind], send_d.at[kind, 2], recv_d.at[kind, 2], cross
        )
        arrive(core_got.at[kind, 1], recv_d.at[kind, 1])

    part_step(d_raised_ref, one_ref, (0,))
    leaving = core_send(0)
    cross_send(0)
    own_part = part_ref[0].astype(full) + core_got[0, 1].astype(full)
    weight_grad(0, d_raised_ref, hidden_all)
    for place, wide in enumerate((2, 4, 6, 0)):
        send_block(0, place, f_at ^ wide ^ 1)
    fold_all(1)
    one_sum = jnp.zeros((1, features), full)
    for image in range(n_dp):
        one_sum = one_sum + column_sums(d_raised_ref[image].astype(full))
    branch_sum = column_sums(branch_all[0].astype(full))

    mods = [mod_ref[row : row + 1, :] for row in range(6)]
    kept = kept_ref[...]
    attended = attended_ref[...]
    middle = kept + mods[2] * attended
    normed_two, rstd_two = normed(middle)
    upstream = cot_ref[...].astype(full)
    arrive(cross_got.at[0], recv_d.at[0, 2])
    d_hidden_two = own_part + cross_got[0].astype(full)
    d_mod_ref[3:4, :] = column_sums(d_hidden_two)
    d_mod_ref[4:5, :] = column_sums(d_hidden_two * normed_two)
    d_middle = upstream + norm_back(d_hidden_two * (1.0 + mods[4]), normed_two, rstd_two)
    d_mod_ref[2:3, :] = column_sums(d_middle * attended)
    d_attended = (mods[2] * d_middle).astype(low)
    d_att_all[0] = d_attended
    d_kept_ref[...] = d_middle
    att_sum = column_sums(d_attended.astype(full))
    d_mixed_ref[...] = contract(d_attended, proj_ref[...], (1,), (1,)).astype(low)
    push(d_att_all.at[0], d_att_all.at[2], send_e.at[2], recv_e.at[2], cross)
    push(d_att_all.at[0], d_att_all.at[1], send_e.at[1], recv_e.at[1], core)

    for copy in leaving:
        copy.wait_send()
    part_step(act_ref, two_ref, (1,))
    core_send(1)
    cross_send(1)

    def pass_block(f):
        push(
            d_proj_all.at[0, f],
            d_proj_all.at[2, f],
            send_p.at[2 + f, 2],
            recv_p.at[2 + f, 2],
            cross,
        )
        push(
            d_proj_all.at[0, f],
            d_proj_all.at[1, f],
            send_p.at[2 + f, 1],
            recv_p.at[2 + f, 1],
            core,
        )

    def relay_block(f):
        arrive(d_proj_all.at[2, f], recv_p.at[2 + f, 2])
        push(
            d_proj_all.at[2, f],
            d_proj_all.at[3, f],
            send_p.at[2 + f, 3],
            recv_p.at[2 + f, 3],
            core,
        )

    allowed = lax.broadcasted_iota(jnp.int32, (slots, slots), 1) < count_ref[0]
    factor = 1.0 / math.sqrt(size)
    done_after = {5: [0], 7: [3], 9: [6], 11: [1], 13: [4], 15: [2, 5, 7]}
    relay_after = {11: [0], 13: [3], 15: [6]}
    for h in range(heads):
        places = [
            ((kind * heads + h) // heads_per, (kind * heads + h) % heads_per)
            for kind in range(3)
        ]
        q, k, v = [projected_ref[f, :, j * size : (j + 1) * size] for f, j in places]
        pair, side = h // 2, h % 2
        start = ((pair % 2) * n_dp + pair // 2) * half_rows + side * size
        d_mix = d_mixed_ref[:, start : start + size]
        scores = contract(q, k, (1,), (1,)) * factor
        scores = jnp.where(allowed, scores, negative)
        exponent = jnp.exp(scores - jnp.max(scores, axis=-1, keepdims=True))
        softmax = exponent / jnp.sum(exponent, axis=-1, keepdims=True)
        d_softmax = contract(d_mix, v, (1,), (1,))
        delta = jnp.sum(d_softmax * softmax, axis=-1, keepdims=True)
        d_scores = (softmax * (d_softmax - delta)).astype(low)
        results = [
            jnp.dot(d_scores, k, preferred_element_type=full) * factor,
            rows_rows(d_scores, q) * factor,
            rows_rows(softmax.astype(low), d_mix),
        ]
        for (f, j), result in zip(places, results):
            d_proj_all[0, f, :, j * size : (j + 1) * size] = result.astype(low)
        for f in done_after.get(h, []):
            pass_block(f)
        for f in relay_after.get(h, []):
            relay_block(f)
        if h == 2:
            fold_all(0)
        if h == 6:
            arrive(d_att_all.at[2], recv_e.at[2])
            push(d_att_all.at[2], d_att_all.at[3], send_e.at[3], recv_e.at[3], core)

    for stay in stays:
        stay.wait()
    for kind in range(2):
        for mask in (2, 3, 1):
            arrive(rows_got.at[kind, mask], recv_p.at[kind, mask])
    for mask in (1, 3):
        arrive(d_att_all.at[mask], recv_e.at[mask])
    grad_proj = rows_rows(
        rows_got[1].reshape(n_dp * slots, row_width),
        d_att_all[...].reshape(n_dp * slots, features),
    ).astype(low)
    for f in range(n_fs):
        for part in range(2):
            grads[
                2,
                f * unit : (f + 1) * unit,
                2 * cols + part * unit : 2 * cols + (part + 1) * unit,
            ] = grad_proj[part * half_rows : (part + 1) * half_rows, f * unit : (f + 1) * unit]

    def qkv_grad(f):
        result = rows_rows(
            rows_got[0].reshape(n_dp * slots, row_width),
            d_proj_all[:, f].reshape(n_dp * slots, cols),
        ).astype(low)
        for part in range(2):
            grads[2, block_rows(f), part * cols : (part + 1) * cols] = result[
                part * half_rows : (part + 1) * half_rows, :
            ]

    odd = f_at % 2
    pairs = [(0, 3), (6, 1), (4, 5), (2, 7)]

    def grad_pair(place):
        even_f, odd_f = pairs[place]
        for f in (even_f, odd_f):
            for mask in (1, 3):
                arrive(d_proj_all.at[mask, f], recv_p.at[2 + f, mask])
        goes = jnp.where(odd == 0, odd_f, even_f)
        qkv_grad(goes)
        send_block(2, place, goes)
        qkv_grad(even_f + odd_f - goes)

    def fold_pair(place):
        even_f, odd_f = pairs[place]
        index = jnp.where(odd == 0, even_f, odd_f)
        fold_block(2, place, index)

        @pl.when(index != f_at)
        def _():
            send_wide(2, index, index ^ f_at).start()

    grad_pair(0)
    relay_block(1)
    relay_block(4)
    grad_pair(1)

    loads = [
        pltpu.make_async_copy(qkv_hbm.at[f], weight_ring.at[f % 2], local.at[2 + f % 2])
        for f in range(n_fs)
    ]
    loads[0].start()
    halves = [jnp.zeros((slots, features // 2), full) for part in range(2)]
    for f in range(n_fs):
        if f + 1 < n_fs:
            loads[f + 1].start()
        loads[f].wait()
        own = d_proj_all[0, f]
        for part in range(2):
            halves[part] = halves[part] + contract(
                own, weight_ring[f % 2, :, part * cols : (part + 1) * cols], (1,), (1,)
            )
        line = jnp.concatenate(
            [
                column_sums(own.astype(full)),
                att_sum[:, f * unit : (f + 1) * unit],
                branch_sum[:, f * unit : (f + 1) * unit],
                one_sum[:, f * unit : (f + 1) * unit],
            ],
            axis=1,
        )
        store_tile(sum_put, f, line)
        if f == 3:
            relay_block(2)
        if f == 6:
            relay_block(5)
    relay_block(7)
    d_hidden_one = jnp.concatenate(
        [
            halves[part][:, d * half_rows : (d + 1) * half_rows]
            for d in range(n_dp)
            for part in range(2)
        ],
        axis=1,
    )
    normed_one, rstd_one = normed(kept)
    d_mod_ref[0:1, :] = column_sums(d_hidden_one)
    d_mod_ref[1:2, :] = column_sums(d_hidden_one * normed_one)

    arrive(cross_got.at[1], recv_d.at[1, 2])
    branch = (
        part_ref[0].astype(full)
        + core_got[1, 1].astype(full)
        + cross_got[1].astype(full)
        + bias_ref[9:10, :]
    )
    d_mod_ref[5:6, :] = column_sums(upstream * branch)

    third = ada_width // 3
    pieces = []
    for row in range(6):
        line = d_mod_ref[row : row + 1, :].astype(low).astype(full)
        pieces += [line[:, step * third : (step + 1) * third] for step in range(n_dp)]
    for f in range(n_fs):
        store_tile(note_put, f, jnp.concatenate(pieces[3 * f : 3 * f + 3], axis=1))
    for mask in range(1, n_fs):
        push(
            sum_put.at[f_at ^ mask],
            sum_got.at[mask],
            send_s.at[mask],
            recv_s.at[mask],
            (d_at, f_at ^ mask),
        )
    for place, (a, b) in enumerate(others):
        push(
            note_put.at[f_at ^ b],
            note_got.at[own_at],
            send_n.at[0, place],
            recv_n.at[0, place],
            (d_at ^ a, f_at ^ b),
        )
    keep_note = pltpu.make_async_copy(note_put.at[f_at], note_got.at[own_at], local.at[0])
    keep_note.start()
    keep_sum = pltpu.make_async_copy(sum_put.at[f_at], sum_got.at[0], local.at[1])
    keep_sum.start()
    grad_pair(2)
    fold_pair(0)
    grad_pair(3)
    fold_pair(1)
    d_kept_ref[...] = d_kept_ref[...] + norm_back(
        d_hidden_one * (1.0 + mods[1]), normed_one, rstd_one
    )
    block_ref[...] = (middle + mods[5] * branch).astype(low)

    keep_mlp = []
    for kind in range(2):
        total = finish(kind).astype(low)
        for d in range(n_dp):
            mlp_put[kind, d] = total[:, d * row_width : (d + 1) * row_width]
        for mask in (2, 3, 1):
            push(
                mlp_put.at[kind, d_at ^ mask],
                mlp_out.at[kind, d_at],
                send_b.at[kind, mask],
                recv_b.at[kind, mask],
                (d_at ^ mask, f_at),
            )
        keep_mlp.append(
            pltpu.make_async_copy(
                mlp_put.at[kind, d_at], mlp_out.at[kind, d_at], local.at[2 + kind]
            )
        )
        keep_mlp[kind].start()

    keep_note.wait()
    keep_sum.wait()
    for mask in range(1, n_fs):
        arrive(sum_got.at[mask], recv_s.at[mask])
    for place, (a, b) in enumerate(others):
        at = (d_at ^ a) * n_fs + (f_at ^ b)
        arrive(note_got.at[at], recv_n.at[0, place])
    sums = sum_got[0]
    for mask in range(1, n_fs):
        sums = sums + sum_got[mask]
    notes = note_got[...]
    all_d = jnp.concatenate([notes[:, row, :] for row in range(7)], axis=1)
    totals = column_sums(all_d)
    all_d = all_d.astype(low)
    terms = contract(all_d, ada_ref[...], (1,), (1,))
    for row in range(3):
        last_put[:, row, :] = terms[:, row * 128 : (row + 1) * 128]
    everyone = (n_dp * n_fs, 128)
    for row in range(7):
        last_put[:, 8 + row, :] = jnp.broadcast_to(sums[row : row + 1, :], everyone)
        last_put[:, 16 + row, :] = jnp.broadcast_to(
            totals[:, row * 128 : (row + 1) * 128], everyone
        )
    fold_pair(2)
    for place, (a, b) in enumerate(others):
        push(
            last_put.at[(d_at ^ a) * n_fs + (f_at ^ b)],
            last_got.at[own_at],
            send_n.at[1, place],
            recv_n.at[1, place],
            (d_at ^ a, f_at ^ b),
        )
    keep_last = pltpu.make_async_copy(last_put.at[own_at], last_got.at[own_at], local.at[0])
    keep_last.start()
    fold_pair(3)
    ada_out[...] = rows_rows(signal_ref[...], all_d)[: ada_out.shape[0], : ada_out.shape[1]]
    att_out[...] = finish(2)
    for kind in range(2):
        keep_mlp[kind].wait()
        for mask in (1, 2, 3):
            arrive(mlp_out.at[kind, d_at ^ mask], recv_b.at[kind, mask])
    keep_last.wait()
    for place, (a, b) in enumerate(others):
        at = (d_at ^ a) * n_fs + (f_at ^ b)
        arrive(last_got.at[at], recv_n.at[1, place])
    for copy in sent:
        if not any(copy is gone for gone in leaving):
            copy.wait_send()
    for place in range(3):
        rows = grads.at[2, block_rows(f_at), :]
        pltpu.make_async_copy(rows, rows, send_m.at[2, 4 + place]).wait()


def backward_kernel(forward, ada, kept, cot, count):
    (
        qkv_all,
        one_all,
        two_all,
        projected,
        attended,
        hidden_all,
        branch_all,
        proj_dense,
        hidden_rows,
        mixed_rows,
        mods,
        bias,
        signals,
    ) = forward
    n_dp, n_fs = lax.axis_size("dp"), lax.axis_size("fsdp")
    n_all = n_dp * n_fs
    slots, features = kept.shape
    row_width = features // n_dp
    unit = features // n_fs
    ada_width = 6 * features // n_fs
    cols = projected.shape[2]
    low, full = jnp.bfloat16, jnp.float32
    vmem = pl.BlockSpec(memory_space=pltpu.VMEM)
    image = (slots, features)
    shapes = [
        (image, low),
        (image, full),
        ((2, n_dp, unit, row_width), low),
        ((unit, features), full),
        ((row_width, ada_width), full),
        ((n_all, 24, 128), full),
    ]
    scratch = [
        ((n_dp,) + image, low),
        ((n_dp,) + image, low),
        ((n_dp,) + image, low),
        ((2, 2) + image, low),
        ((2,) + image, low),
        ((2,) + image, low),
        ((3, features, features), low),
        ((3, 4, unit, features), low),
        ((3, 3, unit, features), low),
        ((2, n_dp, slots, row_width), low),
        ((n_dp,) + image, low),
        (image, low),
        ((n_dp, n_fs, slots, cols), low),
        ((2,) + qkv_all.shape[1:], low),
        ((2, n_dp, unit, row_width), low),
        ((8, features), full),
        ((n_fs, 8, 128), full),
        ((n_fs, 8, 128), full),
        ((n_fs, 8, 128), full),
        ((n_all, 8, 128), full),
        ((n_all, 24, 128), full),
    ]
    dma = pltpu.SemaphoreType.DMA
    sems = [(3, 7), (2, 3), (4,), (2 + n_fs, 4), (2, n_all - 1), (n_fs,), (2, 4)]
    return pl.pallas_call(
        functools.partial(backward_body, (HEADS, features // HEADS, ada_width)),
        out_shape=[jax.ShapeDtypeStruct(shape, kind) for shape, kind in shapes],
        in_specs=[pl.BlockSpec(memory_space=pl.ANY)]
        + [vmem] * 15
        + [pl.BlockSpec(memory_space=pltpu.SMEM)],
        out_specs=[vmem] * len(shapes),
        scratch_shapes=[pltpu.VMEM(shape, kind) for shape, kind in scratch]
        + [dma(shape) for shape in sems for side in range(2)]
        + [dma((4,))],
        compiler_params=pltpu.CompilerParams(
            collective_id=6, has_side_effects=True, vmem_limit_bytes=64 * 1024 * 1024 - 65536
        ),
        name="backward",
    )(
        qkv_all,
        ada,
        signals,
        proj_dense,
        one_all,
        two_all,
        projected,
        attended,
        hidden_all,
        branch_all,
        hidden_rows,
        mixed_rows,
        kept,
        mods,
        bias,
        cot,
        count,
    )


def shards(
    patches_in,
    condition,
    keep_count,
    keep_index,
    w_ada,
    b_ada,
    w_qkv,
    qv_bias,
    w_proj,
    w_fc1,
    fc1_bias,
    w_fc2,
    out_bias,
    cotangent,
):
    n_dp, n_fs = lax.axis_size("dp"), lax.axis_size("fsdp")
    n_all = n_dp * n_fs
    d_at, f_at = lax.axis_index("dp"), lax.axis_index("fsdp")
    features = patches_in.shape[2]
    row_width = features // n_dp
    half_rows = row_width // 2
    low = jnp.bfloat16
    full = jnp.float32

    unit_width = w_fc1.shape[1] // n_dp
    one_pieces = w_fc1.reshape(row_width, n_dp, unit_width).transpose(1, 2, 0)
    two_pieces = (
        w_fc2.reshape(n_fs // n_dp, n_dp, unit_width, w_fc2.shape[1])
        .transpose(1, 3, 0, 2)
        .reshape(n_dp, w_fc2.shape[1], -1)
    )
    pieces = jnp.concatenate([one_pieces, two_pieces], axis=2)

    def beside(shard):
        return jnp.concatenate([shard[:half_rows], shard[half_rows:]], axis=1)

    cond_float = condition.astype(full)
    signal = swish(cond_float).astype(low).astype(full)
    shards_bias = [b_ada, qv_bias, fc1_bias, out_bias]
    biases = jnp.concatenate(shards_bias).astype(full)
    notes = jnp.concatenate(
        [
            jnp.pad(signal.reshape(n_dp, row_width), ((0, 0), (0, 384 - row_width))),
            jnp.broadcast_to(jnp.pad(biases, (0, 640 - biases.shape[0])), (n_dp, 640)),
        ],
        axis=1,
    ).reshape(n_dp, 8, 128)
    ada_width = w_ada.shape[1]
    ada = jnp.pad(w_ada, ((0, 384 - row_width), (0, 896 - ada_width)))

    indices = keep_index[0]
    inputs = patches_in[0]
    kept_in = jnp.take(inputs, indices, axis=0).astype(full)
    forward = forward_kernel(
        notes,
        ada,
        pieces,
        beside(w_qkv),
        beside(w_proj),
        kept_in,
        cotangent[0],
        keep_count,
        (ada_width, qv_bias.shape[0], fc1_bias.shape[0], out_bias.shape[0]),
    )
    block_out, d_kept, mlp_out, att_out, grad_ada, last = backward_kernel(
        forward, ada, kept_in, cotangent[0], keep_count
    )
    grad_patches = jnp.zeros(inputs.shape, full).at[indices].set(d_kept, unique_indices=True)[None]

    qkv_cols, proj_cols = w_qkv.shape[1], w_proj.shape[1]

    def above(left, width):
        return jnp.concatenate(
            [att_out[:, left : left + width], att_out[:, left + width : left + 2 * width]], axis=0
        )

    one_out = mlp_out[0].reshape(-1, row_width).T.astype(full)
    two_out = (
        mlp_out[1]
        .reshape(n_dp, w_fc2.shape[1], n_fs // n_dp, unit_width)
        .transpose(2, 0, 3, 1)
        .reshape(w_fc2.shape)
        .astype(full)
    )

    last = last.reshape(n_dp, n_fs, 3, -1)
    d_signal = jnp.sum(last[:, :, 0, :row_width], axis=1).reshape(1, features)
    unused, swish_pull = jax.vjp(swish, cond_float)
    grad_condition = swish_pull(d_signal)[0]
    own = d_at * n_fs + f_at
    head_size = qv_bias.shape[0]
    heads_per = qkv_cols // head_size

    def line_of(kind, d, f):
        start = (d, f, kind, 0)
        return lax.dynamic_slice(last, start, (1, 1, 1, last.shape[3])).reshape(-1)

    def summed(f):
        start = (0, f, 1, 0)
        return jnp.sum(
            lax.dynamic_slice(last, start, (n_dp, 1, 1, last.shape[3])).reshape(n_dp, -1), axis=0
        )

    ada_count = b_ada.shape[0]
    ada_bias = lax.dynamic_slice_in_dim(
        line_of(2, d_at, own // n_dp), (own % n_dp) * ada_count, ada_count
    )
    block = jnp.where(own < HEADS, own, own + HEADS)
    qv_out = lax.dynamic_slice_in_dim(
        summed(block // heads_per), (block % heads_per) * head_size, head_size
    )
    per = proj_cols // head_size
    place = own % HEADS
    start = jnp.where(own < HEADS, qkv_cols, qkv_cols + proj_cols) + (place % per) * head_size
    out_out = lax.dynamic_slice_in_dim(summed(place // per), start, head_size)
    bias_out = lax.dynamic_slice_in_dim(
        line_of(1, own % n_dp, own // n_dp), qkv_cols + 2 * proj_cols, unit_width
    )
    return (
        block_out[None],
        grad_patches,
        grad_condition,
        grad_ada,
        ada_bias,
        above(0, qkv_cols),
        qv_out,
        above(2 * qkv_cols, proj_cols),
        one_out,
        bias_out,
        two_out,
        out_out,
    )


def kernels_fit(*arrays):
    w_qkv, w_fc1 = arrays[6], arrays[9]
    features = arrays[0].shape[2]
    unit_width = w_fc1.shape[1] // lax.axis_size("dp")
    return (
        w_qkv.shape[1] % (features // HEADS) == 0
        and w_qkv.shape[0] % 16 == 0
        and unit_width % 16 == 0
        and unit_width == arrays[11].shape[1]
        and lax.axis_size("dp") == 4
        and lax.axis_size("fsdp") == 8
    )


def solution(mesh):
    both = ("dp", "fsdp")
    weight = P("dp", "fsdp")
    flat = P(both)
    placed = (
        P(both, None, None),
        P(both, None),
        flat,
        P(both, None),
        weight,
        flat,
        weight,
        flat,
        weight,
        weight,
        flat,
        weight,
        flat,
        P(both, None, None),
    )

    def chosen(*arrays):
        return (shards if kernels_fit(*arrays) else plain_shards)(*arrays)

    return jax.shard_map(
        chosen,
        mesh=mesh,
        in_specs=placed,
        out_specs=(
            P(both, None, None),
            P(both, None, None),
            P(both, None),
            weight,
            flat,
            weight,
            flat,
            weight,
            weight,
            flat,
            weight,
            flat,
        ),
        check_vma=False,
    )
```

```python
import functools
import math

import jax
import jax.numpy as jnp
from jax import lax
from jax.experimental import pallas as pl
from jax.experimental.pallas import tpu as pltpu
from jax.sharding import PartitionSpec as P

HEADS = 16


epsilon = 1e-06
negative = -1e30


def layer_norm(inputs):
    centred = inputs - jnp.mean(inputs, axis=-1, keepdims=True)
    rstd = lax.rsqrt(jnp.mean(centred * centred, axis=-1, keepdims=True) + epsilon)
    return (centred * rstd, rstd)


def norm_back(upstream, normed, rstd):
    return rstd * (
        upstream
        - jnp.mean(upstream, axis=-1, keepdims=True)
        - normed * jnp.mean(upstream * normed, axis=-1, keepdims=True)
    )


def swish(inputs):
    return inputs / (1.0 + jnp.exp(-inputs))


def gelu_tanh(inputs):
    return (
        0.5
        * inputs
        * (1.0 + jnp.tanh(0.7978845608028654 * (inputs + 0.044715 * inputs * inputs * inputs)))
    )


def contract(left, right, left_dims, right_dims):
    return lax.dot_general(
        left, right, ((left_dims, right_dims), ((), ())), preferred_element_type=jnp.float32
    )


def rows_rows(left, right):
    return contract(left, right, (0,), (0,))


def times_transposed(left, right):
    return contract(left, right, (1,), (1,))


def inner_rows(left, right):
    return lax.dot_general(
        left, right, (((0,), (0,)), ((), ())), preferred_element_type=jnp.float32
    )


def flat_bias(collected):
    return collected.reshape(-1)


def gather_forward(w_ada, b_ada, w_qkv, qv_bias, w_proj, w_fc1, fc1_bias, w_fc2, out_bias):
    part_ada, part_qkv, part_proj, part_one, part_two, bias_ada, bias_qv, bias_one, bias_out = (
        lax.all_gather(w_ada, "fsdp", axis=1, tiled=True),
        lax.all_gather(w_qkv, "fsdp", axis=1, tiled=True),
        lax.all_gather(w_proj, "fsdp", axis=1, tiled=True),
        lax.all_gather(w_fc1, "fsdp", axis=1, tiled=True),
        lax.all_gather(w_fc2, "fsdp", axis=1, tiled=True),
        lax.all_gather(b_ada.reshape(1, 1, -1), "fsdp", axis=1, tiled=True),
        lax.all_gather(qv_bias.reshape(1, 1, -1), "fsdp", axis=1, tiled=True),
        lax.all_gather(fc1_bias.reshape(1, 1, -1), "fsdp", axis=1, tiled=True),
        lax.all_gather(out_bias.reshape(1, 1, -1), "fsdp", axis=1, tiled=True),
    )
    gathered = (
        lax.all_gather(part_ada, "dp", axis=0, tiled=True),
        lax.all_gather(part_qkv, "dp", axis=0, tiled=True),
        lax.all_gather(part_proj, "dp", axis=0, tiled=True),
        lax.all_gather(part_one, "dp", axis=0, tiled=True),
        lax.all_gather(part_two, "dp", axis=0, tiled=True),
        lax.all_gather(bias_ada, "dp", axis=0, tiled=True),
        lax.all_gather(bias_qv, "dp", axis=0, tiled=True),
        lax.all_gather(bias_one, "dp", axis=0, tiled=True),
        lax.all_gather(bias_out, "dp", axis=0, tiled=True),
    )
    return (
        gathered[0],
        flat_bias(gathered[5]),
        gathered[1],
        flat_bias(gathered[6]),
        gathered[2],
        gathered[3],
        flat_bias(gathered[7]),
        gathered[4],
        flat_bias(gathered[8]),
    )


def gather_backward(w_ada, w_qkv, w_proj, w_fc1, w_fc2):
    part_ada, part_qkv, part_proj, part_one, part_two = (
        lax.all_gather(w_ada, "fsdp", axis=1, tiled=True),
        lax.all_gather(w_qkv, "fsdp", axis=1, tiled=True),
        lax.all_gather(w_proj, "fsdp", axis=1, tiled=True),
        lax.all_gather(w_fc1, "fsdp", axis=1, tiled=True),
        lax.all_gather(w_fc2, "fsdp", axis=1, tiled=True),
    )
    return (
        lax.all_gather(part_ada, "dp", axis=0, tiled=True),
        lax.all_gather(part_qkv, "dp", axis=0, tiled=True),
        lax.all_gather(part_proj, "dp", axis=0, tiled=True),
        lax.all_gather(part_one, "dp", axis=0, tiled=True),
        lax.all_gather(part_two, "dp", axis=0, tiled=True),
    )


def split_bias(term):
    return term.reshape(lax.axis_size("dp"), lax.axis_size("fsdp"), -1)


def own_bias(summed):
    return lax.dynamic_index_in_dim(summed, lax.axis_index("dp"), 0, keepdims=False).reshape(-1)


def owned_columns(matrix, width):
    return lax.dynamic_slice_in_dim(matrix, lax.axis_index("dp") * width, width, 1)


def column_totals(matrix):
    return jnp.sum(matrix.astype(jnp.float32), axis=0)


def plain_shards(
    patches_in,
    condition,
    keep_count,
    keep_index,
    w_ada,
    b_ada,
    w_qkv,
    qv_bias,
    w_proj,
    w_fc1,
    fc1_bias,
    w_fc2,
    out_bias,
    cotangent,
):
    images, kept_slots = keep_index.shape
    features = patches_in.shape[2]
    hidden_units = w_fc2.shape[0] * lax.axis_size("dp")
    all_rows = images * kept_slots
    head_size = features // HEADS
    factor = 1.0 / math.sqrt(head_size)
    head_shape = (images, kept_slots, HEADS, head_size)
    row_width = features // lax.axis_size("dp")
    unit_width = hidden_units // lax.axis_size("dp")
    ada_full, ada_bias, qkv_full, qv_full, proj_full, one_full, one_bias, two_full, out_full = (
        gather_forward(w_ada, b_ada, w_qkv, qv_bias, w_proj, w_fc1, fc1_bias, w_fc2, out_bias)
    )
    inputs = patches_in.astype(jnp.float32)
    kept_in = jnp.take_along_axis(inputs, keep_index[:, :, None], axis=1)
    allowed = (jnp.arange(kept_slots)[None, :] < keep_count[:, None])[:, None, None, :]
    cond_float = condition.astype(jnp.float32)
    signal = swish(cond_float).astype(jnp.bfloat16)
    modulation = jnp.dot(signal, ada_full, preferred_element_type=jnp.float32) + ada_bias.astype(
        jnp.float32
    )
    shift_one, scale_one, gate_one, shift_two, scale_two, gate_two = [
        modulation[:, None, column * features : (column + 1) * features] for column in range(6)
    ]
    normed_one, rstd_one = layer_norm(kept_in)
    hidden_one = (
        (normed_one * (1.0 + scale_one) + shift_one)
        .astype(jnp.bfloat16)
        .reshape(all_rows, features)
    )
    qv_float = qv_full.astype(jnp.float32)
    qkv_bias = jnp.concatenate(
        [qv_float[:features], jnp.zeros((features,), jnp.float32), qv_float[features:]]
    )
    projected = (
        jnp.dot(hidden_one, qkv_full, preferred_element_type=jnp.float32) + qkv_bias
    ).astype(jnp.bfloat16)
    queries = projected[:, :features].reshape(head_shape)
    key_rows = projected[:, features : 2 * features].reshape(head_shape)
    values = projected[:, 2 * features :].reshape(head_shape)
    scores = (
        jnp.einsum("iqhe,ikhe->ihqk", queries, key_rows, preferred_element_type=jnp.float32)
        * factor
    )
    scores = jnp.where(allowed, scores, negative)
    top_score = jnp.max(scores, axis=-1, keepdims=True)
    exponent = jnp.exp(scores - top_score)
    row_total = jnp.sum(exponent, axis=-1, keepdims=True)
    log_total = top_score + jnp.log(row_total)
    softmax_low = (exponent / row_total).astype(jnp.bfloat16)
    mixed = jnp.einsum("ihqk,ikhe->iqhe", softmax_low, values, preferred_element_type=jnp.float32)
    mixed_low = mixed.reshape(all_rows, features).astype(jnp.bfloat16)
    out_float = out_full.astype(jnp.float32)
    attended = (
        jnp.dot(mixed_low, proj_full, preferred_element_type=jnp.float32) + out_float[:features]
    ).reshape(images, kept_slots, features)
    middle = kept_in + gate_one * attended
    normed_two, rstd_two = layer_norm(middle)
    hidden_two = (
        (normed_two * (1.0 + scale_two) + shift_two)
        .astype(jnp.bfloat16)
        .reshape(all_rows, features)
    )
    raised = jnp.dot(hidden_two, one_full, preferred_element_type=jnp.float32) + one_bias.astype(
        jnp.float32
    )
    activated = gelu_tanh(raised).astype(jnp.bfloat16)
    branch = (
        jnp.dot(activated, two_full, preferred_element_type=jnp.float32) + out_float[features:]
    ).reshape(images, kept_slots, features)
    block_out = (middle + gate_two * branch).astype(jnp.bfloat16)
    ada_back, qkv_back, proj_back, one_back, two_back = gather_backward(
        w_ada, w_qkv, w_proj, w_fc1, w_fc2
    )
    upstream = cotangent.astype(jnp.float32)
    d_gate_two = jnp.sum(upstream * branch, axis=1)
    d_branch = (gate_two * upstream).reshape(all_rows, features).astype(jnp.bfloat16)
    d_activated = times_transposed(d_branch, two_back)
    unused, gelu_pull = jax.vjp(gelu_tanh, raised)
    d_raised = gelu_pull(d_activated)[0].astype(jnp.bfloat16)
    d_hidden_two = times_transposed(d_raised, one_back).reshape(images, kept_slots, features)
    d_shift_two = jnp.sum(d_hidden_two, axis=1)
    d_scale_two = jnp.sum(d_hidden_two * normed_two, axis=1)
    d_middle = upstream + norm_back(d_hidden_two * (1.0 + scale_two), normed_two, rstd_two)
    d_gate_one = jnp.sum(d_middle * attended, axis=1)
    d_attended = (gate_one * d_middle).reshape(all_rows, features).astype(jnp.bfloat16)
    d_mixed = times_transposed(d_attended, proj_back).astype(jnp.bfloat16).reshape(head_shape)
    scores_again = (
        jnp.einsum("iqhe,ikhe->ihqk", queries, key_rows, preferred_element_type=jnp.float32)
        * factor
    )
    scores_again = jnp.where(allowed, scores_again, negative)
    softmax_again = jnp.exp(scores_again - log_total)
    d_softmax = jnp.einsum("iqhe,ikhe->ihqk", d_mixed, values, preferred_element_type=jnp.float32)
    row_delta = jnp.sum(d_softmax * softmax_again, axis=-1, keepdims=True)
    d_scores = (softmax_again * (d_softmax - row_delta)).astype(jnp.bfloat16)
    d_queries = (
        jnp.einsum("ihqk,ikhe->iqhe", d_scores, key_rows, preferred_element_type=jnp.float32)
        * factor
    )
    d_keys = (
        jnp.einsum("ihqk,iqhe->ikhe", d_scores, queries, preferred_element_type=jnp.float32)
        * factor
    )
    d_values = jnp.einsum(
        "ihqk,iqhe->ikhe",
        softmax_again.astype(jnp.bfloat16),
        d_mixed,
        preferred_element_type=jnp.float32,
    )
    d_projected = jnp.concatenate(
        [
            d_queries.reshape(all_rows, features),
            d_keys.reshape(all_rows, features),
            d_values.reshape(all_rows, features),
        ],
        axis=1,
    ).astype(jnp.bfloat16)
    d_hidden_one = times_transposed(d_projected, qkv_back).reshape(images, kept_slots, features)
    d_shift_one = jnp.sum(d_hidden_one, axis=1)
    d_scale_one = jnp.sum(d_hidden_one * normed_one, axis=1)
    d_kept = d_middle + norm_back(d_hidden_one * (1.0 + scale_one), normed_one, rstd_one)
    grad_patches = jnp.zeros_like(inputs).at[jnp.arange(images)[:, None], keep_index].add(d_kept)
    d_modulation = jnp.concatenate(
        [d_shift_one, d_scale_one, d_gate_one, d_shift_two, d_scale_two, d_gate_two], axis=1
    ).astype(jnp.bfloat16)
    d_signal = times_transposed(d_modulation, ada_back)
    unused_too, swish_pull = jax.vjp(swish, cond_float)
    grad_condition = swish_pull(d_signal)[0]
    piece_one = lax.all_gather(hidden_one, "dp", axis=0, tiled=True)
    piece_proj_d = lax.all_gather(d_projected, "dp", axis=0, tiled=True)
    piece_mixed = lax.all_gather(mixed_low, "dp", axis=0, tiled=True)
    piece_att_d = lax.all_gather(d_attended, "dp", axis=0, tiled=True)
    piece_two = lax.all_gather(hidden_two, "dp", axis=0, tiled=True)
    piece_raised_d = lax.all_gather(d_raised, "dp", axis=0, tiled=True)
    piece_act = lax.all_gather(activated, "dp", axis=0, tiled=True)
    piece_branch_d = lax.all_gather(d_branch, "dp", axis=0, tiled=True)
    grad_qkv = inner_rows(owned_columns(piece_one, row_width), piece_proj_d)
    grad_proj = inner_rows(owned_columns(piece_mixed, row_width), piece_att_d)
    grad_one = inner_rows(owned_columns(piece_two, row_width), piece_raised_d)
    grad_two = inner_rows(owned_columns(piece_act, unit_width), piece_branch_d)
    qkv_sums = column_totals(piece_proj_d)
    proj_sums = column_totals(piece_att_d)
    one_sums = column_totals(piece_raised_d)
    two_sums = column_totals(piece_branch_d)
    piece_signal = lax.all_gather(signal, "dp", axis=0, tiled=True)
    piece_mod_d = lax.all_gather(d_modulation, "dp", axis=0, tiled=True)
    grad_ada = inner_rows(owned_columns(piece_signal, row_width), piece_mod_d)
    ada_sums = column_totals(piece_mod_d)
    grad_qv = jnp.concatenate([qkv_sums[:features], qkv_sums[2 * features :]])
    grad_out = jnp.concatenate([proj_sums, two_sums])
    terms = (
        grad_ada,
        grad_qkv,
        grad_proj,
        grad_one,
        grad_two,
        split_bias(ada_sums),
        split_bias(grad_qv),
        split_bias(one_sums),
        split_bias(grad_out),
    )
    (
        final_ada,
        final_qkv,
        final_proj,
        final_one,
        final_two,
        final_ada_bias,
        final_qv,
        final_bias,
        final_out,
    ) = (
        lax.psum_scatter(
            terms[0].astype(jnp.bfloat16), "fsdp", scatter_dimension=1, tiled=True
        ).astype(jnp.float32),
        lax.psum_scatter(
            terms[1].astype(jnp.bfloat16), "fsdp", scatter_dimension=1, tiled=True
        ).astype(jnp.float32),
        lax.psum_scatter(
            terms[2].astype(jnp.bfloat16), "fsdp", scatter_dimension=1, tiled=True
        ).astype(jnp.float32),
        lax.psum_scatter(
            terms[3].astype(jnp.bfloat16), "fsdp", scatter_dimension=1, tiled=True
        ).astype(jnp.float32),
        lax.psum_scatter(
            terms[4].astype(jnp.bfloat16), "fsdp", scatter_dimension=1, tiled=True
        ).astype(jnp.float32),
        lax.psum_scatter(
            terms[5].astype(jnp.bfloat16), "fsdp", scatter_dimension=1, tiled=True
        ).astype(jnp.float32),
        lax.psum_scatter(
            terms[6].astype(jnp.bfloat16), "fsdp", scatter_dimension=1, tiled=True
        ).astype(jnp.float32),
        lax.psum_scatter(
            terms[7].astype(jnp.bfloat16), "fsdp", scatter_dimension=1, tiled=True
        ).astype(jnp.float32),
        lax.psum_scatter(
            terms[8].astype(jnp.bfloat16), "fsdp", scatter_dimension=1, tiled=True
        ).astype(jnp.float32),
    )
    return (
        block_out,
        grad_patches,
        grad_condition,
        final_ada,
        own_bias(final_ada_bias),
        final_qkv,
        own_bias(final_qv),
        final_proj,
        final_one,
        own_bias(final_bias),
        final_two,
        own_bias(final_out),
    )


MESH = pl.DeviceIdType.MESH


def remote(source, target, send, recv, device):
    return pltpu.make_async_remote_copy(
        src_ref=source,
        dst_ref=target,
        send_sem=send,
        recv_sem=recv,
        device_id=device,
        device_id_type=MESH,
    )


def greet(devices):
    barrier = pltpu.get_barrier_semaphore()
    for device in devices:
        pl.semaphore_signal(barrier, 1, device_id=device, device_id_type=MESH)
    pl.semaphore_wait(barrier, len(devices))


def normed(value):
    centred = value - jnp.mean(value, axis=-1, keepdims=True)
    rstd = lax.rsqrt(jnp.mean(centred * centred, axis=-1, keepdims=True) + epsilon)
    return centred * rstd, rstd


def forward_body(
    sizes,
    note_ref,
    ada_ref,
    piece_ref,
    qkv_ref,
    proj_ref,
    kept_ref,
    cot_ref,
    count_ref,
    qkv_hbm,
    one_hbm,
    two_hbm,
    projected_hbm,
    hidden_hbm,
    branch_hbm,
    proj_hbm,
    attended_ref,
    hidden_rows,
    mixed_rows,
    mod_ref,
    bias_ref,
    signal_ref,
    qkv_all,
    one_all,
    two_all,
    projected_ref,
    hidden_all,
    branch_all,
    proj_dense,
    proj_all,
    mixed_ref,
    piece_got,
    one_block,
    two_block,
    note_got,
    row_put,
    row_got,
    send_n,
    recv_n,
    send_z,
    send_y,
    send_x,
    recv_w,
    send_e,
    recv_e,
    local,
    out_sem,
):
    heads, size, widths = sizes
    n_dp, n_fs = 4, 8
    d_at, f_at = lax.axis_index("dp"), lax.axis_index("fsdp")
    own_at = d_at * n_fs + f_at
    slots, features = kept_ref.shape
    half_rows, cols = qkv_ref.shape[0], qkv_ref.shape[1] // 2
    unit = one_block.shape[0]
    row_width = 2 * half_rows
    width = proj_ref.shape[1] // 2
    low = jnp.bfloat16
    full = jnp.float32
    others = [(a, b) for a in range(n_dp) for b in range(n_fs) if a or b]
    greet([(d_at ^ a, f_at ^ b) for a, b in others])

    own_blocks = (qkv_ref, proj_ref, one_block, two_block)
    gathered = (qkv_all, proj_all, one_all, two_all)
    started = []
    middle_copies = []
    stores = []
    z_at = f_at // 2
    in_middle = (z_at == 1) | (z_at == 2)
    second = jnp.where(in_middle, 6, 4)
    third = 10 - second

    def store(source, target):
        copy = pltpu.make_async_copy(source, target, out_sem.at[len(stores)])
        copy.start()
        stores.append(copy)

    def slot(array, a, b):
        if array < 2:
            start = pl.multiple_of((d_at ^ a) * half_rows, 16)
            return gathered[array].at[f_at ^ b, pl.ds(start, half_rows), :]
        start = pl.multiple_of((f_at ^ b) * unit, 16)
        return gathered[array].at[pl.ds(start, unit), :]

    def push(source, target, send, recv, device):
        copy = remote(source, target, send, recv, device)
        copy.start()
        started.append(copy)

    def block(array, a, b):
        own = isinstance(b, int) and a == 0 and b == 0
        return own_blocks[array] if own else slot(array, a, b)

    def pass_on(array, a, b, axis, mask, sem):
        device = (d_at ^ mask, f_at) if axis == 0 else (d_at, f_at ^ mask)
        to_a, to_b = (a ^ mask, b) if axis == 0 else (a, b ^ mask)
        push(block(array, a, b), slot(array, a, b), sem, recv_w.at[array, to_a, to_b], device)

    def relay_middle(array, b, mask, place):
        copy = remote(
            block(array, 0, b),
            slot(array, 0, b),
            send_z.at[array, place],
            recv_w.at[array, 0, b ^ mask],
            (d_at, f_at ^ mask),
        )

        @pl.when(in_middle)
        def _():
            copy.start()

        middle_copies.append(copy)

    def arrive(array, a, b):
        place = slot(array, a, b)
        pltpu.make_async_copy(place, place, recv_w.at[array, a, b]).wait()

    def near(array, b, place):
        pass_on(array, 0, b, 1, 1, send_y.at[array, place])

    def onward(array, a, b, place):
        if a == 0:
            pass_on(array, a, b, 0, 2, send_x.at[array, 0, place])
        pass_on(array, a, b, 0, 1, send_x.at[array, 1 + a // 2, place])

    order = [0, 1, 2, second, 3, third, second ^ 1, third ^ 1]

    def begin(array):
        near(array, 0, 0)
        if array < 2:
            onward(array, 0, 0, 0)
        pass_on(array, 0, 0, 1, 2, send_z.at[array, 0])
        relay_middle(array, 0, 6, 1)

    def follow(array, step):
        arrive(array, 0, order[step])
        if step == 2:
            relay_middle(array, 2, 6, 2)
            near(array, 2, 1)
        if step == 3:
            relay_middle(array, 6, 2, 3)
            near(array, second, 2)
        if step == 5:
            relay_middle(array, 4, 2, 4)
            near(array, third, 3)
        if array < 2:
            onward(array, 0, order[step], step)

    begin(0)
    begin(1)
    for place, (a, b) in enumerate(others):
        push(
            note_ref.at[d_at ^ a],
            note_got.at[own_at],
            send_n.at[0, place],
            recv_n.at[0, place],
            (d_at ^ a, f_at ^ b),
        )
    stays = [
        pltpu.make_async_copy(note_ref.at[d_at], note_got.at[own_at], local.at[0]),
        pltpu.make_async_copy(qkv_ref, slot(0, 0, 0), local.at[1]),
        pltpu.make_async_copy(proj_ref, slot(1, 0, 0), local.at[2]),
        pltpu.make_async_copy(piece_ref.at[d_at], piece_got.at[d_at], local.at[3]),
    ]
    for stay in stays:
        stay.start()
    kept = kept_ref[...]
    normed_one, _ = normed(kept)
    follow(0, 1)
    follow(0, 2)
    for mask in (1, 2, 3):
        push(
            piece_ref.at[d_at ^ mask],
            piece_got.at[d_at],
            send_e.at[2, mask],
            recv_e.at[2, mask],
            (d_at ^ mask, f_at),
        )

    stays[0].wait()
    for place, (a, b) in enumerate(others):
        at = (d_at ^ a) * n_fs + (f_at ^ b)
        pltpu.make_async_copy(note_got.at[at], note_got.at[at], recv_n.at[0, place]).wait()
    notes = note_got[...]
    signals = jnp.concatenate([notes[:, row, :] for row in range(3)], axis=1).astype(low)
    signal_ref[...] = signals
    terms = jnp.dot(signals, ada_ref[...], preferred_element_type=full)
    ada_width = widths[0]
    ada_piece = ada_width * n_fs // (n_dp * n_fs)

    def bias_piece(index, start, count):
        row = note_got[index]
        line = jnp.concatenate([row[3 + step : 4 + step, :] for step in range(5)], axis=1)
        return line[:, start : start + count]

    block_bias = jnp.concatenate(
        [bias_piece(f_at * n_dp + step, 0, ada_piece) for step in range(n_dp)], axis=1
    )
    first = (d_at == 0).astype(full)
    for row in range(7):
        piece = terms[:, row * 128 : (row + 1) * 128]
        count = min(128, ada_width - row * 128)
        add = block_bias[:, row * 128 : row * 128 + count] * first
        if count < 128:
            add = jnp.concatenate([add, jnp.zeros((1, 128 - count), full)], axis=1)
        row_put[:, row, :] = piece + add
    for place, (a, b) in enumerate(others):
        push(
            row_put.at[(d_at ^ a) * n_fs + (f_at ^ b)],
            row_got.at[own_at],
            send_n.at[1, place],
            recv_n.at[1, place],
            (d_at ^ a, f_at ^ b),
        )
    keep_row = pltpu.make_async_copy(row_put.at[own_at], row_got.at[own_at], local.at[0])
    keep_row.start()

    follow(0, 3)
    follow(1, 1)
    follow(1, 2)
    follow(0, 4)
    follow(0, 5)

    stays[3].wait()
    for mask in (1, 2, 3):
        place = piece_got.at[d_at ^ mask]
        pltpu.make_async_copy(place, place, recv_e.at[2, mask]).wait()
    one_block[...] = jnp.concatenate([piece_got[d, :, :row_width] for d in range(n_dp)], axis=1)
    two_block[...] = jnp.concatenate([piece_got[d, :, row_width:] for d in range(n_dp)], axis=1)
    follow(0, 6)
    follow(0, 7)
    follow(1, 3)
    begin(2)
    follow(1, 4)
    follow(1, 5)
    begin(3)
    follow(1, 6)
    follow(1, 7)
    keep_one = pltpu.make_async_copy(one_block, slot(2, 0, 0), local.at[3])
    keep_one.start()
    keep_two = pltpu.make_async_copy(two_block, slot(3, 0, 0), local.at[4])
    keep_two.start()

    qv_width, one_width, out_width = widths[1:]
    starts = [ada_piece, ada_piece + qv_width, ada_piece + qv_width + one_width]
    lines = []
    for index in range(n_dp * n_fs):
        lines.append(
            (
                bias_piece(index, starts[0], qv_width),
                bias_piece(index, starts[2], out_width),
            )
        )
    heads_per = cols // size
    for f in range(n_fs):
        parts = []
        for j in range(heads_per):
            head = f * heads_per + j
            if head < heads:
                parts.append(lines[head][0])
            elif head < 2 * heads:
                parts.append(jnp.zeros((1, size), full))
            else:
                parts.append(lines[head - heads][0])
        bias_ref[f : f + 1, :cols] = jnp.concatenate(parts, axis=1)
    bias_ref[8:9, :] = jnp.concatenate([line[1] for line in lines[:heads]], axis=1)
    bias_ref[9:10, :] = jnp.concatenate([line[1] for line in lines[heads:]], axis=1)
    bias_ref[10:11, :] = jnp.concatenate(
        [bias_piece(f * n_dp + d_at, starts[1], one_width) for f in range(n_fs)], axis=1
    )

    keep_row.wait()
    for place, (a, b) in enumerate(others):
        at = (d_at ^ a) * n_fs + (f_at ^ b)
        pltpu.make_async_copy(row_got.at[at], row_got.at[at], recv_n.at[1, place]).wait()
    sums = row_got[0:n_fs]
    for d in range(1, n_dp):
        sums = sums + row_got[d * n_fs : (d + 1) * n_fs]
    sums = jnp.concatenate([sums[:, row, :] for row in range(7)], axis=1)
    pieces = []
    for index in range(6 * n_dp):
        f, part = index // 3, index % 3
        pieces.append(sums[f : f + 1, part * row_width : (part + 1) * row_width])
    mods = []
    for row in range(6):
        mods.append(jnp.concatenate(pieces[row * n_dp : (row + 1) * n_dp], axis=1))
        mod_ref[row : row + 1, :] = mods[row]
    hidden_one = (normed_one * (1.0 + mods[1]) + mods[0]).astype(low)
    branch_all[0] = (mods[5] * cot_ref[...].astype(full)).astype(low)
    chunks = [
        hidden_one[:, place * half_rows : (place + 1) * half_rows] for place in range(2 * n_dp)
    ]
    for d in range(n_dp):
        hidden_rows[d] = jnp.concatenate(chunks[2 * d : 2 * d + 2], axis=1)
    halves = [jnp.concatenate(chunks[part::2], axis=1) for part in range(2)]

    def spread_step(buffer, kind, mask):
        for key in [0] if mask == 2 else [0, 2]:
            push(
                buffer.at[key],
                buffer.at[key ^ mask],
                send_e.at[kind, key ^ mask],
                recv_e.at[kind, key ^ mask],
                (d_at ^ mask, f_at),
            )

    def spread_wait(buffer, kind, keys):
        for key in keys:
            place = buffer.at[key]
            pltpu.make_async_copy(place, place, recv_e.at[kind, key]).wait()

    store(branch_all.at[0], branch_hbm.at[0])
    spread_step(branch_all, 0, 2)

    stays[1].wait()
    for step, b in enumerate(order):
        arrive(0, 2, b)
        onward(0, 2, b, step)
        arrive(0, 1, b)
        arrive(0, 3, b)
        f = f_at ^ b
        out = jnp.dot(halves[0], qkv_all[f, :, :cols], preferred_element_type=full)
        out = out + jnp.dot(halves[1], qkv_all[f, :, cols:], preferred_element_type=full)
        projected_ref[f] = (out + bias_ref[pl.ds(f, 1), :cols]).astype(low)
        store(qkv_all.at[f], qkv_hbm.at[f])
        if step in (2, 3, 4, 6):
            follow(2, {2: 1, 3: 2, 4: 3, 6: 5}[step])
        if step in (3, 5):
            follow(3, {3: 1, 5: 2}[step])

    allowed = lax.broadcasted_iota(jnp.int32, (slots, slots), 1) < count_ref[0]
    factor = 1.0 / math.sqrt(size)
    for h in range(heads):
        q, k, v = [
            projected_ref[f, :, j * size : (j + 1) * size]
            for f, j in (
                ((kind * heads + h) // heads_per, (kind * heads + h) % heads_per)
                for kind in range(3)
            )
        ]
        scores = contract(q, k, (1,), (1,)) * factor
        scores = jnp.where(allowed, scores, negative)
        exponent = jnp.exp(scores - jnp.max(scores, axis=-1, keepdims=True))
        softmax = exponent / jnp.sum(exponent, axis=-1, keepdims=True)
        mix = jnp.dot(softmax.astype(low), v, preferred_element_type=full).astype(low)
        pair, side = h // 2, h % 2
        start = ((pair % 2) * n_dp + pair // 2) * half_rows + side * size
        mixed_ref[:, start : start + size] = mix
        start = (pair % 2) * half_rows + side * size
        mixed_rows[pair // 2, :, start : start + size] = mix
        if h == 8:
            follow(3, 3)

    store(projected_ref, projected_hbm)
    for step, b in enumerate(order):
        arrive(1, 2, b)
        onward(1, 2, b, step)
    stays[2].wait()
    for b in order:
        arrive(1, 1, b)
        arrive(1, 3, b)
    for f in range(n_fs):
        for part in range(2):
            proj_dense[
                part * n_dp * half_rows : (part + 1) * n_dp * half_rows,
                f * width : (f + 1) * width,
            ] = proj_all[f, :, part * width : (part + 1) * width]
    attended = (
        jnp.dot(mixed_ref[...], proj_dense[...], preferred_element_type=full) + bias_ref[8:9, :]
    )
    attended_ref[...] = attended
    middle = kept + mods[2] * attended
    normed_two, _ = normed(middle)
    hidden_all[0] = (normed_two * (1.0 + mods[4]) + mods[3]).astype(low)
    spread_step(hidden_all, 1, 2)
    store(hidden_all.at[0], hidden_hbm.at[0])
    store(proj_dense, proj_hbm)
    follow(3, 5)
    spread_wait(branch_all, 0, [2])
    spread_step(branch_all, 0, 1)
    spread_wait(hidden_all, 1, [2])
    spread_step(hidden_all, 1, 1)
    for step in (4, 6, 7):
        arrive(2, 0, order[step])
    keep_one.wait()
    store(one_all, one_hbm)
    spread_wait(branch_all, 0, [1, 3])
    spread_wait(hidden_all, 1, [1, 3])
    for key in (1, 2, 3):
        store(hidden_all.at[key], hidden_hbm.at[key])
        store(branch_all.at[key], branch_hbm.at[key])
    for step in (4, 6, 7):
        arrive(3, 0, order[step])
    keep_two.wait()
    store(two_all, two_hbm)
    for copy in started:
        copy.wait_send()

    @pl.when(in_middle)
    def _():
        for copy in middle_copies:
            copy.wait_send()

    for copy in stores:
        copy.wait()


def forward_kernel(notes, ada, pieces, qkv, proj, kept, cot, count, widths):
    n_dp, n_fs = lax.axis_size("dp"), lax.axis_size("fsdp")
    slots, features = kept.shape
    unit = pieces.shape[1]
    size = features // HEADS
    half_rows = qkv.shape[0]
    cols = qkv.shape[1] // 2
    n_all = n_dp * n_fs
    low, full = jnp.bfloat16, jnp.float32
    vmem = pl.BlockSpec(memory_space=pltpu.VMEM)
    image = (slots, features)
    shapes = [
        ((n_fs, n_dp * half_rows, 2 * cols), low),
        ((n_fs * unit, features), low),
        ((features, n_fs * unit), low),
        ((n_fs, slots, cols), low),
        ((n_dp,) + image, low),
        ((n_dp,) + image, low),
        ((features, features), low),
        (image, full),
        ((n_dp, slots, 2 * half_rows), low),
        ((n_dp, slots, 2 * half_rows), low),
        ((8, features), full),
        ((16, features), full),
        ((n_all, 384), low),
    ]
    scratch = shapes[:7] + [
        ((n_fs, n_dp * half_rows, proj.shape[1]), low),
        (image, low),
        (pieces.shape, low),
        ((unit, features), low),
        ((unit, features), low),
        ((n_all, 8, 128), full),
        ((n_all, 8, 128), full),
        ((n_all, 8, 128), full),
    ]
    dma = pltpu.SemaphoreType.DMA
    return pl.pallas_call(
        functools.partial(forward_body, (HEADS, size, widths)),
        out_shape=[jax.ShapeDtypeStruct(shape, kind) for shape, kind in shapes],
        in_specs=[vmem] * 7 + [pl.BlockSpec(memory_space=pltpu.SMEM)],
        out_specs=[pl.BlockSpec(memory_space=pl.ANY)] * 7 + [vmem] * 6,
        scratch_shapes=[pltpu.VMEM(shape, kind) for shape, kind in scratch]
        + [dma((2, n_all - 1)), dma((2, n_all - 1)), dma((4, 5)), dma((4, 4))]
        + [dma((2, 3, n_fs)), dma((4, n_dp, n_fs)), dma((3, 4)), dma((3, 4)), dma((5,))]
        + [dma((24,))],
        compiler_params=pltpu.CompilerParams(
            collective_id=5, has_side_effects=True, vmem_limit_bytes=64 * 1024 * 1024 - 65536
        ),
        name="forward",
    )(notes, ada, pieces, qkv, proj, kept, cot, count)


def gelu_parts(raised):
    square = raised * raised
    inner = 0.7978845608028654 * raised * (1.0 + 0.044715 * square)
    bend = jnp.tanh(inner)
    slope = 0.7978845608028654 * (1.0 + 3.0 * 0.044715 * square)
    half = 0.5 * (1.0 + bend)
    return raised * half, half + 0.5 * raised * (1.0 - bend * bend) * slope


def column_sums(value):
    return jnp.sum(value, axis=0, keepdims=True)


def store_tile(ref, index, line):
    for row in range(8):
        piece = line[:, row * 128 : (row + 1) * 128]
        if piece.shape[1] == 0:
            break
        if piece.shape[1] < 128:
            rest = jnp.zeros((1, 128 - piece.shape[1]), line.dtype)
            piece = jnp.concatenate([piece, rest], axis=1)
        ref[index, row : row + 1, :] = piece


def backward_body(
    sizes,
    qkv_hbm,
    one_hbm,
    two_hbm,
    projected_hbm,
    hidden_hbm,
    branch_hbm,
    proj_hbm,
    ada_ref,
    signal_ref,
    attended_ref,
    hidden_rows,
    mixed_rows,
    kept_ref,
    mod_ref,
    bias_ref,
    cot_ref,
    count_ref,
    block_ref,
    d_kept_ref,
    mlp_out,
    att_out,
    ada_out,
    last_got,
    one_ref,
    two_ref,
    projected_ref,
    hidden_all,
    branch_all,
    proj_ref,
    act_ref,
    d_raised_ref,
    part_ref,
    core_got,
    cross_put,
    cross_got,
    grads,
    got_y,
    got_z,
    rows_got,
    d_att_all,
    d_mixed_ref,
    d_proj_all,
    weight_ring,
    mlp_put,
    d_mod_ref,
    sum_put,
    sum_got,
    note_put,
    note_got,
    last_put,
    send_m,
    recv_m,
    send_d,
    recv_d,
    send_e,
    recv_e,
    send_p,
    recv_p,
    send_n,
    recv_n,
    send_s,
    recv_s,
    send_b,
    recv_b,
    local,
    load_sem,
):
    heads, size, ada_width = sizes
    n_dp, n_fs = 4, 8
    d_at, f_at = lax.axis_index("dp"), lax.axis_index("fsdp")
    own_at = d_at * n_fs + f_at
    slots, features = kept_ref.shape
    cols = projected_ref.shape[2]
    heads_per = cols // size
    row_width = features // n_dp
    half_rows = row_width // 2
    unit = features // n_fs
    low = jnp.bfloat16
    full = jnp.float32
    core, cross, near = (d_at ^ 1, f_at), (d_at ^ 2, f_at), (d_at, f_at ^ 1)
    loads = [
        pltpu.make_async_copy(source, target, load_sem.at[place])
        for place, (source, target) in enumerate(
            [
                (hidden_hbm, hidden_all),
                (one_hbm, one_ref),
                (branch_hbm, branch_all),
                (two_hbm, two_ref),
                (proj_hbm, proj_ref),
                (projected_hbm, projected_ref),
            ]
        )
    ]
    for load in loads:
        load.start()
    others = [(a, b) for a in range(n_dp) for b in range(n_fs) if a or b]
    greet([(d_at ^ a, f_at ^ b) for a, b in others])
    sent = []

    def push(source, target, send, recv, device):
        copy = remote(source, target, send, recv, device)
        copy.start()
        sent.append(copy)
        return copy

    def arrive(place, recv):
        pltpu.make_async_copy(place, place, recv).wait()

    stays = []
    for kind, source in enumerate((hidden_rows, mixed_rows)):
        for mask in (2, 3, 1):
            push(
                source.at[d_at ^ mask],
                rows_got.at[kind, mask],
                send_p.at[kind, mask],
                recv_p.at[kind, mask],
                (d_at ^ mask, f_at),
            )
        stays.append(
            pltpu.make_async_copy(source.at[d_at], rows_got.at[kind, 0], local.at[kind])
        )
        stays[kind].start()

    def image_step(image, carry):
        raised = contract(hidden_all[image], one_ref[...], (1,), (1,)) + bias_ref[10:11, :]
        active, slope = gelu_parts(raised)
        act_ref[image] = active.astype(low)
        d_active = jnp.dot(branch_all[image], two_ref[...], preferred_element_type=full)
        d_raised_ref[image] = (d_active * slope).astype(low)
        return carry

    for load in loads[:4]:
        load.wait()
    lax.fori_loop(0, n_dp, image_step, 0)

    def flat(ref, start, count):
        return ref[:, :, pl.ds(start, count)].reshape(n_dp * slots, count)

    def weight_grad(kind, left, right):
        step = features // 3
        for part in range(3):
            grads[kind, part * step : (part + 1) * step, :] = rows_rows(
                flat(left, part * step, step), flat(right, 0, features)
            ).astype(low)

    def block_rows(index):
        return pl.ds(pl.multiple_of(index * unit, 16), unit)

    def send_block(kind, place, index):
        push(
            grads.at[kind, block_rows(index), :],
            got_y.at[kind, place],
            send_m.at[kind, place],
            recv_m.at[kind, place],
            near,
        )

    def fold_block(kind, place, index):
        arrive(got_y.at[kind, place], recv_m.at[kind, place])
        rows = block_rows(index)
        grads[kind, rows, :] = (
            grads[kind, rows, :].astype(full) + got_y[kind, place].astype(full)
        ).astype(low)

    def send_wide(kind, index, mask):
        place = mask // 2 - 1
        return remote(
            grads.at[kind, block_rows(index), :],
            got_z.at[kind, place],
            send_m.at[kind, 4 + place],
            recv_m.at[kind, 4 + place],
            (d_at, index),
        )

    waves = (2, 4, 6, 0)

    def fold_wave(kind, place):
        fold_block(kind, place, f_at ^ waves[place])
        if waves[place]:
            copy = send_wide(kind, f_at ^ waves[place], waves[place])
            copy.start()
            sent.append(copy)

    def finish(kind):
        total = grads[kind, block_rows(f_at), :].astype(full)
        for place in range(3):
            arrive(got_z.at[kind, place], recv_m.at[kind, 4 + place])
            total = total + got_z[kind, place].astype(full)
        return total

    weight_grad(1, branch_all, act_ref)
    for place, wide in enumerate((2, 4, 6, 0)):
        send_block(1, place, f_at ^ wide ^ 1)

    def part_step(left, right, dims):
        def step(image, carry):
            part_ref[image] = contract(left[image], right[...], (1,), dims).astype(low)
            return carry

        lax.fori_loop(0, n_dp, step, 0)

    def core_send(kind):
        return [
            push(
                part_ref.at[image],
                core_got.at[kind, place],
                send_d.at[kind, place],
                recv_d.at[kind, place],
                core,
            )
            for place, image in enumerate((3, 1))
        ]

    def cross_send(kind):
        arrive(core_got.at[kind, 0], recv_d.at[kind, 0])
        cross_put[kind] = (
            part_ref[2].astype(full) + core_got[kind, 0].astype(full)
        ).astype(low)
        push(
            cross_put.at[kind], cross_got.at[kind], send_d.at[kind, 2], recv_d.at[kind, 2], cross
        )
        arrive(core_got.at[kind, 1], recv_d.at[kind, 1])

    part_step(d_raised_ref, one_ref, (0,))
    leaving = core_send(0)
    cross_send(0)
    own_part = part_ref[0].astype(full) + core_got[0, 1].astype(full)
    weight_grad(0, d_raised_ref, hidden_all)
    for place, wide in enumerate((2, 4, 6, 0)):
        send_block(0, place, f_at ^ wide ^ 1)
    fold_wave(1, 0)
    one_sum = jnp.zeros((1, features), full)
    for image in range(n_dp):
        one_sum = one_sum + column_sums(d_raised_ref[image].astype(full))
    branch_sum = column_sums(branch_all[0].astype(full))

    mods = [mod_ref[row : row + 1, :] for row in range(6)]
    kept = kept_ref[...]
    attended = attended_ref[...]
    middle = kept + mods[2] * attended
    normed_two, rstd_two = normed(middle)
    upstream = cot_ref[...].astype(full)
    fold_wave(1, 1)
    loads[4].wait()
    arrive(cross_got.at[0], recv_d.at[0, 2])
    d_hidden_two = own_part + cross_got[0].astype(full)
    d_mod_ref[3:4, :] = column_sums(d_hidden_two)
    d_mod_ref[4:5, :] = column_sums(d_hidden_two * normed_two)
    d_middle = upstream + norm_back(d_hidden_two * (1.0 + mods[4]), normed_two, rstd_two)
    d_mod_ref[2:3, :] = column_sums(d_middle * attended)
    d_attended = (mods[2] * d_middle).astype(low)
    d_att_all[0] = d_attended
    d_kept_ref[...] = d_middle
    att_sum = column_sums(d_attended.astype(full))
    d_mixed_ref[...] = contract(d_attended, proj_ref[...], (1,), (1,)).astype(low)
    push(d_att_all.at[0], d_att_all.at[2], send_e.at[2], recv_e.at[2], cross)
    push(d_att_all.at[0], d_att_all.at[1], send_e.at[1], recv_e.at[1], core)

    fold_wave(1, 2)
    loads[5].wait()

    n_pairs = n_fs // 2

    def pass_pair(place):
        push(
            d_proj_all.at[0, place],
            d_proj_all.at[2, place],
            send_p.at[2 + place, 2],
            recv_p.at[2 + place, 2],
            cross,
        )
        push(
            d_proj_all.at[0, place],
            d_proj_all.at[1, place],
            send_p.at[2 + place, 1],
            recv_p.at[2 + place, 1],
            core,
        )

    def relay_pair(place):
        arrive(d_proj_all.at[2, place], recv_p.at[2 + place, 2])
        push(
            d_proj_all.at[2, place],
            d_proj_all.at[3, place],
            send_p.at[2 + place, 3],
            recv_p.at[2 + place, 3],
            core,
        )

    allowed = lax.broadcasted_iota(jnp.int32, (slots, slots), 1) < count_ref[0]
    factor = 1.0 / math.sqrt(size)
    for h in range(heads):
        places = [
            ((kind * heads + h) // heads_per, (kind * heads + h) % heads_per)
            for kind in range(3)
        ]
        q, k, v = [projected_ref[f, :, j * size : (j + 1) * size] for f, j in places]
        pair, side = h // 2, h % 2
        start = ((pair % 2) * n_dp + pair // 2) * half_rows + side * size
        d_mix = d_mixed_ref[:, start : start + size]
        scores = contract(q, k, (1,), (1,)) * factor
        scores = jnp.where(allowed, scores, negative)
        exponent = jnp.exp(scores - jnp.max(scores, axis=-1, keepdims=True))
        softmax = exponent / jnp.sum(exponent, axis=-1, keepdims=True)
        d_softmax = contract(d_mix, v, (1,), (1,))
        delta = jnp.sum(d_softmax * softmax, axis=-1, keepdims=True)
        d_scores = (softmax * (d_softmax - delta)).astype(low)
        results = [
            jnp.dot(d_scores, k, preferred_element_type=full) * factor,
            rows_rows(d_scores, q) * factor,
            rows_rows(softmax.astype(low), d_mix),
        ]
        for (f, j), result in zip(places, results):
            start = (f % 2) * cols + j * size
            d_proj_all[0, f // 2, :, start : start + size] = result.astype(low)
        if h == 11:
            pass_pair(0)
        if h == 8:
            arrive(d_att_all.at[2], recv_e.at[2])
            push(d_att_all.at[2], d_att_all.at[3], send_e.at[3], recv_e.at[3], core)
    for place in range(1, n_pairs):
        pass_pair(place)
    fold_wave(1, 3)

    for copy in leaving:
        copy.wait_send()
    part_step(act_ref, two_ref, (1,))
    core_send(1)
    cross_send(1)
    fold_wave(0, 0)

    for stay in stays:
        stay.wait()
    for kind in range(2):
        for mask in (2, 3, 1):
            arrive(rows_got.at[kind, mask], recv_p.at[kind, mask])
    for mask in (1, 3):
        arrive(d_att_all.at[mask], recv_e.at[mask])
    grad_proj = rows_rows(
        rows_got[1].reshape(n_dp * slots, row_width),
        d_att_all[...].reshape(n_dp * slots, features),
    ).astype(low)
    for f in range(n_fs):
        for part in range(2):
            grads[
                2,
                f * unit : (f + 1) * unit,
                2 * cols + part * unit : 2 * cols + (part + 1) * unit,
            ] = grad_proj[part * half_rows : (part + 1) * half_rows, f * unit : (f + 1) * unit]

    odd = f_at % 2

    def grad_pair(place):
        for mask in (1, 3):
            arrive(d_proj_all.at[mask, place], recv_p.at[2 + place, mask])
        result = rows_rows(
            rows_got[0].reshape(n_dp * slots, row_width),
            d_proj_all[:, place].reshape(n_dp * slots, 2 * cols),
        ).astype(low)
        for side in range(2):
            start = (2 * place + side) * unit
            for part in range(2):
                grads[2, start : start + unit, part * cols : (part + 1) * cols] = result[
                    part * half_rows : (part + 1) * half_rows, side * cols : (side + 1) * cols
                ]
        send_block(2, place, 2 * place + 1 - odd)

    def fold_pair(place):
        index = 2 * place + odd
        fold_block(2, place, index)

        @pl.when(index != f_at)
        def _():
            send_wide(2, index, index ^ f_at).start()

    weights = [
        pltpu.make_async_copy(qkv_hbm.at[f], weight_ring.at[f % 2], local.at[2 + f % 2])
        for f in range(n_fs)
    ]
    weights[0].start()
    halves = [jnp.zeros((slots, features // 2), full) for part in range(2)]
    for f in range(n_fs):
        if f + 1 < n_fs:
            weights[f + 1].start()
        weights[f].wait()
        own = d_proj_all[0, f // 2, :, (f % 2) * cols : (f % 2 + 1) * cols]
        for part in range(2):
            halves[part] = halves[part] + contract(
                own, weight_ring[f % 2, :, part * cols : (part + 1) * cols], (1,), (1,)
            )
        line = jnp.concatenate(
            [
                column_sums(own.astype(full)),
                att_sum[:, f * unit : (f + 1) * unit],
                branch_sum[:, f * unit : (f + 1) * unit],
                one_sum[:, f * unit : (f + 1) * unit],
            ],
            axis=1,
        )
        store_tile(sum_put, f, line)
        if f == 3:
            relay_pair(0)
            fold_wave(0, 1)
            grad_pair(0)
    relay_pair(1)
    fold_wave(0, 2)
    grad_pair(1)
    d_hidden_one = jnp.concatenate(
        [
            halves[part][:, d * half_rows : (d + 1) * half_rows]
            for d in range(n_dp)
            for part in range(2)
        ],
        axis=1,
    )
    normed_one, rstd_one = normed(kept)
    d_mod_ref[0:1, :] = column_sums(d_hidden_one)
    d_mod_ref[1:2, :] = column_sums(d_hidden_one * normed_one)

    relay_pair(2)
    fold_wave(0, 3)
    grad_pair(2)
    fold_pair(0)
    relay_pair(3)
    grad_pair(3)
    fold_pair(1)

    arrive(cross_got.at[1], recv_d.at[1, 2])
    branch = (
        part_ref[0].astype(full)
        + core_got[1, 1].astype(full)
        + cross_got[1].astype(full)
        + bias_ref[9:10, :]
    )
    d_mod_ref[5:6, :] = column_sums(upstream * branch)

    third = ada_width // 3
    pieces = []
    for row in range(6):
        line = d_mod_ref[row : row + 1, :].astype(low).astype(full)
        pieces += [line[:, step * third : (step + 1) * third] for step in range(n_dp)]
    for f in range(n_fs):
        store_tile(note_put, f, jnp.concatenate(pieces[3 * f : 3 * f + 3], axis=1))
    for mask in range(1, n_fs):
        push(
            sum_put.at[f_at ^ mask],
            sum_got.at[mask],
            send_s.at[mask],
            recv_s.at[mask],
            (d_at, f_at ^ mask),
        )
    for place, (a, b) in enumerate(others):
        push(
            note_put.at[f_at ^ b],
            note_got.at[own_at],
            send_n.at[0, place],
            recv_n.at[0, place],
            (d_at ^ a, f_at ^ b),
        )
    keep_note = pltpu.make_async_copy(note_put.at[f_at], note_got.at[own_at], local.at[0])
    keep_note.start()
    keep_sum = pltpu.make_async_copy(sum_put.at[f_at], sum_got.at[0], local.at[1])
    keep_sum.start()
    fold_pair(2)
    d_kept_ref[...] = d_kept_ref[...] + norm_back(
        d_hidden_one * (1.0 + mods[1]), normed_one, rstd_one
    )
    block_ref[...] = (middle + mods[5] * branch).astype(low)

    keep_mlp = []
    for kind in (1, 0):
        total = finish(kind).astype(low)
        for d in range(n_dp):
            mlp_put[kind, d] = total[:, d * row_width : (d + 1) * row_width]
        for mask in (2, 3, 1):
            push(
                mlp_put.at[kind, d_at ^ mask],
                mlp_out.at[kind, d_at],
                send_b.at[kind, mask],
                recv_b.at[kind, mask],
                (d_at ^ mask, f_at),
            )
        keep_mlp.append(
            pltpu.make_async_copy(
                mlp_put.at[kind, d_at], mlp_out.at[kind, d_at], local.at[2 + kind]
            )
        )
        keep_mlp[-1].start()

    fold_pair(3)

    keep_note.wait()
    keep_sum.wait()
    for mask in range(1, n_fs):
        arrive(sum_got.at[mask], recv_s.at[mask])
    for place, (a, b) in enumerate(others):
        at = (d_at ^ a) * n_fs + (f_at ^ b)
        arrive(note_got.at[at], recv_n.at[0, place])
    sums = sum_got[0]
    for mask in range(1, n_fs):
        sums = sums + sum_got[mask]
    notes = note_got[...]
    all_d = jnp.concatenate([notes[:, row, :] for row in range(7)], axis=1)
    totals = column_sums(all_d)
    all_d = all_d.astype(low)
    terms = contract(all_d, ada_ref[...], (1,), (1,))
    for row in range(3):
        last_put[:, row, :] = terms[:, row * 128 : (row + 1) * 128]
    everyone = (n_dp * n_fs, 128)
    for row in range(7):
        last_put[:, 8 + row, :] = jnp.broadcast_to(sums[row : row + 1, :], everyone)
        last_put[:, 16 + row, :] = jnp.broadcast_to(
            totals[:, row * 128 : (row + 1) * 128], everyone
        )
    for place, (a, b) in enumerate(others):
        push(
            last_put.at[(d_at ^ a) * n_fs + (f_at ^ b)],
            last_got.at[own_at],
            send_n.at[1, place],
            recv_n.at[1, place],
            (d_at ^ a, f_at ^ b),
        )
    keep_last = pltpu.make_async_copy(last_put.at[own_at], last_got.at[own_at], local.at[0])
    keep_last.start()
    ada_out[...] = rows_rows(signal_ref[...], all_d)[: ada_out.shape[0], : ada_out.shape[1]]
    att_out[...] = finish(2)
    for kind in range(2):
        keep_mlp[kind].wait()
        for mask in (1, 2, 3):
            arrive(mlp_out.at[kind, d_at ^ mask], recv_b.at[kind, mask])
    keep_last.wait()
    for place, (a, b) in enumerate(others):
        at = (d_at ^ a) * n_fs + (f_at ^ b)
        arrive(last_got.at[at], recv_n.at[1, place])
    for copy in sent:
        if not any(copy is gone for gone in leaving):
            copy.wait_send()
    for place in range(3):
        rows = grads.at[2, block_rows(f_at), :]
        pltpu.make_async_copy(rows, rows, send_m.at[2, 4 + place]).wait()


def backward_kernel(forward, ada, kept, cot, count):
    (
        qkv_all,
        one_all,
        two_all,
        projected,
        hidden_all,
        branch_all,
        proj_dense,
        attended,
        hidden_rows,
        mixed_rows,
        mods,
        bias,
        signals,
    ) = forward
    n_dp, n_fs = lax.axis_size("dp"), lax.axis_size("fsdp")
    n_all = n_dp * n_fs
    slots, features = kept.shape
    row_width = features // n_dp
    unit = features // n_fs
    ada_width = 6 * features // n_fs
    cols = projected.shape[2]
    low, full = jnp.bfloat16, jnp.float32
    vmem = pl.BlockSpec(memory_space=pltpu.VMEM)
    anywhere = pl.BlockSpec(memory_space=pl.ANY)
    image = (slots, features)
    shapes = [
        (image, low),
        (image, full),
        ((2, n_dp, unit, row_width), low),
        ((unit, features), full),
        ((row_width, ada_width), full),
        ((n_all, 24, 128), full),
    ]
    scratch = [
        (one_all.shape, low),
        (two_all.shape, low),
        (projected.shape, low),
        ((n_dp,) + image, low),
        ((n_dp,) + image, low),
        (proj_dense.shape, low),
        ((n_dp,) + image, low),
        ((n_dp,) + image, low),
        ((n_dp,) + image, low),
        ((2, 2) + image, low),
        ((2,) + image, low),
        ((2,) + image, low),
        ((3, features, features), low),
        ((3, 4, unit, features), low),
        ((3, 3, unit, features), low),
        ((2, n_dp, slots, row_width), low),
        ((n_dp,) + image, low),
        (image, low),
        ((n_dp, n_fs // 2, slots, 2 * cols), low),
        ((2,) + qkv_all.shape[1:], low),
        ((2, n_dp, unit, row_width), low),
        ((8, features), full),
        ((n_fs, 8, 128), full),
        ((n_fs, 8, 128), full),
        ((n_fs, 8, 128), full),
        ((n_all, 8, 128), full),
        ((n_all, 24, 128), full),
    ]
    dma = pltpu.SemaphoreType.DMA
    sems = [(3, 7), (2, 3), (4,), (2 + n_fs // 2, 4), (2, n_all - 1), (n_fs,), (2, 4)]
    return pl.pallas_call(
        functools.partial(backward_body, (HEADS, features // HEADS, ada_width)),
        out_shape=[jax.ShapeDtypeStruct(shape, kind) for shape, kind in shapes],
        in_specs=[anywhere] * 7
        + [vmem] * 9
        + [pl.BlockSpec(memory_space=pltpu.SMEM)],
        out_specs=[vmem] * len(shapes),
        scratch_shapes=[pltpu.VMEM(shape, kind) for shape, kind in scratch]
        + [dma(shape) for shape in sems for side in range(2)]
        + [dma((4,)), dma((6,))],
        compiler_params=pltpu.CompilerParams(
            collective_id=6, has_side_effects=True, vmem_limit_bytes=64 * 1024 * 1024 - 65536
        ),
        name="backward",
    )(
        qkv_all,
        one_all,
        two_all,
        projected,
        hidden_all,
        branch_all,
        proj_dense,
        ada,
        signals,
        attended,
        hidden_rows,
        mixed_rows,
        kept,
        mods,
        bias,
        cot,
        count,
    )


def shards(
    patches_in,
    condition,
    keep_count,
    keep_index,
    w_ada,
    b_ada,
    w_qkv,
    qv_bias,
    w_proj,
    w_fc1,
    fc1_bias,
    w_fc2,
    out_bias,
    cotangent,
):
    n_dp, n_fs = lax.axis_size("dp"), lax.axis_size("fsdp")
    n_all = n_dp * n_fs
    d_at, f_at = lax.axis_index("dp"), lax.axis_index("fsdp")
    features = patches_in.shape[2]
    row_width = features // n_dp
    half_rows = row_width // 2
    low = jnp.bfloat16
    full = jnp.float32

    unit_width = w_fc1.shape[1] // n_dp
    one_pieces = w_fc1.reshape(row_width, n_dp, unit_width).transpose(1, 2, 0)
    two_pieces = (
        w_fc2.reshape(n_fs // n_dp, n_dp, unit_width, w_fc2.shape[1])
        .transpose(1, 3, 0, 2)
        .reshape(n_dp, w_fc2.shape[1], -1)
    )
    pieces = jnp.concatenate([one_pieces, two_pieces], axis=2)

    def beside(shard):
        return jnp.concatenate([shard[:half_rows], shard[half_rows:]], axis=1)

    cond_float = condition.astype(full)
    signal = swish(cond_float).astype(low).astype(full)
    shards_bias = [b_ada, qv_bias, fc1_bias, out_bias]
    biases = jnp.concatenate(shards_bias).astype(full)
    notes = jnp.concatenate(
        [
            jnp.pad(signal.reshape(n_dp, row_width), ((0, 0), (0, 384 - row_width))),
            jnp.broadcast_to(jnp.pad(biases, (0, 640 - biases.shape[0])), (n_dp, 640)),
        ],
        axis=1,
    ).reshape(n_dp, 8, 128)
    ada_width = w_ada.shape[1]
    ada = jnp.pad(w_ada, ((0, 384 - row_width), (0, 896 - ada_width)))

    indices = keep_index[0]
    inputs = patches_in[0]
    kept_in = jnp.take(inputs, indices, axis=0).astype(full)
    forward = forward_kernel(
        notes,
        ada,
        pieces,
        beside(w_qkv),
        beside(w_proj),
        kept_in,
        cotangent[0],
        keep_count,
        (ada_width, qv_bias.shape[0], fc1_bias.shape[0], out_bias.shape[0]),
    )
    block_out, d_kept, mlp_out, att_out, grad_ada, last = backward_kernel(
        forward, ada, kept_in, cotangent[0], keep_count
    )
    grad_patches = jnp.zeros(inputs.shape, full).at[indices].set(d_kept, unique_indices=True)[None]

    qkv_cols, proj_cols = w_qkv.shape[1], w_proj.shape[1]

    def above(left, width):
        return jnp.concatenate(
            [att_out[:, left : left + width], att_out[:, left + width : left + 2 * width]], axis=0
        )

    one_out = mlp_out[0].reshape(-1, row_width).T.astype(full)
    two_out = (
        mlp_out[1]
        .reshape(n_dp, w_fc2.shape[1], n_fs // n_dp, unit_width)
        .transpose(2, 0, 3, 1)
        .reshape(w_fc2.shape)
        .astype(full)
    )

    last = last.reshape(n_dp, n_fs, 3, -1)
    d_signal = jnp.sum(last[:, :, 0, :row_width], axis=1).reshape(1, features)
    unused, swish_pull = jax.vjp(swish, cond_float)
    grad_condition = swish_pull(d_signal)[0]
    own = d_at * n_fs + f_at
    head_size = qv_bias.shape[0]
    heads_per = qkv_cols // head_size

    def line_of(kind, d, f):
        start = (d, f, kind, 0)
        return lax.dynamic_slice(last, start, (1, 1, 1, last.shape[3])).reshape(-1)

    def summed(f):
        start = (0, f, 1, 0)
        return jnp.sum(
            lax.dynamic_slice(last, start, (n_dp, 1, 1, last.shape[3])).reshape(n_dp, -1), axis=0
        )

    ada_count = b_ada.shape[0]
    ada_bias = lax.dynamic_slice_in_dim(
        line_of(2, d_at, own // n_dp), (own % n_dp) * ada_count, ada_count
    )
    block = jnp.where(own < HEADS, own, own + HEADS)
    qv_out = lax.dynamic_slice_in_dim(
        summed(block // heads_per), (block % heads_per) * head_size, head_size
    )
    per = proj_cols // head_size
    place = own % HEADS
    start = jnp.where(own < HEADS, qkv_cols, qkv_cols + proj_cols) + (place % per) * head_size
    out_out = lax.dynamic_slice_in_dim(summed(place // per), start, head_size)
    bias_out = lax.dynamic_slice_in_dim(
        line_of(1, own % n_dp, own // n_dp), qkv_cols + 2 * proj_cols, unit_width
    )
    return (
        block_out[None],
        grad_patches,
        grad_condition,
        grad_ada,
        ada_bias,
        above(0, qkv_cols),
        qv_out,
        above(2 * qkv_cols, proj_cols),
        one_out,
        bias_out,
        two_out,
        out_out,
    )


def kernels_fit(*arrays):
    w_qkv, w_fc1 = arrays[6], arrays[9]
    features = arrays[0].shape[2]
    unit_width = w_fc1.shape[1] // lax.axis_size("dp")
    return (
        w_qkv.shape[1] % (features // HEADS) == 0
        and w_qkv.shape[0] % 16 == 0
        and unit_width % 16 == 0
        and unit_width == arrays[11].shape[1]
        and lax.axis_size("dp") == 4
        and lax.axis_size("fsdp") == 8
    )


def solution(mesh):
    both = ("dp", "fsdp")
    weight = P("dp", "fsdp")
    flat = P(both)
    placed = (
        P(both, None, None),
        P(both, None),
        flat,
        P(both, None),
        weight,
        flat,
        weight,
        flat,
        weight,
        weight,
        flat,
        weight,
        flat,
        P(both, None, None),
    )

    def chosen(*arrays):
        return (shards if kernels_fit(*arrays) else plain_shards)(*arrays)

    return jax.shard_map(
        chosen,
        mesh=mesh,
        in_specs=placed,
        out_specs=(
            P(both, None, None),
            P(both, None, None),
            P(both, None),
            weight,
            flat,
            weight,
            flat,
            weight,
            weight,
            flat,
            weight,
            flat,
        ),
        check_vma=False,
    )
```

```python
import functools
import math

import jax
import jax.numpy as jnp
from jax import lax
from jax.experimental import pallas as pl
from jax.experimental.pallas import tpu as pltpu
from jax.sharding import PartitionSpec as P

HEADS = 16


epsilon = 1e-06
negative = -1e30


def layer_norm(inputs):
    centred = inputs - jnp.mean(inputs, axis=-1, keepdims=True)
    rstd = lax.rsqrt(jnp.mean(centred * centred, axis=-1, keepdims=True) + epsilon)
    return (centred * rstd, rstd)


def norm_back(upstream, normed, rstd):
    return rstd * (
        upstream
        - jnp.mean(upstream, axis=-1, keepdims=True)
        - normed * jnp.mean(upstream * normed, axis=-1, keepdims=True)
    )


def swish(inputs):
    return inputs / (1.0 + jnp.exp(-inputs))


def gelu_tanh(inputs):
    return (
        0.5
        * inputs
        * (1.0 + jnp.tanh(0.7978845608028654 * (inputs + 0.044715 * inputs * inputs * inputs)))
    )


def contract(left, right, left_dims, right_dims):
    return lax.dot_general(
        left, right, ((left_dims, right_dims), ((), ())), preferred_element_type=jnp.float32
    )


def rows_rows(left, right):
    return contract(left, right, (0,), (0,))


def times_transposed(left, right):
    return contract(left, right, (1,), (1,))


def inner_rows(left, right):
    return lax.dot_general(
        left, right, (((0,), (0,)), ((), ())), preferred_element_type=jnp.float32
    )


def flat_bias(collected):
    return collected.reshape(-1)


def gather_forward(w_ada, b_ada, w_qkv, qv_bias, w_proj, w_fc1, fc1_bias, w_fc2, out_bias):
    part_ada, part_qkv, part_proj, part_one, part_two, bias_ada, bias_qv, bias_one, bias_out = (
        lax.all_gather(w_ada, "fsdp", axis=1, tiled=True),
        lax.all_gather(w_qkv, "fsdp", axis=1, tiled=True),
        lax.all_gather(w_proj, "fsdp", axis=1, tiled=True),
        lax.all_gather(w_fc1, "fsdp", axis=1, tiled=True),
        lax.all_gather(w_fc2, "fsdp", axis=1, tiled=True),
        lax.all_gather(b_ada.reshape(1, 1, -1), "fsdp", axis=1, tiled=True),
        lax.all_gather(qv_bias.reshape(1, 1, -1), "fsdp", axis=1, tiled=True),
        lax.all_gather(fc1_bias.reshape(1, 1, -1), "fsdp", axis=1, tiled=True),
        lax.all_gather(out_bias.reshape(1, 1, -1), "fsdp", axis=1, tiled=True),
    )
    gathered = (
        lax.all_gather(part_ada, "dp", axis=0, tiled=True),
        lax.all_gather(part_qkv, "dp", axis=0, tiled=True),
        lax.all_gather(part_proj, "dp", axis=0, tiled=True),
        lax.all_gather(part_one, "dp", axis=0, tiled=True),
        lax.all_gather(part_two, "dp", axis=0, tiled=True),
        lax.all_gather(bias_ada, "dp", axis=0, tiled=True),
        lax.all_gather(bias_qv, "dp", axis=0, tiled=True),
        lax.all_gather(bias_one, "dp", axis=0, tiled=True),
        lax.all_gather(bias_out, "dp", axis=0, tiled=True),
    )
    return (
        gathered[0],
        flat_bias(gathered[5]),
        gathered[1],
        flat_bias(gathered[6]),
        gathered[2],
        gathered[3],
        flat_bias(gathered[7]),
        gathered[4],
        flat_bias(gathered[8]),
    )


def gather_backward(w_ada, w_qkv, w_proj, w_fc1, w_fc2):
    part_ada, part_qkv, part_proj, part_one, part_two = (
        lax.all_gather(w_ada, "fsdp", axis=1, tiled=True),
        lax.all_gather(w_qkv, "fsdp", axis=1, tiled=True),
        lax.all_gather(w_proj, "fsdp", axis=1, tiled=True),
        lax.all_gather(w_fc1, "fsdp", axis=1, tiled=True),
        lax.all_gather(w_fc2, "fsdp", axis=1, tiled=True),
    )
    return (
        lax.all_gather(part_ada, "dp", axis=0, tiled=True),
        lax.all_gather(part_qkv, "dp", axis=0, tiled=True),
        lax.all_gather(part_proj, "dp", axis=0, tiled=True),
        lax.all_gather(part_one, "dp", axis=0, tiled=True),
        lax.all_gather(part_two, "dp", axis=0, tiled=True),
    )


def split_bias(term):
    return term.reshape(lax.axis_size("dp"), lax.axis_size("fsdp"), -1)


def own_bias(summed):
    return lax.dynamic_index_in_dim(summed, lax.axis_index("dp"), 0, keepdims=False).reshape(-1)


def owned_columns(matrix, width):
    return lax.dynamic_slice_in_dim(matrix, lax.axis_index("dp") * width, width, 1)


def column_totals(matrix):
    return jnp.sum(matrix.astype(jnp.float32), axis=0)


def plain_shards(
    patches_in,
    condition,
    keep_count,
    keep_index,
    w_ada,
    b_ada,
    w_qkv,
    qv_bias,
    w_proj,
    w_fc1,
    fc1_bias,
    w_fc2,
    out_bias,
    cotangent,
):
    images, kept_slots = keep_index.shape
    features = patches_in.shape[2]
    hidden_units = w_fc2.shape[0] * lax.axis_size("dp")
    all_rows = images * kept_slots
    head_size = features // HEADS
    factor = 1.0 / math.sqrt(head_size)
    head_shape = (images, kept_slots, HEADS, head_size)
    row_width = features // lax.axis_size("dp")
    unit_width = hidden_units // lax.axis_size("dp")
    ada_full, ada_bias, qkv_full, qv_full, proj_full, one_full, one_bias, two_full, out_full = (
        gather_forward(w_ada, b_ada, w_qkv, qv_bias, w_proj, w_fc1, fc1_bias, w_fc2, out_bias)
    )
    inputs = patches_in.astype(jnp.float32)
    kept_in = jnp.take_along_axis(inputs, keep_index[:, :, None], axis=1)
    allowed = (jnp.arange(kept_slots)[None, :] < keep_count[:, None])[:, None, None, :]
    cond_float = condition.astype(jnp.float32)
    signal = swish(cond_float).astype(jnp.bfloat16)
    modulation = jnp.dot(signal, ada_full, preferred_element_type=jnp.float32) + ada_bias.astype(
        jnp.float32
    )
    shift_one, scale_one, gate_one, shift_two, scale_two, gate_two = [
        modulation[:, None, column * features : (column + 1) * features] for column in range(6)
    ]
    normed_one, rstd_one = layer_norm(kept_in)
    hidden_one = (
        (normed_one * (1.0 + scale_one) + shift_one)
        .astype(jnp.bfloat16)
        .reshape(all_rows, features)
    )
    qv_float = qv_full.astype(jnp.float32)
    qkv_bias = jnp.concatenate(
        [qv_float[:features], jnp.zeros((features,), jnp.float32), qv_float[features:]]
    )
    projected = (
        jnp.dot(hidden_one, qkv_full, preferred_element_type=jnp.float32) + qkv_bias
    ).astype(jnp.bfloat16)
    queries = projected[:, :features].reshape(head_shape)
    key_rows = projected[:, features : 2 * features].reshape(head_shape)
    values = projected[:, 2 * features :].reshape(head_shape)
    scores = (
        jnp.einsum("iqhe,ikhe->ihqk", queries, key_rows, preferred_element_type=jnp.float32)
        * factor
    )
    scores = jnp.where(allowed, scores, negative)
    top_score = jnp.max(scores, axis=-1, keepdims=True)
    exponent = jnp.exp(scores - top_score)
    row_total = jnp.sum(exponent, axis=-1, keepdims=True)
    log_total = top_score + jnp.log(row_total)
    softmax_low = (exponent / row_total).astype(jnp.bfloat16)
    mixed = jnp.einsum("ihqk,ikhe->iqhe", softmax_low, values, preferred_element_type=jnp.float32)
    mixed_low = mixed.reshape(all_rows, features).astype(jnp.bfloat16)
    out_float = out_full.astype(jnp.float32)
    attended = (
        jnp.dot(mixed_low, proj_full, preferred_element_type=jnp.float32) + out_float[:features]
    ).reshape(images, kept_slots, features)
    middle = kept_in + gate_one * attended
    normed_two, rstd_two = layer_norm(middle)
    hidden_two = (
        (normed_two * (1.0 + scale_two) + shift_two)
        .astype(jnp.bfloat16)
        .reshape(all_rows, features)
    )
    raised = jnp.dot(hidden_two, one_full, preferred_element_type=jnp.float32) + one_bias.astype(
        jnp.float32
    )
    activated = gelu_tanh(raised).astype(jnp.bfloat16)
    branch = (
        jnp.dot(activated, two_full, preferred_element_type=jnp.float32) + out_float[features:]
    ).reshape(images, kept_slots, features)
    block_out = (middle + gate_two * branch).astype(jnp.bfloat16)
    ada_back, qkv_back, proj_back, one_back, two_back = gather_backward(
        w_ada, w_qkv, w_proj, w_fc1, w_fc2
    )
    upstream = cotangent.astype(jnp.float32)
    d_gate_two = jnp.sum(upstream * branch, axis=1)
    d_branch = (gate_two * upstream).reshape(all_rows, features).astype(jnp.bfloat16)
    d_activated = times_transposed(d_branch, two_back)
    unused, gelu_pull = jax.vjp(gelu_tanh, raised)
    d_raised = gelu_pull(d_activated)[0].astype(jnp.bfloat16)
    d_hidden_two = times_transposed(d_raised, one_back).reshape(images, kept_slots, features)
    d_shift_two = jnp.sum(d_hidden_two, axis=1)
    d_scale_two = jnp.sum(d_hidden_two * normed_two, axis=1)
    d_middle = upstream + norm_back(d_hidden_two * (1.0 + scale_two), normed_two, rstd_two)
    d_gate_one = jnp.sum(d_middle * attended, axis=1)
    d_attended = (gate_one * d_middle).reshape(all_rows, features).astype(jnp.bfloat16)
    d_mixed = times_transposed(d_attended, proj_back).astype(jnp.bfloat16).reshape(head_shape)
    scores_again = (
        jnp.einsum("iqhe,ikhe->ihqk", queries, key_rows, preferred_element_type=jnp.float32)
        * factor
    )
    scores_again = jnp.where(allowed, scores_again, negative)
    softmax_again = jnp.exp(scores_again - log_total)
    d_softmax = jnp.einsum("iqhe,ikhe->ihqk", d_mixed, values, preferred_element_type=jnp.float32)
    row_delta = jnp.sum(d_softmax * softmax_again, axis=-1, keepdims=True)
    d_scores = (softmax_again * (d_softmax - row_delta)).astype(jnp.bfloat16)
    d_queries = (
        jnp.einsum("ihqk,ikhe->iqhe", d_scores, key_rows, preferred_element_type=jnp.float32)
        * factor
    )
    d_keys = (
        jnp.einsum("ihqk,iqhe->ikhe", d_scores, queries, preferred_element_type=jnp.float32)
        * factor
    )
    d_values = jnp.einsum(
        "ihqk,iqhe->ikhe",
        softmax_again.astype(jnp.bfloat16),
        d_mixed,
        preferred_element_type=jnp.float32,
    )
    d_projected = jnp.concatenate(
        [
            d_queries.reshape(all_rows, features),
            d_keys.reshape(all_rows, features),
            d_values.reshape(all_rows, features),
        ],
        axis=1,
    ).astype(jnp.bfloat16)
    d_hidden_one = times_transposed(d_projected, qkv_back).reshape(images, kept_slots, features)
    d_shift_one = jnp.sum(d_hidden_one, axis=1)
    d_scale_one = jnp.sum(d_hidden_one * normed_one, axis=1)
    d_kept = d_middle + norm_back(d_hidden_one * (1.0 + scale_one), normed_one, rstd_one)
    grad_patches = jnp.zeros_like(inputs).at[jnp.arange(images)[:, None], keep_index].add(d_kept)
    d_modulation = jnp.concatenate(
        [d_shift_one, d_scale_one, d_gate_one, d_shift_two, d_scale_two, d_gate_two], axis=1
    ).astype(jnp.bfloat16)
    d_signal = times_transposed(d_modulation, ada_back)
    unused_too, swish_pull = jax.vjp(swish, cond_float)
    grad_condition = swish_pull(d_signal)[0]
    piece_one = lax.all_gather(hidden_one, "dp", axis=0, tiled=True)
    piece_proj_d = lax.all_gather(d_projected, "dp", axis=0, tiled=True)
    piece_mixed = lax.all_gather(mixed_low, "dp", axis=0, tiled=True)
    piece_att_d = lax.all_gather(d_attended, "dp", axis=0, tiled=True)
    piece_two = lax.all_gather(hidden_two, "dp", axis=0, tiled=True)
    piece_raised_d = lax.all_gather(d_raised, "dp", axis=0, tiled=True)
    piece_act = lax.all_gather(activated, "dp", axis=0, tiled=True)
    piece_branch_d = lax.all_gather(d_branch, "dp", axis=0, tiled=True)
    grad_qkv = inner_rows(owned_columns(piece_one, row_width), piece_proj_d)
    grad_proj = inner_rows(owned_columns(piece_mixed, row_width), piece_att_d)
    grad_one = inner_rows(owned_columns(piece_two, row_width), piece_raised_d)
    grad_two = inner_rows(owned_columns(piece_act, unit_width), piece_branch_d)
    qkv_sums = column_totals(piece_proj_d)
    proj_sums = column_totals(piece_att_d)
    one_sums = column_totals(piece_raised_d)
    two_sums = column_totals(piece_branch_d)
    piece_signal = lax.all_gather(signal, "dp", axis=0, tiled=True)
    piece_mod_d = lax.all_gather(d_modulation, "dp", axis=0, tiled=True)
    grad_ada = inner_rows(owned_columns(piece_signal, row_width), piece_mod_d)
    ada_sums = column_totals(piece_mod_d)
    grad_qv = jnp.concatenate([qkv_sums[:features], qkv_sums[2 * features :]])
    grad_out = jnp.concatenate([proj_sums, two_sums])
    terms = (
        grad_ada,
        grad_qkv,
        grad_proj,
        grad_one,
        grad_two,
        split_bias(ada_sums),
        split_bias(grad_qv),
        split_bias(one_sums),
        split_bias(grad_out),
    )
    (
        final_ada,
        final_qkv,
        final_proj,
        final_one,
        final_two,
        final_ada_bias,
        final_qv,
        final_bias,
        final_out,
    ) = (
        lax.psum_scatter(
            terms[0].astype(jnp.bfloat16), "fsdp", scatter_dimension=1, tiled=True
        ).astype(jnp.float32),
        lax.psum_scatter(
            terms[1].astype(jnp.bfloat16), "fsdp", scatter_dimension=1, tiled=True
        ).astype(jnp.float32),
        lax.psum_scatter(
            terms[2].astype(jnp.bfloat16), "fsdp", scatter_dimension=1, tiled=True
        ).astype(jnp.float32),
        lax.psum_scatter(
            terms[3].astype(jnp.bfloat16), "fsdp", scatter_dimension=1, tiled=True
        ).astype(jnp.float32),
        lax.psum_scatter(
            terms[4].astype(jnp.bfloat16), "fsdp", scatter_dimension=1, tiled=True
        ).astype(jnp.float32),
        lax.psum_scatter(
            terms[5].astype(jnp.bfloat16), "fsdp", scatter_dimension=1, tiled=True
        ).astype(jnp.float32),
        lax.psum_scatter(
            terms[6].astype(jnp.bfloat16), "fsdp", scatter_dimension=1, tiled=True
        ).astype(jnp.float32),
        lax.psum_scatter(
            terms[7].astype(jnp.bfloat16), "fsdp", scatter_dimension=1, tiled=True
        ).astype(jnp.float32),
        lax.psum_scatter(
            terms[8].astype(jnp.bfloat16), "fsdp", scatter_dimension=1, tiled=True
        ).astype(jnp.float32),
    )
    return (
        block_out,
        grad_patches,
        grad_condition,
        final_ada,
        own_bias(final_ada_bias),
        final_qkv,
        own_bias(final_qv),
        final_proj,
        final_one,
        own_bias(final_bias),
        final_two,
        own_bias(final_out),
    )


MESH = pl.DeviceIdType.MESH


def remote(source, target, send, recv, device):
    return pltpu.make_async_remote_copy(
        src_ref=source,
        dst_ref=target,
        send_sem=send,
        recv_sem=recv,
        device_id=device,
        device_id_type=MESH,
    )


def greet(devices):
    barrier = pltpu.get_barrier_semaphore()
    for device in devices:
        pl.semaphore_signal(barrier, 1, device_id=device, device_id_type=MESH)
    pl.semaphore_wait(barrier, len(devices))


def normed(value):
    centred = value - jnp.mean(value, axis=-1, keepdims=True)
    rstd = lax.rsqrt(jnp.mean(centred * centred, axis=-1, keepdims=True) + epsilon)
    return centred * rstd, rstd


def forward_body(
    sizes,
    note_ref,
    ada_ref,
    one_raw,
    two_raw,
    qkv_raw,
    proj_raw,
    patch_ref,
    index_ref,
    cot_ref,
    count_ref,
    qkv_hbm,
    one_hbm,
    two_hbm,
    projected_hbm,
    hidden_hbm,
    branch_hbm,
    proj_hbm,
    attended_ref,
    hidden_rows,
    mixed_rows,
    mod_ref,
    bias_ref,
    signal_ref,
    kept_ref,
    qkv_all,
    one_all,
    two_all,
    projected_ref,
    hidden_all,
    branch_all,
    proj_dense,
    proj_all,
    mixed_ref,
    piece_got,
    one_block,
    two_block,
    note_got,
    row_put,
    row_got,
    qkv_ref,
    proj_ref,
    piece_ref,
    send_n,
    recv_n,
    send_z,
    send_y,
    send_x,
    recv_w,
    send_e,
    recv_e,
    local,
    out_sem,
):
    heads, size, widths = sizes
    n_dp, n_fs = 4, 8
    d_at, f_at = lax.axis_index("dp"), lax.axis_index("fsdp")
    own_at = d_at * n_fs + f_at
    slots, features = kept_ref.shape
    half_rows, cols = qkv_ref.shape[0], qkv_ref.shape[1] // 2
    unit = one_block.shape[0]
    row_width = 2 * half_rows
    width = proj_ref.shape[1] // 2
    low = jnp.bfloat16
    full = jnp.float32
    others = [(a, b) for a in range(n_dp) for b in range(n_fs) if a or b]
    barrier = pltpu.get_barrier_semaphore()
    for a, b in others:
        pl.semaphore_signal(
            barrier, 1, device_id=(d_at ^ a, f_at ^ b), device_id_type=MESH
        )
    for part in range(2):
        rows = slice(part * half_rows, (part + 1) * half_rows)
        qkv_ref[:, part * cols : (part + 1) * cols] = qkv_raw[rows, :]
        proj_ref[:, part * width : (part + 1) * width] = proj_raw[:, rows].T
    pl.semaphore_wait(barrier, len(others))

    own_blocks = (qkv_ref, proj_ref, one_block, two_block)
    gathered = (qkv_all, proj_all, one_all, two_all)
    started = []
    middle_copies = []
    stores = []
    z_at = f_at // 2
    in_middle = (z_at == 1) | (z_at == 2)
    second = jnp.where(in_middle, 6, 4)
    third = 10 - second

    def store(source, target):
        copy = pltpu.make_async_copy(source, target, out_sem.at[len(stores)])
        copy.start()
        stores.append(copy)

    def slot(array, a, b):
        if array < 2:
            start = pl.multiple_of((d_at ^ a) * half_rows, 16)
            return gathered[array].at[f_at ^ b, pl.ds(start, half_rows), :]
        start = pl.multiple_of((f_at ^ b) * unit, 16)
        return gathered[array].at[pl.ds(start, unit), :]

    def push(source, target, send, recv, device):
        copy = remote(source, target, send, recv, device)
        copy.start()
        started.append(copy)

    def block(array, a, b):
        own = isinstance(b, int) and a == 0 and b == 0
        return own_blocks[array] if own else slot(array, a, b)

    def pass_on(array, a, b, axis, mask, sem):
        device = (d_at ^ mask, f_at) if axis == 0 else (d_at, f_at ^ mask)
        to_a, to_b = (a ^ mask, b) if axis == 0 else (a, b ^ mask)
        push(block(array, a, b), slot(array, a, b), sem, recv_w.at[array, to_a, to_b], device)

    def relay_middle(array, b, mask, place):
        copy = remote(
            block(array, 0, b),
            slot(array, 0, b),
            send_z.at[array, place],
            recv_w.at[array, 0, b ^ mask],
            (d_at, f_at ^ mask),
        )

        @pl.when(in_middle)
        def _():
            copy.start()

        middle_copies.append(copy)

    def arrive(array, a, b):
        place = slot(array, a, b)
        pltpu.make_async_copy(place, place, recv_w.at[array, a, b]).wait()

    def near(array, b, place):
        pass_on(array, 0, b, 1, 1, send_y.at[array, place])

    def onward(array, a, b, place):
        if a == 0:
            pass_on(array, a, b, 0, 2, send_x.at[array, 0, place])
        pass_on(array, a, b, 0, 1, send_x.at[array, 1 + a // 2, place])

    order = [0, 1, 2, second, 3, third, second ^ 1, third ^ 1]

    def begin(array):
        near(array, 0, 0)
        if array < 2:
            onward(array, 0, 0, 0)
        pass_on(array, 0, 0, 1, 2, send_z.at[array, 0])
        relay_middle(array, 0, 6, 1)

    def follow(array, step):
        arrive(array, 0, order[step])
        if step == 2:
            relay_middle(array, 2, 6, 2)
            near(array, 2, 1)
        if step == 3:
            relay_middle(array, 6, 2, 3)
            near(array, second, 2)
        if step == 5:
            relay_middle(array, 4, 2, 4)
            near(array, third, 3)
        if array < 2:
            onward(array, 0, order[step], step)

    begin(0)
    begin(1)
    for place, (a, b) in enumerate(others):
        push(
            note_ref.at[d_at ^ a],
            note_got.at[own_at],
            send_n.at[0, place],
            recv_n.at[0, place],
            (d_at ^ a, f_at ^ b),
        )
    for d in range(n_dp):
        piece_ref[d, :, :row_width] = one_raw[:, d * unit : (d + 1) * unit].T
        for e in range(2):
            start = (e * n_dp + d) * unit
            piece_ref[d, :, row_width + e * unit : row_width + (e + 1) * unit] = two_raw[
                :, start : start + unit
            ]
    stays = [
        pltpu.make_async_copy(note_ref.at[d_at], note_got.at[own_at], local.at[0]),
        pltpu.make_async_copy(qkv_ref, slot(0, 0, 0), local.at[1]),
        pltpu.make_async_copy(proj_ref, slot(1, 0, 0), local.at[2]),
        pltpu.make_async_copy(piece_ref.at[d_at], piece_got.at[d_at], local.at[3]),
    ]
    for stay in stays:
        stay.start()
    chosen = lax.broadcasted_iota(jnp.int32, (slots, patch_ref.shape[0]), 1) == index_ref[...]
    kept_ref[...] = jnp.dot(
        chosen.astype(full).astype(low), patch_ref[...], preferred_element_type=full
    )
    kept = kept_ref[...]
    normed_one, _ = normed(kept)
    follow(0, 1)
    follow(0, 2)
    for mask in (1, 2, 3):
        push(
            piece_ref.at[d_at ^ mask],
            piece_got.at[d_at],
            send_e.at[2, mask],
            recv_e.at[2, mask],
            (d_at ^ mask, f_at),
        )

    stays[0].wait()
    for place, (a, b) in enumerate(others):
        at = (d_at ^ a) * n_fs + (f_at ^ b)
        pltpu.make_async_copy(note_got.at[at], note_got.at[at], recv_n.at[0, place]).wait()
    notes = note_got[...]
    signals = jnp.concatenate([notes[:, row, :] for row in range(3)], axis=1).astype(low)
    signals = signals[:, :row_width]
    signal_ref[...] = signals
    terms = jnp.dot(signals, ada_ref[...], preferred_element_type=full)
    ada_width = widths[0]
    ada_piece = ada_width * n_fs // (n_dp * n_fs)

    def bias_piece(index, start, count):
        row = note_got[index]
        line = jnp.concatenate([row[3 + step : 4 + step, :] for step in range(5)], axis=1)
        return line[:, start : start + count]

    block_bias = jnp.concatenate(
        [bias_piece(f_at * n_dp + step, 0, ada_piece) for step in range(n_dp)], axis=1
    )
    first = (d_at == 0).astype(full)
    for row in range(7):
        count = min(128, ada_width - row * 128)
        span = slice(row * 128, row * 128 + count)
        piece = terms[:, span] + block_bias[:, span] * first
        if count < 128:
            piece = jnp.concatenate(
                [piece, jnp.zeros((piece.shape[0], 128 - count), full)], axis=1
            )
        row_put[:, row, :] = piece
    for place, (a, b) in enumerate(others):
        push(
            row_put.at[(d_at ^ a) * n_fs + (f_at ^ b)],
            row_got.at[own_at],
            send_n.at[1, place],
            recv_n.at[1, place],
            (d_at ^ a, f_at ^ b),
        )
    keep_row = pltpu.make_async_copy(row_put.at[own_at], row_got.at[own_at], local.at[0])
    keep_row.start()

    follow(0, 3)
    follow(1, 1)
    follow(1, 2)
    follow(0, 4)
    follow(0, 5)

    stays[3].wait()
    for mask in (1, 2, 3):
        place = piece_got.at[d_at ^ mask]
        pltpu.make_async_copy(place, place, recv_e.at[2, mask]).wait()
    one_block[...] = jnp.concatenate([piece_got[d, :, :row_width] for d in range(n_dp)], axis=1)
    two_block[...] = jnp.concatenate([piece_got[d, :, row_width:] for d in range(n_dp)], axis=1)
    follow(0, 6)
    follow(0, 7)
    follow(1, 3)
    begin(2)
    follow(1, 4)
    follow(1, 5)
    begin(3)
    follow(1, 6)
    follow(1, 7)
    keep_one = pltpu.make_async_copy(one_block, slot(2, 0, 0), local.at[3])
    keep_one.start()
    keep_two = pltpu.make_async_copy(two_block, slot(3, 0, 0), local.at[4])
    keep_two.start()

    qv_width, one_width, out_width = widths[1:]
    starts = [ada_piece, ada_piece + qv_width, ada_piece + qv_width + one_width]
    lines = []
    for index in range(n_dp * n_fs):
        lines.append(
            (
                bias_piece(index, starts[0], qv_width),
                bias_piece(index, starts[2], out_width),
            )
        )
    heads_per = cols // size
    for f in range(n_fs):
        parts = []
        for j in range(heads_per):
            head = f * heads_per + j
            if head < heads:
                parts.append(lines[head][0])
            elif head < 2 * heads:
                parts.append(jnp.zeros((1, size), full))
            else:
                parts.append(lines[head - heads][0])
        bias_ref[f : f + 1, :cols] = jnp.concatenate(parts, axis=1)
    bias_ref[8:9, :] = jnp.concatenate([line[1] for line in lines[:heads]], axis=1)
    bias_ref[9:10, :] = jnp.concatenate([line[1] for line in lines[heads:]], axis=1)
    bias_ref[10:11, :] = jnp.concatenate(
        [bias_piece(f * n_dp + d_at, starts[1], one_width) for f in range(n_fs)], axis=1
    )

    keep_row.wait()
    for place, (a, b) in enumerate(others):
        at = (d_at ^ a) * n_fs + (f_at ^ b)
        pltpu.make_async_copy(row_got.at[at], row_got.at[at], recv_n.at[1, place]).wait()
    sums = row_got[0:n_fs]
    for d in range(1, n_dp):
        sums = sums + row_got[d * n_fs : (d + 1) * n_fs]
    sums = jnp.concatenate([sums[:, row, :] for row in range(7)], axis=1)
    pieces = []
    for index in range(6 * n_dp):
        f, part = index // 3, index % 3
        pieces.append(sums[f : f + 1, part * row_width : (part + 1) * row_width])
    mods = []
    for row in range(6):
        mods.append(jnp.concatenate(pieces[row * n_dp : (row + 1) * n_dp], axis=1))
        mod_ref[row : row + 1, :] = mods[row]
    hidden_one = (normed_one * (1.0 + mods[1]) + mods[0]).astype(low)
    branch_all[0] = (mods[5] * cot_ref[...].astype(full)).astype(low)
    chunks = [
        hidden_one[:, place * half_rows : (place + 1) * half_rows] for place in range(2 * n_dp)
    ]
    for d in range(n_dp):
        hidden_rows[d] = jnp.concatenate(chunks[2 * d : 2 * d + 2], axis=1)
    halves = [jnp.concatenate(chunks[part::2], axis=1) for part in range(2)]

    def spread_step(buffer, kind, mask):
        for key in [0] if mask == 2 else [0, 2]:
            push(
                buffer.at[key],
                buffer.at[key ^ mask],
                send_e.at[kind, key ^ mask],
                recv_e.at[kind, key ^ mask],
                (d_at ^ mask, f_at),
            )

    def spread_wait(buffer, kind, keys):
        for key in keys:
            place = buffer.at[key]
            pltpu.make_async_copy(place, place, recv_e.at[kind, key]).wait()

    store(branch_all.at[0], branch_hbm.at[0])
    spread_step(branch_all, 0, 2)

    stays[1].wait()
    for step, b in enumerate(order):
        arrive(0, 2, b)
        onward(0, 2, b, step)
        arrive(0, 1, b)
        arrive(0, 3, b)
        f = f_at ^ b
        out = jnp.dot(halves[0], qkv_all[f, :, :cols], preferred_element_type=full)
        out = out + jnp.dot(halves[1], qkv_all[f, :, cols:], preferred_element_type=full)
        projected_ref[f] = (out + bias_ref[pl.ds(f, 1), :cols]).astype(low)
        store(qkv_all.at[f], qkv_hbm.at[f])
        if step in (2, 3, 4, 6):
            follow(2, {2: 1, 3: 2, 4: 3, 6: 5}[step])
        if step in (3, 5):
            follow(3, {3: 1, 5: 2}[step])

    allowed = lax.broadcasted_iota(jnp.int32, (slots, slots), 1) < count_ref[0]
    factor = 1.0 / math.sqrt(size)
    for h in range(heads):
        q, k, v = [
            projected_ref[f, :, j * size : (j + 1) * size]
            for f, j in (
                ((kind * heads + h) // heads_per, (kind * heads + h) % heads_per)
                for kind in range(3)
            )
        ]
        scores = contract(q, k, (1,), (1,)) * factor
        scores = jnp.where(allowed, scores, negative)
        exponent = jnp.exp(scores - jnp.max(scores, axis=-1, keepdims=True))
        softmax = exponent / jnp.sum(exponent, axis=-1, keepdims=True)
        mix = jnp.dot(softmax.astype(low), v, preferred_element_type=full).astype(low)
        pair, side = h // 2, h % 2
        start = ((pair % 2) * n_dp + pair // 2) * half_rows + side * size
        mixed_ref[:, start : start + size] = mix
        start = (pair % 2) * half_rows + side * size
        mixed_rows[pair // 2, :, start : start + size] = mix
        if h == 8:
            follow(3, 3)

    store(projected_ref, projected_hbm)
    for step, b in enumerate(order):
        arrive(1, 2, b)
        onward(1, 2, b, step)
    stays[2].wait()
    for b in order:
        arrive(1, 1, b)
        arrive(1, 3, b)
    for f in range(n_fs):
        for part in range(2):
            proj_dense[
                part * n_dp * half_rows : (part + 1) * n_dp * half_rows,
                f * width : (f + 1) * width,
            ] = proj_all[f, :, part * width : (part + 1) * width]
    attended = (
        jnp.dot(mixed_ref[...], proj_dense[...], preferred_element_type=full) + bias_ref[8:9, :]
    )
    attended_ref[...] = attended
    middle = kept + mods[2] * attended
    normed_two, _ = normed(middle)
    hidden_all[0] = (normed_two * (1.0 + mods[4]) + mods[3]).astype(low)
    spread_step(hidden_all, 1, 2)
    store(hidden_all.at[0], hidden_hbm.at[0])
    store(proj_dense, proj_hbm)
    follow(3, 5)
    spread_wait(branch_all, 0, [2])
    spread_step(branch_all, 0, 1)
    spread_wait(hidden_all, 1, [2])
    spread_step(hidden_all, 1, 1)
    for step in (4, 6, 7):
        arrive(2, 0, order[step])
    keep_one.wait()
    store(one_all, one_hbm)
    spread_wait(branch_all, 0, [1, 3])
    spread_wait(hidden_all, 1, [1, 3])
    for key in (1, 2, 3):
        store(hidden_all.at[key], hidden_hbm.at[key])
        store(branch_all.at[key], branch_hbm.at[key])
    for step in (4, 6, 7):
        arrive(3, 0, order[step])
    keep_two.wait()
    store(two_all, two_hbm)
    for copy in started:
        copy.wait_send()

    @pl.when(in_middle)
    def _():
        for copy in middle_copies:
            copy.wait_send()

    for copy in stores:
        copy.wait()


def forward_kernel(notes, ada, one, two, qkv, proj, patches, index, cot, count, widths):
    n_dp, n_fs = lax.axis_size("dp"), lax.axis_size("fsdp")
    slots, features = cot.shape
    unit = features // n_fs
    size = features // HEADS
    half_rows = qkv.shape[0] // 2
    cols = qkv.shape[1]
    pieces = (n_dp, unit, 4 * half_rows)
    n_all = n_dp * n_fs
    low, full = jnp.bfloat16, jnp.float32
    vmem = pl.BlockSpec(memory_space=pltpu.VMEM)
    image = (slots, features)
    shapes = [
        ((n_fs, n_dp * half_rows, 2 * cols), low),
        ((n_fs * unit, features), low),
        ((features, n_fs * unit), low),
        ((n_fs, slots, cols), low),
        ((n_dp,) + image, low),
        ((n_dp,) + image, low),
        ((features, features), low),
        (image, full),
        ((n_dp, slots, 2 * half_rows), low),
        ((n_dp, slots, 2 * half_rows), low),
        ((8, features), full),
        ((16, features), full),
        ((n_all, 2 * half_rows), low),
        (image, full),
    ]
    scratch = shapes[:7] + [
        ((n_fs, n_dp * half_rows, 2 * unit), low),
        (image, low),
        (pieces, low),
        ((unit, features), low),
        ((unit, features), low),
        ((n_all, 8, 128), full),
        ((n_all, 8, 128), full),
        ((n_all, 8, 128), full),
        ((half_rows, 2 * cols), low),
        ((half_rows, 2 * unit), low),
        (pieces, low),
    ]
    dma = pltpu.SemaphoreType.DMA
    return pl.pallas_call(
        functools.partial(forward_body, (HEADS, size, widths)),
        out_shape=[jax.ShapeDtypeStruct(shape, kind) for shape, kind in shapes],
        in_specs=[vmem] * 9 + [pl.BlockSpec(memory_space=pltpu.SMEM)],
        out_specs=[pl.BlockSpec(memory_space=pl.ANY)] * 7 + [vmem] * 7,
        scratch_shapes=[pltpu.VMEM(shape, kind) for shape, kind in scratch]
        + [dma((2, n_all - 1)), dma((2, n_all - 1)), dma((4, 5)), dma((4, 4))]
        + [dma((2, 3, n_fs)), dma((4, n_dp, n_fs)), dma((3, 4)), dma((3, 4)), dma((5,))]
        + [dma((24,))],
        compiler_params=pltpu.CompilerParams(
            collective_id=5, has_side_effects=True, vmem_limit_bytes=64 * 1024 * 1024 - 65536
        ),
        name="forward",
    )(notes, ada, one, two, qkv, proj, patches, index, cot, count)


def gelu_parts(raised):
    square = raised * raised
    inner = 0.7978845608028654 * raised * (1.0 + 0.044715 * square)
    bend = jnp.tanh(inner)
    slope = 0.7978845608028654 * (1.0 + 3.0 * 0.044715 * square)
    half = 0.5 * (1.0 + bend)
    return raised * half, half + 0.5 * raised * (1.0 - bend * bend) * slope


def column_sums(value):
    return jnp.sum(value, axis=0, keepdims=True)


def store_tile(ref, index, line):
    for row in range(8):
        piece = line[:, row * 128 : (row + 1) * 128]
        if piece.shape[1] == 0:
            break
        if piece.shape[1] < 128:
            rest = jnp.zeros((1, 128 - piece.shape[1]), line.dtype)
            piece = jnp.concatenate([piece, rest], axis=1)
        ref[index, row : row + 1, :] = piece


def backward_body(
    sizes,
    qkv_hbm,
    one_hbm,
    two_hbm,
    projected_hbm,
    hidden_hbm,
    branch_hbm,
    proj_hbm,
    hidden_rows,
    mixed_rows,
    ada_ref,
    signal_ref,
    attended_ref,
    kept_ref,
    mod_ref,
    bias_ref,
    index_ref,
    cot_ref,
    count_ref,
    block_ref,
    patch_out,
    qkv_out,
    proj_out,
    one_out,
    two_out,
    ada_out,
    last_got,
    mlp_out,
    one_ref,
    two_ref,
    projected_ref,
    hidden_all,
    branch_all,
    proj_ref,
    act_ref,
    d_raised_ref,
    part_ref,
    core_got,
    cross_put,
    cross_got,
    grads,
    got_y,
    got_z,
    rows_got,
    d_att_all,
    d_mixed_ref,
    d_proj_all,
    weight_ring,
    mlp_put,
    d_mod_ref,
    sum_put,
    sum_got,
    note_put,
    note_got,
    last_put,
    send_m,
    recv_m,
    send_d,
    recv_d,
    send_e,
    recv_e,
    send_p,
    recv_p,
    send_n,
    recv_n,
    send_s,
    recv_s,
    send_b,
    recv_b,
    local,
    load_sem,
):
    heads, size, ada_width = sizes
    n_dp, n_fs = 4, 8
    d_at, f_at = lax.axis_index("dp"), lax.axis_index("fsdp")
    own_at = d_at * n_fs + f_at
    slots, features = kept_ref.shape
    cols = projected_ref.shape[2]
    heads_per = cols // size
    row_width = features // n_dp
    half_rows = row_width // 2
    unit = features // n_fs
    low = jnp.bfloat16
    full = jnp.float32
    core, cross, near = (d_at ^ 1, f_at), (d_at ^ 2, f_at), (d_at, f_at ^ 1)
    loads = [
        pltpu.make_async_copy(source, target, load_sem.at[place])
        for place, (source, target) in enumerate(
            [
                (hidden_hbm, hidden_all),
                (one_hbm, one_ref),
                (branch_hbm, branch_all),
                (two_hbm, two_ref),
                (proj_hbm, proj_ref),
                (projected_hbm, projected_ref),
            ]
        )
    ]
    for load in loads:
        load.start()
    others = [(a, b) for a in range(n_dp) for b in range(n_fs) if a or b]
    greet([(d_at ^ a, f_at ^ b) for a, b in others])
    sent = []

    def push(source, target, send, recv, device):
        copy = remote(source, target, send, recv, device)
        copy.start()
        sent.append(copy)
        return copy

    def arrive(place, recv):
        pltpu.make_async_copy(place, place, recv).wait()

    stays = []
    for kind, source in enumerate((hidden_rows, mixed_rows)):
        for mask in (2, 3, 1):
            push(
                source.at[d_at ^ mask],
                rows_got.at[kind, mask],
                send_p.at[kind, mask],
                recv_p.at[kind, mask],
                (d_at ^ mask, f_at),
            )
        stays.append(
            pltpu.make_async_copy(source.at[d_at], rows_got.at[kind, 0], local.at[kind])
        )
        stays[kind].start()

    def image_step(image, carry):
        raised = contract(hidden_all[image], one_ref[...], (1,), (1,)) + bias_ref[10:11, :]
        active, slope = gelu_parts(raised)
        act_ref[image] = active.astype(low)
        d_active = jnp.dot(branch_all[image], two_ref[...], preferred_element_type=full)
        d_raised_ref[image] = (d_active * slope).astype(low)
        return carry

    for load in loads[:4]:
        load.wait()
    lax.fori_loop(0, n_dp, image_step, 0)

    def flat(ref, start, count):
        return ref[:, :, pl.ds(start, count)].reshape(n_dp * slots, count)

    def weight_grad(kind, left, right):
        step = features // 3
        for part in range(3):
            grads[kind, part * step : (part + 1) * step, :] = rows_rows(
                flat(left, part * step, step), flat(right, 0, features)
            ).astype(low)

    def block_rows(index):
        return pl.ds(pl.multiple_of(index * unit, 16), unit)

    def send_block(kind, place, index):
        push(
            grads.at[kind, block_rows(index), :],
            got_y.at[kind, place],
            send_m.at[kind, place],
            recv_m.at[kind, place],
            near,
        )

    def fold_block(kind, place, index):
        arrive(got_y.at[kind, place], recv_m.at[kind, place])
        rows = block_rows(index)
        grads[kind, rows, :] = (
            grads[kind, rows, :].astype(full) + got_y[kind, place].astype(full)
        ).astype(low)

    def send_wide(kind, index, mask):
        place = mask // 2 - 1
        return remote(
            grads.at[kind, block_rows(index), :],
            got_z.at[kind, place],
            send_m.at[kind, 4 + place],
            recv_m.at[kind, 4 + place],
            (d_at, index),
        )

    waves = (2, 4, 6, 0)

    def fold_wave(kind, place):
        fold_block(kind, place, f_at ^ waves[place])
        if waves[place]:
            copy = send_wide(kind, f_at ^ waves[place], waves[place])
            copy.start()
            sent.append(copy)

    def finish(kind):
        total = grads[kind, block_rows(f_at), :].astype(full)
        for place in range(3):
            arrive(got_z.at[kind, place], recv_m.at[kind, 4 + place])
            total = total + got_z[kind, place].astype(full)
        return total

    weight_grad(1, branch_all, act_ref)
    for place, wide in enumerate((2, 4, 6, 0)):
        send_block(1, place, f_at ^ wide ^ 1)

    def part_step(left, right, dims):
        def step(image, carry):
            part_ref[image] = contract(left[image], right[...], (1,), dims).astype(low)
            return carry

        lax.fori_loop(0, n_dp, step, 0)

    def core_send(kind):
        return [
            push(
                part_ref.at[image],
                core_got.at[kind, place],
                send_d.at[kind, place],
                recv_d.at[kind, place],
                core,
            )
            for place, image in enumerate((3, 1))
        ]

    def cross_send(kind):
        arrive(core_got.at[kind, 0], recv_d.at[kind, 0])
        cross_put[kind] = (
            part_ref[2].astype(full) + core_got[kind, 0].astype(full)
        ).astype(low)
        push(
            cross_put.at[kind], cross_got.at[kind], send_d.at[kind, 2], recv_d.at[kind, 2], cross
        )
        arrive(core_got.at[kind, 1], recv_d.at[kind, 1])

    part_step(d_raised_ref, one_ref, (0,))
    leaving = core_send(0)
    cross_send(0)
    own_part = part_ref[0].astype(full) + core_got[0, 1].astype(full)
    weight_grad(0, d_raised_ref, hidden_all)
    for place, wide in enumerate((2, 4, 6, 0)):
        send_block(0, place, f_at ^ wide ^ 1)
    for copy in leaving:
        copy.wait_send()
    part_step(act_ref, two_ref, (1,))
    core_send(1)
    cross_send(1)
    fold_wave(1, 0)
    one_sum = jnp.zeros((1, features), full)
    for image in range(n_dp):
        one_sum = one_sum + column_sums(d_raised_ref[image].astype(full))
    branch_sum = column_sums(branch_all[0].astype(full))

    mods = [mod_ref[row : row + 1, :] for row in range(6)]
    kept = kept_ref[...]
    attended = attended_ref[...]
    middle = kept + mods[2] * attended
    normed_two, rstd_two = normed(middle)
    upstream = cot_ref[...].astype(full)
    fold_wave(1, 1)
    loads[4].wait()
    arrive(cross_got.at[0], recv_d.at[0, 2])
    d_hidden_two = own_part + cross_got[0].astype(full)
    d_mod_ref[3:4, :] = column_sums(d_hidden_two)
    d_mod_ref[4:5, :] = column_sums(d_hidden_two * normed_two)
    d_middle = upstream + norm_back(d_hidden_two * (1.0 + mods[4]), normed_two, rstd_two)
    d_mod_ref[2:3, :] = column_sums(d_middle * attended)
    d_attended = (mods[2] * d_middle).astype(low)
    d_att_all[0] = d_attended
    patch_out[:slots, :] = d_middle
    att_sum = column_sums(d_attended.astype(full))
    d_mixed_ref[...] = contract(d_attended, proj_ref[...], (1,), (1,)).astype(low)
    push(d_att_all.at[0], d_att_all.at[2], send_e.at[2], recv_e.at[2], cross)
    push(d_att_all.at[0], d_att_all.at[1], send_e.at[1], recv_e.at[1], core)

    fold_wave(1, 2)
    loads[5].wait()

    leaps = (3, 2, 1, 0)
    turn = [(f_at // 2) ^ leap for leap in leaps]

    def pass_pair(place):
        push(
            d_proj_all.at[0, turn[place]],
            d_proj_all.at[2, turn[place]],
            send_p.at[2 + place, 2],
            recv_p.at[2 + place, 2],
            cross,
        )
        push(
            d_proj_all.at[0, turn[place]],
            d_proj_all.at[1, turn[place]],
            send_p.at[2 + place, 1],
            recv_p.at[2 + place, 1],
            core,
        )

    def relay_pair(place):
        arrive(d_proj_all.at[2, turn[place]], recv_p.at[2 + place, 2])
        push(
            d_proj_all.at[2, turn[place]],
            d_proj_all.at[3, turn[place]],
            send_p.at[2 + place, 3],
            recv_p.at[2 + place, 3],
            core,
        )

    allowed = lax.broadcasted_iota(jnp.int32, (slots, slots), 1) < count_ref[0]
    factor = 1.0 / math.sqrt(size)
    for h in range(heads):
        places = [
            ((kind * heads + h) // heads_per, (kind * heads + h) % heads_per)
            for kind in range(3)
        ]
        q, k, v = [projected_ref[f, :, j * size : (j + 1) * size] for f, j in places]
        pair, side = h // 2, h % 2
        start = ((pair % 2) * n_dp + pair // 2) * half_rows + side * size
        d_mix = d_mixed_ref[:, start : start + size]
        scores = contract(q, k, (1,), (1,)) * factor
        scores = jnp.where(allowed, scores, negative)
        exponent = jnp.exp(scores - jnp.max(scores, axis=-1, keepdims=True))
        softmax = exponent / jnp.sum(exponent, axis=-1, keepdims=True)
        d_softmax = contract(d_mix, v, (1,), (1,))
        delta = jnp.sum(d_softmax * softmax, axis=-1, keepdims=True)
        d_scores = (softmax * (d_softmax - delta)).astype(low)
        results = [
            jnp.dot(d_scores, k, preferred_element_type=full) * factor,
            rows_rows(d_scores, q) * factor,
            rows_rows(softmax.astype(low), d_mix),
        ]
        for (f, j), result in zip(places, results):
            start = (f % 2) * cols + j * size
            d_proj_all[0, f // 2, :, start : start + size] = result.astype(low)
    for place in range(4):
        pass_pair(place)
    fold_wave(1, 3)


    odd = f_at % 2

    def grad_pair(place):
        for mask in (1, 3):
            arrive(d_proj_all.at[mask, turn[place]], recv_p.at[2 + place, mask])
        result = rows_rows(
            rows_got[0].reshape(n_dp * slots, row_width),
            d_proj_all[:, turn[place]].reshape(n_dp * slots, 2 * cols),
        ).astype(low)
        for side in range(2):
            rows = block_rows(2 * turn[place] + side)
            for part in range(2):
                grads[2, rows, part * cols : (part + 1) * cols] = result[
                    part * half_rows : (part + 1) * half_rows, side * cols : (side + 1) * cols
                ]
        send_block(2, place, 2 * turn[place] + 1 - odd)

    def fold_pair(place):
        fold_block(2, place, 2 * turn[place] + odd)
        if leaps[place]:
            copy = send_wide(2, 2 * turn[place] + odd, 2 * leaps[place])
            copy.start()
            sent.append(copy)

    arrive(cross_got.at[1], recv_d.at[1, 2])
    branch = (
        part_ref[0].astype(full)
        + core_got[1, 1].astype(full)
        + cross_got[1].astype(full)
        + bias_ref[9:10, :]
    )
    d_mod_ref[5:6, :] = column_sums(upstream * branch)

    tall = weight_ring.shape[1]
    weights = [
        pltpu.make_async_copy(
            qkv_hbm.at[place // 2, pl.ds((place % 2) * tall, tall), :],
            weight_ring.at[place % 2],
            local.at[2 + place % 2],
        )
        for place in range(2 * n_fs)
    ]
    weights[0].start()
    quarters = [[jnp.zeros((slots, tall), full) for side in range(2)] for part in range(2)]
    for f in range(n_fs):
        own = d_proj_all[0, f // 2, :, (f % 2) * cols : (f % 2 + 1) * cols]
        for side in range(2):
            place = 2 * f + side
            if place + 1 < 2 * n_fs:
                weights[place + 1].start()
            weights[place].wait()
            for part in range(2):
                quarters[part][side] = quarters[part][side] + contract(
                    own, weight_ring[side, :, part * cols : (part + 1) * cols], (1,), (1,)
                )
        line = jnp.concatenate(
            [
                column_sums(own.astype(full)),
                att_sum[:, f * unit : (f + 1) * unit],
                branch_sum[:, f * unit : (f + 1) * unit],
                one_sum[:, f * unit : (f + 1) * unit],
            ],
            axis=1,
        )
        store_tile(sum_put, f, line)
    d_hidden_one = jnp.concatenate(
        [
            quarters[part][d // 2][:, (d % 2) * half_rows : (d % 2 + 1) * half_rows]
            for d in range(n_dp)
            for part in range(2)
        ],
        axis=1,
    )
    normed_one, rstd_one = normed(kept)
    d_mod_ref[0:1, :] = column_sums(d_hidden_one)
    d_mod_ref[1:2, :] = column_sums(d_hidden_one * normed_one)

    third = ada_width // 3
    pieces = []
    for row in range(6):
        line = d_mod_ref[row : row + 1, :].astype(low).astype(full)
        pieces += [line[:, step * third : (step + 1) * third] for step in range(n_dp)]
    for f in range(n_fs):
        store_tile(note_put, f, jnp.concatenate(pieces[3 * f : 3 * f + 3], axis=1))
    for mask in range(1, n_fs):
        push(
            sum_put.at[f_at ^ mask],
            sum_got.at[mask],
            send_s.at[mask],
            recv_s.at[mask],
            (d_at, f_at ^ mask),
        )
    for place, (a, b) in enumerate(others):
        push(
            note_put.at[f_at ^ b],
            note_got.at[own_at],
            send_n.at[0, place],
            recv_n.at[0, place],
            (d_at ^ a, f_at ^ b),
        )
    keep_note = pltpu.make_async_copy(note_put.at[f_at], note_got.at[own_at], local.at[4])
    keep_note.start()
    keep_sum = pltpu.make_async_copy(sum_put.at[f_at], sum_got.at[0], local.at[5])
    keep_sum.start()
    arrive(d_att_all.at[2], recv_e.at[2])
    push(d_att_all.at[2], d_att_all.at[3], send_e.at[3], recv_e.at[3], core)
    d_kept = patch_out[:slots, :] + norm_back(
        d_hidden_one * (1.0 + mods[1]), normed_one, rstd_one
    )
    chosen = lax.broadcasted_iota(jnp.int32, (slots, patch_out.shape[0]), 1) == index_ref[...]
    chosen = chosen.astype(full).astype(low)
    left = d_kept
    spread_out = jnp.zeros(patch_out.shape, full)
    for step in range(3):
        part = left.astype(low)
        spread_out = spread_out + rows_rows(chosen, part)
        left = left - part.astype(full)
    patch_out[...] = spread_out
    block_ref[...] = (middle + mods[5] * branch).astype(low)
    fold_wave(0, 0)
    for stay in stays:
        stay.wait()
    for kind in range(2):
        for mask in (2, 3, 1):
            arrive(rows_got.at[kind, mask], recv_p.at[kind, mask])
    for mask in (1, 3):
        arrive(d_att_all.at[mask], recv_e.at[mask])
    grad_proj = rows_rows(
        rows_got[1].reshape(n_dp * slots, row_width),
        d_att_all[...].reshape(n_dp * slots, features),
    ).astype(low)
    for f in range(n_fs):
        for part in range(2):
            grads[
                2,
                f * unit : (f + 1) * unit,
                2 * cols + part * unit : 2 * cols + (part + 1) * unit,
            ] = grad_proj[part * half_rows : (part + 1) * half_rows, f * unit : (f + 1) * unit]

    relay_pair(0)
    grad_pair(0)
    fold_wave(0, 1)

    relay_pair(1)
    grad_pair(1)
    fold_wave(0, 2)
    relay_pair(2)
    grad_pair(2)
    fold_wave(0, 3)
    fold_pair(0)

    keep_mlp = []

    def give_back(kind):
        total = finish(kind).astype(low)
        for d in range(n_dp):
            mlp_put[kind, d] = total[:, d * row_width : (d + 1) * row_width]
        for mask in (2, 3, 1):
            push(
                mlp_put.at[kind, d_at ^ mask],
                mlp_out.at[kind, d_at],
                send_b.at[kind, mask],
                recv_b.at[kind, mask],
                (d_at ^ mask, f_at),
            )
        keep_mlp.append(
            pltpu.make_async_copy(
                mlp_put.at[kind, d_at], mlp_out.at[kind, d_at], local.at[2 + kind]
            )
        )
        keep_mlp[-1].start()

    relay_pair(3)
    grad_pair(3)
    keep_note.wait()
    keep_sum.wait()
    for mask in range(1, n_fs):
        arrive(sum_got.at[mask], recv_s.at[mask])
    for place, (a, b) in enumerate(others):
        at = (d_at ^ a) * n_fs + (f_at ^ b)
        arrive(note_got.at[at], recv_n.at[0, place])
    sums = sum_got[0]
    for mask in range(1, n_fs):
        sums = sums + sum_got[mask]
    notes = note_got[...]
    all_d = jnp.concatenate([notes[:, row, :] for row in range(7)], axis=1)
    totals = column_sums(all_d)
    all_d = all_d.astype(low)
    all_d = all_d[:, :ada_width]
    terms = contract(all_d, ada_ref[...], (1,), (1,))
    sum_line = jnp.concatenate([sums[row : row + 1, :] for row in range(7)], axis=1)
    common = jnp.concatenate(
        [sum_line[:, :ada_width], totals[:, :ada_width], jnp.zeros((1, 32), full)], axis=1
    )
    lines = jnp.concatenate(
        [terms, jnp.broadcast_to(common, (n_dp * n_fs, common.shape[1]))], axis=1
    )
    for row in range(16):
        last_put[:, row, :] = lines[:, row * 128 : (row + 1) * 128]
    for place, (a, b) in enumerate(others):
        push(
            last_put.at[(d_at ^ a) * n_fs + (f_at ^ b)],
            last_got.at[own_at],
            send_n.at[1, place],
            recv_n.at[1, place],
            (d_at ^ a, f_at ^ b),
        )
    keep_last = pltpu.make_async_copy(last_put.at[own_at], last_got.at[own_at], local.at[0])
    keep_last.start()
    fold_pair(1)
    give_back(1)
    fold_pair(2)
    give_back(0)
    ada_out[...] = rows_rows(signal_ref[...], all_d)
    fold_pair(3)
    for kind in (1, 0):
        keep_mlp[1 - kind].wait()
        for mask in (1, 2, 3):
            arrive(mlp_out.at[kind, d_at ^ mask], recv_b.at[kind, mask])
    for d in range(n_dp):
        one_out[:, d * unit : (d + 1) * unit] = mlp_out[0, d].astype(full).T
        for e in range(2):
            start = (e * n_dp + d) * unit
            two_out[:, start : start + unit] = mlp_out[1, d, :, e * unit : (e + 1) * unit].astype(
                full
            )
    total = finish(2)
    for part in range(2):
        rows = slice(part * half_rows, (part + 1) * half_rows)
        qkv_out[rows, :] = total[:, part * cols : (part + 1) * cols]
        start = 2 * cols + part * unit
        proj_out[:, rows] = total[:, start : start + unit].T
    keep_last.wait()
    for place, (a, b) in enumerate(others):
        at = (d_at ^ a) * n_fs + (f_at ^ b)
        arrive(last_got.at[at], recv_n.at[1, place])
    for copy in sent:
        if not any(copy is gone for gone in leaving):
            copy.wait_send()


def backward_kernel(forward, ada, index, patches, cot, count):
    (
        qkv_all,
        one_all,
        two_all,
        projected,
        hidden_all,
        branch_all,
        proj_dense,
        attended,
        hidden_rows,
        mixed_rows,
        mods,
        bias,
        signals,
        kept,
    ) = forward
    n_dp, n_fs = lax.axis_size("dp"), lax.axis_size("fsdp")
    n_all = n_dp * n_fs
    slots, features = kept.shape
    row_width = features // n_dp
    unit = features // n_fs
    ada_width = 6 * features // n_fs
    cols = projected.shape[2]
    low, full = jnp.bfloat16, jnp.float32
    vmem = pl.BlockSpec(memory_space=pltpu.VMEM)
    anywhere = pl.BlockSpec(memory_space=pl.ANY)
    image = (slots, features)
    shapes = [
        (image, low),
        (patches, full),
        ((row_width, cols), full),
        ((unit, row_width), full),
        ((row_width, n_dp * unit), full),
        ((unit, features), full),
        ((row_width, ada_width), full),
        ((n_all, 16, 128), full),
    ]
    scratch = [
        ((2, n_dp, unit, row_width), low),
        (one_all.shape, low),
        (two_all.shape, low),
        (projected.shape, low),
        ((n_dp,) + image, low),
        ((n_dp,) + image, low),
        (proj_dense.shape, low),
        ((n_dp,) + image, low),
        ((n_dp,) + image, low),
        ((n_dp,) + image, low),
        ((2, 2) + image, low),
        ((2,) + image, low),
        ((2,) + image, low),
        ((3, features, features), low),
        ((3, 4, unit, features), low),
        ((3, 3, unit, features), low),
        ((2, n_dp, slots, row_width), low),
        ((n_dp,) + image, low),
        (image, low),
        ((n_dp, n_fs // 2, slots, 2 * cols), low),
        ((2, qkv_all.shape[1] // 2, qkv_all.shape[2]), low),
        ((2, n_dp, unit, row_width), low),
        ((8, features), full),
        ((n_fs, 8, 128), full),
        ((n_fs, 8, 128), full),
        ((n_fs, 8, 128), full),
        ((n_all, 8, 128), full),
        ((n_all, 16, 128), full),
    ]
    dma = pltpu.SemaphoreType.DMA
    sems = [(3, 7), (2, 3), (4,), (2 + n_fs // 2, 4), (2, n_all - 1), (n_fs,), (2, 4)]
    return pl.pallas_call(
        functools.partial(backward_body, (HEADS, features // HEADS, ada_width)),
        out_shape=[jax.ShapeDtypeStruct(shape, kind) for shape, kind in shapes],
        in_specs=[anywhere] * 9
        + [vmem] * 8
        + [pl.BlockSpec(memory_space=pltpu.SMEM)],
        out_specs=[vmem] * len(shapes),
        scratch_shapes=[pltpu.VMEM(shape, kind) for shape, kind in scratch]
        + [dma(shape) for shape in sems for side in range(2)]
        + [dma((6,)), dma((6,))],
        compiler_params=pltpu.CompilerParams(
            collective_id=6, has_side_effects=True, vmem_limit_bytes=64 * 1024 * 1024 - 65536
        ),
        name="backward",
    )(
        qkv_all,
        one_all,
        two_all,
        projected,
        hidden_all,
        branch_all,
        proj_dense,
        hidden_rows,
        mixed_rows,
        ada,
        signals,
        attended,
        kept,
        mods,
        bias,
        index,
        cot,
        count,
    )


def shards(
    patches_in,
    condition,
    keep_count,
    keep_index,
    w_ada,
    b_ada,
    w_qkv,
    qv_bias,
    w_proj,
    w_fc1,
    fc1_bias,
    w_fc2,
    out_bias,
    cotangent,
):
    n_dp, n_fs = lax.axis_size("dp"), lax.axis_size("fsdp")
    n_all = n_dp * n_fs
    d_at, f_at = lax.axis_index("dp"), lax.axis_index("fsdp")
    features = patches_in.shape[2]
    row_width = features // n_dp
    half_rows = row_width // 2
    low = jnp.bfloat16
    full = jnp.float32

    cond_float = condition.astype(full)
    signal = swish(cond_float).astype(low).astype(full)
    shards_bias = [b_ada, qv_bias, fc1_bias, out_bias]
    biases = jnp.concatenate(shards_bias).astype(full)
    notes = jnp.concatenate(
        [
            jnp.pad(signal.reshape(n_dp, row_width), ((0, 0), (0, 384 - row_width))),
            jnp.broadcast_to(jnp.pad(biases, (0, 640 - biases.shape[0])), (n_dp, 640)),
        ],
        axis=1,
    ).reshape(n_dp, 8, 128)
    ada_width = w_ada.shape[1]
    unit_width = w_fc1.shape[1] // n_dp
    index = keep_index.reshape(-1, 1)
    patches = patches_in.reshape(patches_in.shape[1:])
    upstream = cotangent.reshape(cotangent.shape[1:])
    forward = forward_kernel(
        notes,
        w_ada,
        w_fc1,
        w_fc2.T,
        w_qkv,
        w_proj.T,
        patches,
        index,
        upstream,
        keep_count,
        (ada_width, qv_bias.shape[0], fc1_bias.shape[0], out_bias.shape[0]),
    )
    block_out, grad_patches, qkv_out, proj_out, one_out, two_out, grad_ada, last = (
        backward_kernel(forward, w_ada, index, patches.shape, upstream, keep_count)
    )
    qkv_cols, proj_cols = w_qkv.shape[1], w_proj.shape[1]

    groups = last[:, :3, :].reshape(n_dp, n_fs, 3, 128).sum(axis=1)
    d_signal = groups.reshape(n_dp, 384)[:, :row_width].reshape(1, features)
    unused, swish_pull = jax.vjp(swish, cond_float)
    grad_condition = swish_pull(d_signal)[0]
    own = d_at * n_fs + f_at
    head_size = qv_bias.shape[0]
    heads_per = qkv_cols // head_size

    def line_of(kind, d, f):
        source = lax.dynamic_slice_in_dim(last, d * n_fs + f, 1, 0).reshape(-1)
        start = row_width + kind * ada_width
        return source[start : start + ada_width]

    def summed(f):
        return sum(line_of(0, d, f) for d in range(n_dp))

    ada_count = b_ada.shape[0]
    ada_bias = lax.dynamic_slice_in_dim(
        line_of(1, d_at, own // n_dp), (own % n_dp) * ada_count, ada_count
    )
    block = jnp.where(own < HEADS, own, own + HEADS)
    qv_out = lax.dynamic_slice_in_dim(
        summed(block // heads_per), (block % heads_per) * head_size, head_size
    )
    per = proj_cols // head_size
    place = own % HEADS
    start = jnp.where(own < HEADS, qkv_cols, qkv_cols + proj_cols) + (place % per) * head_size
    out_out = lax.dynamic_slice_in_dim(summed(place // per), start, head_size)
    bias_out = lax.dynamic_slice_in_dim(
        line_of(0, own % n_dp, own // n_dp), qkv_cols + 2 * proj_cols, unit_width
    )
    return (
        block_out[None],
        grad_patches[None],
        grad_condition,
        grad_ada,
        ada_bias,
        qkv_out,
        qv_out,
        proj_out.T,
        one_out,
        bias_out,
        two_out.T,
        out_out,
    )


def kernels_fit(*arrays):
    w_qkv, w_fc1 = arrays[6], arrays[9]
    features = arrays[0].shape[2]
    unit_width = w_fc1.shape[1] // lax.axis_size("dp")
    return (
        w_qkv.shape[1] % (features // HEADS) == 0
        and w_qkv.shape[0] % 16 == 0
        and unit_width % 16 == 0
        and unit_width == arrays[11].shape[1]
        and lax.axis_size("dp") == 4
        and lax.axis_size("fsdp") == 8
    )


def solution(mesh):
    both = ("dp", "fsdp")
    weight = P("dp", "fsdp")
    flat = P(both)
    placed = (
        P(both, None, None),
        P(both, None),
        flat,
        P(both, None),
        weight,
        flat,
        weight,
        flat,
        weight,
        weight,
        flat,
        weight,
        flat,
        P(both, None, None),
    )

    def chosen(*arrays):
        return (shards if kernels_fit(*arrays) else plain_shards)(*arrays)

    return jax.shard_map(
        chosen,
        mesh=mesh,
        in_specs=placed,
        out_specs=(
            P(both, None, None),
            P(both, None, None),
            P(both, None),
            weight,
            flat,
            weight,
            flat,
            weight,
            weight,
            flat,
            weight,
            flat,
        ),
        check_vma=False,
    )
```

```python
import functools
import math

import jax
import jax.numpy as jnp
from jax import lax
from jax.experimental import pallas as pl
from jax.experimental.pallas import tpu as pltpu
from jax.sharding import PartitionSpec as P

HEADS = 16


epsilon = 1e-06
negative = -1e30


def layer_norm(inputs):
    centred = inputs - jnp.mean(inputs, axis=-1, keepdims=True)
    rstd = lax.rsqrt(jnp.mean(centred * centred, axis=-1, keepdims=True) + epsilon)
    return (centred * rstd, rstd)


def norm_back(upstream, normed, rstd):
    return rstd * (
        upstream
        - jnp.mean(upstream, axis=-1, keepdims=True)
        - normed * jnp.mean(upstream * normed, axis=-1, keepdims=True)
    )


def swish(inputs):
    return inputs / (1.0 + jnp.exp(-inputs))


def gelu_tanh(inputs):
    return (
        0.5
        * inputs
        * (1.0 + jnp.tanh(0.7978845608028654 * (inputs + 0.044715 * inputs * inputs * inputs)))
    )


def contract(left, right, left_dims, right_dims):
    return lax.dot_general(
        left, right, ((left_dims, right_dims), ((), ())), preferred_element_type=jnp.float32
    )


def rows_rows(left, right):
    return contract(left, right, (0,), (0,))


def times_transposed(left, right):
    return contract(left, right, (1,), (1,))


def inner_rows(left, right):
    return lax.dot_general(
        left, right, (((0,), (0,)), ((), ())), preferred_element_type=jnp.float32
    )


def flat_bias(collected):
    return collected.reshape(-1)


def gather_forward(w_ada, b_ada, w_qkv, qv_bias, w_proj, w_fc1, fc1_bias, w_fc2, out_bias):
    part_ada, part_qkv, part_proj, part_one, part_two, bias_ada, bias_qv, bias_one, bias_out = (
        lax.all_gather(w_ada, "fsdp", axis=1, tiled=True),
        lax.all_gather(w_qkv, "fsdp", axis=1, tiled=True),
        lax.all_gather(w_proj, "fsdp", axis=1, tiled=True),
        lax.all_gather(w_fc1, "fsdp", axis=1, tiled=True),
        lax.all_gather(w_fc2, "fsdp", axis=1, tiled=True),
        lax.all_gather(b_ada.reshape(1, 1, -1), "fsdp", axis=1, tiled=True),
        lax.all_gather(qv_bias.reshape(1, 1, -1), "fsdp", axis=1, tiled=True),
        lax.all_gather(fc1_bias.reshape(1, 1, -1), "fsdp", axis=1, tiled=True),
        lax.all_gather(out_bias.reshape(1, 1, -1), "fsdp", axis=1, tiled=True),
    )
    gathered = (
        lax.all_gather(part_ada, "dp", axis=0, tiled=True),
        lax.all_gather(part_qkv, "dp", axis=0, tiled=True),
        lax.all_gather(part_proj, "dp", axis=0, tiled=True),
        lax.all_gather(part_one, "dp", axis=0, tiled=True),
        lax.all_gather(part_two, "dp", axis=0, tiled=True),
        lax.all_gather(bias_ada, "dp", axis=0, tiled=True),
        lax.all_gather(bias_qv, "dp", axis=0, tiled=True),
        lax.all_gather(bias_one, "dp", axis=0, tiled=True),
        lax.all_gather(bias_out, "dp", axis=0, tiled=True),
    )
    return (
        gathered[0],
        flat_bias(gathered[5]),
        gathered[1],
        flat_bias(gathered[6]),
        gathered[2],
        gathered[3],
        flat_bias(gathered[7]),
        gathered[4],
        flat_bias(gathered[8]),
    )


def gather_backward(w_ada, w_qkv, w_proj, w_fc1, w_fc2):
    part_ada, part_qkv, part_proj, part_one, part_two = (
        lax.all_gather(w_ada, "fsdp", axis=1, tiled=True),
        lax.all_gather(w_qkv, "fsdp", axis=1, tiled=True),
        lax.all_gather(w_proj, "fsdp", axis=1, tiled=True),
        lax.all_gather(w_fc1, "fsdp", axis=1, tiled=True),
        lax.all_gather(w_fc2, "fsdp", axis=1, tiled=True),
    )
    return (
        lax.all_gather(part_ada, "dp", axis=0, tiled=True),
        lax.all_gather(part_qkv, "dp", axis=0, tiled=True),
        lax.all_gather(part_proj, "dp", axis=0, tiled=True),
        lax.all_gather(part_one, "dp", axis=0, tiled=True),
        lax.all_gather(part_two, "dp", axis=0, tiled=True),
    )


def split_bias(term):
    return term.reshape(lax.axis_size("dp"), lax.axis_size("fsdp"), -1)


def own_bias(summed):
    return lax.dynamic_index_in_dim(summed, lax.axis_index("dp"), 0, keepdims=False).reshape(-1)


def owned_columns(matrix, width):
    return lax.dynamic_slice_in_dim(matrix, lax.axis_index("dp") * width, width, 1)


def column_totals(matrix):
    return jnp.sum(matrix.astype(jnp.float32), axis=0)


def plain_shards(
    patches_in,
    condition,
    keep_count,
    keep_index,
    w_ada,
    b_ada,
    w_qkv,
    qv_bias,
    w_proj,
    w_fc1,
    fc1_bias,
    w_fc2,
    out_bias,
    cotangent,
):
    images, kept_slots = keep_index.shape
    features = patches_in.shape[2]
    hidden_units = w_fc2.shape[0] * lax.axis_size("dp")
    all_rows = images * kept_slots
    head_size = features // HEADS
    factor = 1.0 / math.sqrt(head_size)
    head_shape = (images, kept_slots, HEADS, head_size)
    row_width = features // lax.axis_size("dp")
    unit_width = hidden_units // lax.axis_size("dp")
    ada_full, ada_bias, qkv_full, qv_full, proj_full, one_full, one_bias, two_full, out_full = (
        gather_forward(w_ada, b_ada, w_qkv, qv_bias, w_proj, w_fc1, fc1_bias, w_fc2, out_bias)
    )
    inputs = patches_in.astype(jnp.float32)
    kept_in = jnp.take_along_axis(inputs, keep_index[:, :, None], axis=1)
    allowed = (jnp.arange(kept_slots)[None, :] < keep_count[:, None])[:, None, None, :]
    cond_float = condition.astype(jnp.float32)
    signal = swish(cond_float).astype(jnp.bfloat16)
    modulation = jnp.dot(signal, ada_full, preferred_element_type=jnp.float32) + ada_bias.astype(
        jnp.float32
    )
    shift_one, scale_one, gate_one, shift_two, scale_two, gate_two = [
        modulation[:, None, column * features : (column + 1) * features] for column in range(6)
    ]
    normed_one, rstd_one = layer_norm(kept_in)
    hidden_one = (
        (normed_one * (1.0 + scale_one) + shift_one)
        .astype(jnp.bfloat16)
        .reshape(all_rows, features)
    )
    qv_float = qv_full.astype(jnp.float32)
    qkv_bias = jnp.concatenate(
        [qv_float[:features], jnp.zeros((features,), jnp.float32), qv_float[features:]]
    )
    projected = (
        jnp.dot(hidden_one, qkv_full, preferred_element_type=jnp.float32) + qkv_bias
    ).astype(jnp.bfloat16)
    queries = projected[:, :features].reshape(head_shape)
    key_rows = projected[:, features : 2 * features].reshape(head_shape)
    values = projected[:, 2 * features :].reshape(head_shape)
    scores = (
        jnp.einsum("iqhe,ikhe->ihqk", queries, key_rows, preferred_element_type=jnp.float32)
        * factor
    )
    scores = jnp.where(allowed, scores, negative)
    top_score = jnp.max(scores, axis=-1, keepdims=True)
    exponent = jnp.exp(scores - top_score)
    row_total = jnp.sum(exponent, axis=-1, keepdims=True)
    log_total = top_score + jnp.log(row_total)
    softmax_low = (exponent / row_total).astype(jnp.bfloat16)
    mixed = jnp.einsum("ihqk,ikhe->iqhe", softmax_low, values, preferred_element_type=jnp.float32)
    mixed_low = mixed.reshape(all_rows, features).astype(jnp.bfloat16)
    out_float = out_full.astype(jnp.float32)
    attended = (
        jnp.dot(mixed_low, proj_full, preferred_element_type=jnp.float32) + out_float[:features]
    ).reshape(images, kept_slots, features)
    middle = kept_in + gate_one * attended
    normed_two, rstd_two = layer_norm(middle)
    hidden_two = (
        (normed_two * (1.0 + scale_two) + shift_two)
        .astype(jnp.bfloat16)
        .reshape(all_rows, features)
    )
    raised = jnp.dot(hidden_two, one_full, preferred_element_type=jnp.float32) + one_bias.astype(
        jnp.float32
    )
    activated = gelu_tanh(raised).astype(jnp.bfloat16)
    branch = (
        jnp.dot(activated, two_full, preferred_element_type=jnp.float32) + out_float[features:]
    ).reshape(images, kept_slots, features)
    block_out = (middle + gate_two * branch).astype(jnp.bfloat16)
    ada_back, qkv_back, proj_back, one_back, two_back = gather_backward(
        w_ada, w_qkv, w_proj, w_fc1, w_fc2
    )
    upstream = cotangent.astype(jnp.float32)
    d_gate_two = jnp.sum(upstream * branch, axis=1)
    d_branch = (gate_two * upstream).reshape(all_rows, features).astype(jnp.bfloat16)
    d_activated = times_transposed(d_branch, two_back)
    unused, gelu_pull = jax.vjp(gelu_tanh, raised)
    d_raised = gelu_pull(d_activated)[0].astype(jnp.bfloat16)
    d_hidden_two = times_transposed(d_raised, one_back).reshape(images, kept_slots, features)
    d_shift_two = jnp.sum(d_hidden_two, axis=1)
    d_scale_two = jnp.sum(d_hidden_two * normed_two, axis=1)
    d_middle = upstream + norm_back(d_hidden_two * (1.0 + scale_two), normed_two, rstd_two)
    d_gate_one = jnp.sum(d_middle * attended, axis=1)
    d_attended = (gate_one * d_middle).reshape(all_rows, features).astype(jnp.bfloat16)
    d_mixed = times_transposed(d_attended, proj_back).astype(jnp.bfloat16).reshape(head_shape)
    scores_again = (
        jnp.einsum("iqhe,ikhe->ihqk", queries, key_rows, preferred_element_type=jnp.float32)
        * factor
    )
    scores_again = jnp.where(allowed, scores_again, negative)
    softmax_again = jnp.exp(scores_again - log_total)
    d_softmax = jnp.einsum("iqhe,ikhe->ihqk", d_mixed, values, preferred_element_type=jnp.float32)
    row_delta = jnp.sum(d_softmax * softmax_again, axis=-1, keepdims=True)
    d_scores = (softmax_again * (d_softmax - row_delta)).astype(jnp.bfloat16)
    d_queries = (
        jnp.einsum("ihqk,ikhe->iqhe", d_scores, key_rows, preferred_element_type=jnp.float32)
        * factor
    )
    d_keys = (
        jnp.einsum("ihqk,iqhe->ikhe", d_scores, queries, preferred_element_type=jnp.float32)
        * factor
    )
    d_values = jnp.einsum(
        "ihqk,iqhe->ikhe",
        softmax_again.astype(jnp.bfloat16),
        d_mixed,
        preferred_element_type=jnp.float32,
    )
    d_projected = jnp.concatenate(
        [
            d_queries.reshape(all_rows, features),
            d_keys.reshape(all_rows, features),
            d_values.reshape(all_rows, features),
        ],
        axis=1,
    ).astype(jnp.bfloat16)
    d_hidden_one = times_transposed(d_projected, qkv_back).reshape(images, kept_slots, features)
    d_shift_one = jnp.sum(d_hidden_one, axis=1)
    d_scale_one = jnp.sum(d_hidden_one * normed_one, axis=1)
    d_kept = d_middle + norm_back(d_hidden_one * (1.0 + scale_one), normed_one, rstd_one)
    grad_patches = jnp.zeros_like(inputs).at[jnp.arange(images)[:, None], keep_index].add(d_kept)
    d_modulation = jnp.concatenate(
        [d_shift_one, d_scale_one, d_gate_one, d_shift_two, d_scale_two, d_gate_two], axis=1
    ).astype(jnp.bfloat16)
    d_signal = times_transposed(d_modulation, ada_back)
    unused_too, swish_pull = jax.vjp(swish, cond_float)
    grad_condition = swish_pull(d_signal)[0]
    piece_one = lax.all_gather(hidden_one, "dp", axis=0, tiled=True)
    piece_proj_d = lax.all_gather(d_projected, "dp", axis=0, tiled=True)
    piece_mixed = lax.all_gather(mixed_low, "dp", axis=0, tiled=True)
    piece_att_d = lax.all_gather(d_attended, "dp", axis=0, tiled=True)
    piece_two = lax.all_gather(hidden_two, "dp", axis=0, tiled=True)
    piece_raised_d = lax.all_gather(d_raised, "dp", axis=0, tiled=True)
    piece_act = lax.all_gather(activated, "dp", axis=0, tiled=True)
    piece_branch_d = lax.all_gather(d_branch, "dp", axis=0, tiled=True)
    grad_qkv = inner_rows(owned_columns(piece_one, row_width), piece_proj_d)
    grad_proj = inner_rows(owned_columns(piece_mixed, row_width), piece_att_d)
    grad_one = inner_rows(owned_columns(piece_two, row_width), piece_raised_d)
    grad_two = inner_rows(owned_columns(piece_act, unit_width), piece_branch_d)
    qkv_sums = column_totals(piece_proj_d)
    proj_sums = column_totals(piece_att_d)
    one_sums = column_totals(piece_raised_d)
    two_sums = column_totals(piece_branch_d)
    piece_signal = lax.all_gather(signal, "dp", axis=0, tiled=True)
    piece_mod_d = lax.all_gather(d_modulation, "dp", axis=0, tiled=True)
    grad_ada = inner_rows(owned_columns(piece_signal, row_width), piece_mod_d)
    ada_sums = column_totals(piece_mod_d)
    grad_qv = jnp.concatenate([qkv_sums[:features], qkv_sums[2 * features :]])
    grad_out = jnp.concatenate([proj_sums, two_sums])
    terms = (
        grad_ada,
        grad_qkv,
        grad_proj,
        grad_one,
        grad_two,
        split_bias(ada_sums),
        split_bias(grad_qv),
        split_bias(one_sums),
        split_bias(grad_out),
    )
    (
        final_ada,
        final_qkv,
        final_proj,
        final_one,
        final_two,
        final_ada_bias,
        final_qv,
        final_bias,
        final_out,
    ) = (
        lax.psum_scatter(
            terms[0].astype(jnp.bfloat16), "fsdp", scatter_dimension=1, tiled=True
        ).astype(jnp.float32),
        lax.psum_scatter(
            terms[1].astype(jnp.bfloat16), "fsdp", scatter_dimension=1, tiled=True
        ).astype(jnp.float32),
        lax.psum_scatter(
            terms[2].astype(jnp.bfloat16), "fsdp", scatter_dimension=1, tiled=True
        ).astype(jnp.float32),
        lax.psum_scatter(
            terms[3].astype(jnp.bfloat16), "fsdp", scatter_dimension=1, tiled=True
        ).astype(jnp.float32),
        lax.psum_scatter(
            terms[4].astype(jnp.bfloat16), "fsdp", scatter_dimension=1, tiled=True
        ).astype(jnp.float32),
        lax.psum_scatter(
            terms[5].astype(jnp.bfloat16), "fsdp", scatter_dimension=1, tiled=True
        ).astype(jnp.float32),
        lax.psum_scatter(
            terms[6].astype(jnp.bfloat16), "fsdp", scatter_dimension=1, tiled=True
        ).astype(jnp.float32),
        lax.psum_scatter(
            terms[7].astype(jnp.bfloat16), "fsdp", scatter_dimension=1, tiled=True
        ).astype(jnp.float32),
        lax.psum_scatter(
            terms[8].astype(jnp.bfloat16), "fsdp", scatter_dimension=1, tiled=True
        ).astype(jnp.float32),
    )
    return (
        block_out,
        grad_patches,
        grad_condition,
        final_ada,
        own_bias(final_ada_bias),
        final_qkv,
        own_bias(final_qv),
        final_proj,
        final_one,
        own_bias(final_bias),
        final_two,
        own_bias(final_out),
    )


MESH = pl.DeviceIdType.MESH


def remote(source, target, send, recv, device):
    return pltpu.make_async_remote_copy(
        src_ref=source,
        dst_ref=target,
        send_sem=send,
        recv_sem=recv,
        device_id=device,
        device_id_type=MESH,
    )


def greet(devices):
    barrier = pltpu.get_barrier_semaphore()
    for device in devices:
        pl.semaphore_signal(barrier, 1, device_id=device, device_id_type=MESH)
    pl.semaphore_wait(barrier, len(devices))


def normed(value):
    centred = value - jnp.mean(value, axis=-1, keepdims=True)
    rstd = lax.rsqrt(jnp.mean(centred * centred, axis=-1, keepdims=True) + epsilon)
    return centred * rstd, rstd


def forward_body(
    sizes,
    note_ref,
    ada_ref,
    one_raw,
    two_raw,
    qkv_raw,
    proj_raw,
    patch_ref,
    index_ref,
    cot_ref,
    count_ref,
    qkv_hbm,
    one_hbm,
    two_hbm,
    projected_hbm,
    hidden_hbm,
    branch_hbm,
    proj_hbm,
    attended_ref,
    hidden_rows,
    mixed_rows,
    mod_ref,
    bias_ref,
    signal_ref,
    kept_ref,
    att_all,
    one_all,
    two_all,
    projected_ref,
    hidden_all,
    branch_all,
    proj_dense,
    mixed_ref,
    piece_got,
    one_block,
    two_block,
    note_got,
    row_put,
    row_got,
    att_ref,
    piece_ref,
    send_n,
    recv_n,
    send_z,
    send_y,
    send_x,
    recv_w,
    send_e,
    recv_e,
    local,
    out_sem,
):
    heads, size, widths = sizes
    n_dp, n_fs = 4, 8
    d_at, f_at = lax.axis_index("dp"), lax.axis_index("fsdp")
    own_at = d_at * n_fs + f_at
    slots, features = kept_ref.shape
    half_rows, cols = att_ref.shape[0], qkv_raw.shape[1]
    unit = one_block.shape[0]
    row_width = 2 * half_rows
    width = proj_raw.shape[0]
    low = jnp.bfloat16
    full = jnp.float32
    others = [(a, b) for a in range(n_dp) for b in range(n_fs) if a or b]
    barrier = pltpu.get_barrier_semaphore()
    for a, b in others:
        pl.semaphore_signal(
            barrier, 1, device_id=(d_at ^ a, f_at ^ b), device_id_type=MESH
        )
    for part in range(2):
        rows = slice(part * half_rows, (part + 1) * half_rows)
        att_ref[:, part * cols : (part + 1) * cols] = qkv_raw[rows, :]
        start = 2 * cols + part * width
        att_ref[:, start : start + width] = proj_raw[:, rows].T
    pl.semaphore_wait(barrier, len(others))

    own_blocks = (att_ref, one_block, two_block)
    gathered = (att_all, one_all, two_all)
    started = []
    middle_copies = []
    stores = []
    z_at = f_at // 2
    in_middle = (z_at == 1) | (z_at == 2)
    second = jnp.where(in_middle, 6, 4)
    third = 10 - second

    def store(source, target):
        copy = pltpu.make_async_copy(source, target, out_sem.at[len(stores)])
        copy.start()
        stores.append(copy)

    def slot(array, a, b):
        if array == 0:
            start = pl.multiple_of((d_at ^ a) * half_rows, 16)
            return gathered[array].at[f_at ^ b, pl.ds(start, half_rows), :]
        start = pl.multiple_of((f_at ^ b) * unit, 16)
        return gathered[array].at[pl.ds(start, unit), :]

    def push(source, target, send, recv, device):
        copy = remote(source, target, send, recv, device)
        copy.start()
        started.append(copy)

    def block(array, a, b):
        own = isinstance(b, int) and a == 0 and b == 0
        return own_blocks[array] if own else slot(array, a, b)

    def pass_on(array, a, b, axis, mask, sem):
        device = (d_at ^ mask, f_at) if axis == 0 else (d_at, f_at ^ mask)
        to_a, to_b = (a ^ mask, b) if axis == 0 else (a, b ^ mask)
        push(block(array, a, b), slot(array, a, b), sem, recv_w.at[array, to_a, to_b], device)

    def relay_middle(array, b, mask, place):
        copy = remote(
            block(array, 0, b),
            slot(array, 0, b),
            send_z.at[array, place],
            recv_w.at[array, 0, b ^ mask],
            (d_at, f_at ^ mask),
        )

        @pl.when(in_middle)
        def _():
            copy.start()

        middle_copies.append(copy)

    def arrive(array, a, b):
        place = slot(array, a, b)
        pltpu.make_async_copy(place, place, recv_w.at[array, a, b]).wait()

    def near(array, b, place):
        pass_on(array, 0, b, 1, 1, send_y.at[array, place])

    def onward(array, a, b, place):
        if a == 0:
            pass_on(array, a, b, 0, 2, send_x.at[array, 0, place])
        pass_on(array, a, b, 0, 1, send_x.at[array, 1 + a // 2, place])

    order = [0, 1, 2, second, 3, third, second ^ 1, third ^ 1]

    def begin(array):
        near(array, 0, 0)
        if array == 0:
            onward(array, 0, 0, 0)
        pass_on(array, 0, 0, 1, 2, send_z.at[array, 0])
        relay_middle(array, 0, 6, 1)

    def follow(array, step):
        arrive(array, 0, order[step])
        if step == 2:
            relay_middle(array, 2, 6, 2)
            near(array, 2, 1)
        if step == 3:
            relay_middle(array, 6, 2, 3)
            near(array, second, 2)
        if step == 5:
            relay_middle(array, 4, 2, 4)
            near(array, third, 3)
        if array == 0:
            onward(array, 0, order[step], step)

    begin(0)
    for place, (a, b) in enumerate(others):
        push(
            note_ref.at[d_at ^ a],
            note_got.at[own_at],
            send_n.at[0, place],
            recv_n.at[0, place],
            (d_at ^ a, f_at ^ b),
        )
    for d in range(n_dp):
        piece_ref[d, :, :row_width] = one_raw[:, d * unit : (d + 1) * unit].T
        for e in range(2):
            start = (e * n_dp + d) * unit
            piece_ref[d, :, row_width + e * unit : row_width + (e + 1) * unit] = two_raw[
                :, start : start + unit
            ]
    stays = [
        pltpu.make_async_copy(note_ref.at[d_at], note_got.at[own_at], local.at[0]),
        pltpu.make_async_copy(att_ref, slot(0, 0, 0), local.at[1]),
        pltpu.make_async_copy(piece_ref.at[d_at], piece_got.at[d_at], local.at[3]),
    ]
    for stay in stays:
        stay.start()
    chosen = lax.broadcasted_iota(jnp.int32, (patch_ref.shape[0], slots), 0) == index_ref[...]
    kept_ref[...] = rows_rows(chosen.astype(full).astype(low), patch_ref[...])
    kept = kept_ref[...]
    normed_one, _ = normed(kept)
    follow(0, 1)
    follow(0, 2)
    for mask in (1, 2, 3):
        push(
            piece_ref.at[d_at ^ mask],
            piece_got.at[d_at],
            send_e.at[2, mask],
            recv_e.at[2, mask],
            (d_at ^ mask, f_at),
        )

    stays[0].wait()
    for place, (a, b) in enumerate(others):
        at = (d_at ^ a) * n_fs + (f_at ^ b)
        pltpu.make_async_copy(note_got.at[at], note_got.at[at], recv_n.at[0, place]).wait()
    notes = note_got[...]
    signals = jnp.concatenate([notes[:, row, :] for row in range(3)], axis=1).astype(low)
    signals = signals[:, :row_width]
    signal_ref[...] = signals
    terms = jnp.dot(signals, ada_ref[...], preferred_element_type=full)
    ada_width = widths[0]
    ada_piece = ada_width * n_fs // (n_dp * n_fs)

    def bias_piece(index, start, count):
        row = note_got[index]
        line = jnp.concatenate([row[3 + step : 4 + step, :] for step in range(5)], axis=1)
        return line[:, start : start + count]

    block_bias = jnp.concatenate(
        [bias_piece(f_at * n_dp + step, 0, ada_piece) for step in range(n_dp)], axis=1
    )
    first = (d_at == 0).astype(full)
    for row in range(7):
        count = min(128, ada_width - row * 128)
        span = slice(row * 128, row * 128 + count)
        piece = terms[:, span] + block_bias[:, span] * first
        if count < 128:
            piece = jnp.concatenate(
                [piece, jnp.zeros((piece.shape[0], 128 - count), full)], axis=1
            )
        row_put[:, row, :] = piece
    for place, (a, b) in enumerate(others):
        push(
            row_put.at[(d_at ^ a) * n_fs + (f_at ^ b)],
            row_got.at[own_at],
            send_n.at[1, place],
            recv_n.at[1, place],
            (d_at ^ a, f_at ^ b),
        )
    keep_row = pltpu.make_async_copy(row_put.at[own_at], row_got.at[own_at], local.at[0])
    keep_row.start()

    follow(0, 3)
    follow(0, 4)
    follow(0, 5)

    stays[2].wait()
    for mask in (1, 2, 3):
        place = piece_got.at[d_at ^ mask]
        pltpu.make_async_copy(place, place, recv_e.at[2, mask]).wait()
    one_block[...] = jnp.concatenate([piece_got[d, :, :row_width] for d in range(n_dp)], axis=1)
    two_block[...] = jnp.concatenate([piece_got[d, :, row_width:] for d in range(n_dp)], axis=1)
    follow(0, 6)
    follow(0, 7)
    begin(1)
    begin(2)
    keep_one = pltpu.make_async_copy(one_block, slot(1, 0, 0), local.at[3])
    keep_one.start()
    keep_two = pltpu.make_async_copy(two_block, slot(2, 0, 0), local.at[4])
    keep_two.start()

    qv_width, one_width, out_width = widths[1:]
    starts = [ada_piece, ada_piece + qv_width, ada_piece + qv_width + one_width]
    lines = []
    for index in range(n_dp * n_fs):
        lines.append(
            (
                bias_piece(index, starts[0], qv_width),
                bias_piece(index, starts[2], out_width),
            )
        )
    heads_per = cols // size
    for f in range(n_fs):
        parts = []
        for j in range(heads_per):
            head = f * heads_per + j
            if head < heads:
                parts.append(lines[head][0])
            elif head < 2 * heads:
                parts.append(jnp.zeros((1, size), full))
            else:
                parts.append(lines[head - heads][0])
        bias_ref[f : f + 1, :cols] = jnp.concatenate(parts, axis=1)
    bias_ref[8:9, :] = jnp.concatenate([line[1] for line in lines[:heads]], axis=1)
    bias_ref[9:10, :] = jnp.concatenate([line[1] for line in lines[heads:]], axis=1)
    bias_ref[10:11, :] = jnp.concatenate(
        [bias_piece(f * n_dp + d_at, starts[1], one_width) for f in range(n_fs)], axis=1
    )

    keep_row.wait()
    for place, (a, b) in enumerate(others):
        at = (d_at ^ a) * n_fs + (f_at ^ b)
        pltpu.make_async_copy(row_got.at[at], row_got.at[at], recv_n.at[1, place]).wait()
    sums = row_got[0:n_fs]
    for d in range(1, n_dp):
        sums = sums + row_got[d * n_fs : (d + 1) * n_fs]
    sums = jnp.concatenate([sums[:, row, :] for row in range(7)], axis=1)
    pieces = []
    for index in range(6 * n_dp):
        f, part = index // 3, index % 3
        pieces.append(sums[f : f + 1, part * row_width : (part + 1) * row_width])
    mods = []
    for row in range(6):
        mods.append(jnp.concatenate(pieces[row * n_dp : (row + 1) * n_dp], axis=1))
        mod_ref[row : row + 1, :] = mods[row]
    hidden_one = (normed_one * (1.0 + mods[1]) + mods[0]).astype(low)
    branch_all[0] = (mods[5] * cot_ref[...].astype(full)).astype(low)
    chunks = [
        hidden_one[:, place * half_rows : (place + 1) * half_rows] for place in range(2 * n_dp)
    ]
    for d in range(n_dp):
        hidden_rows[d] = jnp.concatenate(chunks[2 * d : 2 * d + 2], axis=1)
    halves = [jnp.concatenate(chunks[part::2], axis=1) for part in range(2)]

    def spread_step(buffer, kind, mask):
        for key in [0] if mask == 2 else [0, 2]:
            push(
                buffer.at[key],
                buffer.at[key ^ mask],
                send_e.at[kind, key ^ mask],
                recv_e.at[kind, key ^ mask],
                (d_at ^ mask, f_at),
            )

    def spread_wait(buffer, kind, keys):
        for key in keys:
            place = buffer.at[key]
            pltpu.make_async_copy(place, place, recv_e.at[kind, key]).wait()

    store(branch_all.at[0], branch_hbm.at[0])
    spread_step(branch_all, 0, 2)

    stays[1].wait()
    for step, b in enumerate(order):
        arrive(0, 2, b)
        onward(0, 2, b, step)
        arrive(0, 1, b)
        arrive(0, 3, b)
        f = f_at ^ b
        out = jnp.dot(halves[0], att_all[f, :, :cols], preferred_element_type=full)
        out = out + jnp.dot(halves[1], att_all[f, :, cols : 2 * cols], preferred_element_type=full)
        projected_ref[f] = (out + bias_ref[pl.ds(f, 1), :cols]).astype(low)
        store(att_all.at[f], qkv_hbm.at[f])
        if step in (2, 3, 4, 6):
            follow(1, {2: 1, 3: 2, 4: 3, 6: 5}[step])
        if step in (3, 5):
            follow(2, {3: 1, 5: 2}[step])

    allowed = lax.broadcasted_iota(jnp.int32, (slots, slots), 1) < count_ref[0]
    factor = 1.0 / math.sqrt(size)
    for h in range(heads):
        q, k, v = [
            projected_ref[f, :, j * size : (j + 1) * size]
            for f, j in (
                ((kind * heads + h) // heads_per, (kind * heads + h) % heads_per)
                for kind in range(3)
            )
        ]
        scores = contract(q, k, (1,), (1,)) * factor
        scores = jnp.where(allowed, scores, negative)
        exponent = jnp.exp(scores - jnp.max(scores, axis=-1, keepdims=True))
        softmax = exponent / jnp.sum(exponent, axis=-1, keepdims=True)
        mix = jnp.dot(softmax.astype(low), v, preferred_element_type=full).astype(low)
        pair, side = h // 2, h % 2
        start = ((pair % 2) * n_dp + pair // 2) * half_rows + side * size
        mixed_ref[:, start : start + size] = mix
        start = (pair % 2) * half_rows + side * size
        mixed_rows[pair // 2, :, start : start + size] = mix
        if h == 8:
            follow(2, 3)

    store(projected_ref, projected_hbm)
    for f in range(n_fs):
        for part in range(2):
            proj_dense[
                part * n_dp * half_rows : (part + 1) * n_dp * half_rows,
                f * width : (f + 1) * width,
            ] = att_all[f, :, 2 * cols + part * width : 2 * cols + (part + 1) * width]
    attended = (
        jnp.dot(mixed_ref[...], proj_dense[...], preferred_element_type=full) + bias_ref[8:9, :]
    )
    attended_ref[...] = attended
    middle = kept + mods[2] * attended
    normed_two, _ = normed(middle)
    hidden_all[0] = (normed_two * (1.0 + mods[4]) + mods[3]).astype(low)
    spread_step(hidden_all, 1, 2)
    store(hidden_all.at[0], hidden_hbm.at[0])
    store(proj_dense, proj_hbm)
    follow(2, 5)
    spread_wait(branch_all, 0, [2])
    spread_step(branch_all, 0, 1)
    spread_wait(hidden_all, 1, [2])
    spread_step(hidden_all, 1, 1)
    for step in (4, 6, 7):
        arrive(1, 0, order[step])
    keep_one.wait()
    store(one_all, one_hbm)
    spread_wait(branch_all, 0, [1, 3])
    spread_wait(hidden_all, 1, [1, 3])
    for key in (1, 2, 3):
        store(hidden_all.at[key], hidden_hbm.at[key])
        store(branch_all.at[key], branch_hbm.at[key])
    for step in (4, 6, 7):
        arrive(2, 0, order[step])
    keep_two.wait()
    store(two_all, two_hbm)
    for copy in started:
        copy.wait_send()

    @pl.when(in_middle)
    def _():
        for copy in middle_copies:
            copy.wait_send()

    for copy in stores:
        copy.wait()


def forward_kernel(notes, ada, one, two, qkv, proj, patches, index, cot, count, widths):
    n_dp, n_fs = lax.axis_size("dp"), lax.axis_size("fsdp")
    slots, features = cot.shape
    unit = features // n_fs
    size = features // HEADS
    half_rows = qkv.shape[0] // 2
    cols = qkv.shape[1]
    pieces = (n_dp, unit, 4 * half_rows)
    n_all = n_dp * n_fs
    low, full = jnp.bfloat16, jnp.float32
    vmem = pl.BlockSpec(memory_space=pltpu.VMEM)
    image = (slots, features)
    shapes = [
        ((n_fs, n_dp * half_rows, 2 * (cols + unit)), low),
        ((n_fs * unit, features), low),
        ((features, n_fs * unit), low),
        ((n_fs, slots, cols), low),
        ((n_dp,) + image, low),
        ((n_dp,) + image, low),
        ((features, features), low),
        (image, full),
        ((n_dp, slots, 2 * half_rows), low),
        ((n_dp, slots, 2 * half_rows), low),
        ((8, features), full),
        ((16, features), full),
        ((n_all, 2 * half_rows), low),
        (image, full),
    ]
    scratch = shapes[:7] + [
        (image, low),
        (pieces, low),
        ((unit, features), low),
        ((unit, features), low),
        ((n_all, 8, 128), full),
        ((n_all, 8, 128), full),
        ((n_all, 8, 128), full),
        ((half_rows, 2 * (cols + unit)), low),
        (pieces, low),
    ]
    dma = pltpu.SemaphoreType.DMA
    return pl.pallas_call(
        functools.partial(forward_body, (HEADS, size, widths)),
        out_shape=[jax.ShapeDtypeStruct(shape, kind) for shape, kind in shapes],
        in_specs=[vmem] * 9 + [pl.BlockSpec(memory_space=pltpu.SMEM)],
        out_specs=[pl.BlockSpec(memory_space=pl.ANY)] * 7 + [vmem] * 7,
        scratch_shapes=[pltpu.VMEM(shape, kind) for shape, kind in scratch]
        + [dma((2, n_all - 1)), dma((2, n_all - 1)), dma((3, 5)), dma((3, 4))]
        + [dma((1, 3, n_fs)), dma((3, n_dp, n_fs)), dma((3, 4)), dma((3, 4)), dma((5,))]
        + [dma((24,))],
        compiler_params=pltpu.CompilerParams(
            collective_id=5, has_side_effects=True, vmem_limit_bytes=64 * 1024 * 1024 - 65536
        ),
        name="forward",
    )(notes, ada, one, two, qkv, proj, patches, index, cot, count)


def gelu_parts(raised):
    square = raised * raised
    inner = 0.7978845608028654 * raised * (1.0 + 0.044715 * square)
    bend = jnp.tanh(inner)
    slope = 0.7978845608028654 * (1.0 + 3.0 * 0.044715 * square)
    half = 0.5 * (1.0 + bend)
    return raised * half, half + 0.5 * raised * (1.0 - bend * bend) * slope


def column_sums(value):
    return jnp.sum(value, axis=0, keepdims=True)


def store_tile(ref, index, line):
    for row in range(8):
        piece = line[:, row * 128 : (row + 1) * 128]
        if piece.shape[1] == 0:
            break
        if piece.shape[1] < 128:
            rest = jnp.zeros((1, 128 - piece.shape[1]), line.dtype)
            piece = jnp.concatenate([piece, rest], axis=1)
        ref[index, row : row + 1, :] = piece


def backward_body(
    sizes,
    qkv_hbm,
    one_hbm,
    two_hbm,
    projected_hbm,
    hidden_hbm,
    branch_hbm,
    proj_hbm,
    hidden_rows,
    mixed_rows,
    ada_ref,
    signal_ref,
    attended_ref,
    kept_ref,
    mod_ref,
    bias_ref,
    index_ref,
    cot_ref,
    count_ref,
    block_ref,
    patch_out,
    qkv_out,
    proj_out,
    one_out,
    two_out,
    ada_out,
    last_got,
    mlp_out,
    one_ref,
    two_ref,
    projected_ref,
    hidden_all,
    branch_all,
    proj_ref,
    act_ref,
    d_raised_ref,
    part_ref,
    core_got,
    cross_put,
    cross_got,
    grads,
    got_y,
    got_z,
    rows_got,
    d_att_all,
    d_mixed_ref,
    d_proj_all,
    weight_ring,
    mlp_put,
    d_mod_ref,
    sum_put,
    sum_got,
    note_put,
    note_got,
    last_put,
    send_m,
    recv_m,
    send_d,
    recv_d,
    send_e,
    recv_e,
    send_p,
    recv_p,
    send_n,
    recv_n,
    send_s,
    recv_s,
    send_b,
    recv_b,
    local,
    load_sem,
):
    heads, size, ada_width = sizes
    n_dp, n_fs = 4, 8
    d_at, f_at = lax.axis_index("dp"), lax.axis_index("fsdp")
    own_at = d_at * n_fs + f_at
    slots, features = kept_ref.shape
    cols = projected_ref.shape[2]
    heads_per = cols // size
    row_width = features // n_dp
    half_rows = row_width // 2
    unit = features // n_fs
    low = jnp.bfloat16
    full = jnp.float32
    core, cross, near = (d_at ^ 1, f_at), (d_at ^ 2, f_at), (d_at, f_at ^ 1)
    loads = [
        pltpu.make_async_copy(source, target, load_sem.at[place])
        for place, (source, target) in enumerate(
            [
                (hidden_hbm, hidden_all),
                (one_hbm, one_ref),
                (branch_hbm, branch_all),
                (two_hbm, two_ref),
                (proj_hbm, proj_ref),
                (projected_hbm, projected_ref),
            ]
        )
    ]
    for load in loads:
        load.start()
    others = [(a, b) for a in range(n_dp) for b in range(n_fs) if a or b]
    greet([(d_at ^ a, f_at ^ b) for a, b in others])
    sent = []

    def push(source, target, send, recv, device):
        copy = remote(source, target, send, recv, device)
        copy.start()
        sent.append(copy)
        return copy

    def arrive(place, recv):
        pltpu.make_async_copy(place, place, recv).wait()

    stays = []
    for kind, source in enumerate((hidden_rows, mixed_rows)):
        for mask in (2, 3, 1):
            push(
                source.at[d_at ^ mask],
                rows_got.at[kind, mask],
                send_p.at[kind, mask],
                recv_p.at[kind, mask],
                (d_at ^ mask, f_at),
            )
        stays.append(
            pltpu.make_async_copy(source.at[d_at], rows_got.at[kind, 0], local.at[kind])
        )
        stays[kind].start()

    def image_step(image, carry):
        raised = contract(hidden_all[image], one_ref[...], (1,), (1,)) + bias_ref[10:11, :]
        active, slope = gelu_parts(raised)
        act_ref[image] = active.astype(low)
        coarse = raised.astype(low)
        d_raised_ref[image] = coarse
        part_ref[image] = (raised - coarse.astype(full)).astype(low)
        return carry

    def back_step(image, carry):
        raised = d_raised_ref[image].astype(full) + part_ref[image].astype(full)
        active, slope = gelu_parts(raised)
        d_active = jnp.dot(branch_all[image], two_ref[...], preferred_element_type=full)
        d_raised_ref[image] = (d_active * slope).astype(low)
        return carry

    for load in loads[:3]:
        load.wait()
    lax.fori_loop(0, n_dp, image_step, 0)

    def flat(ref, start, count):
        return ref[:, :, pl.ds(start, count)].reshape(n_dp * slots, count)

    def weight_grad(kind, left, right):
        step = features // 3
        for part in range(3):
            grads[kind, part * step : (part + 1) * step, :] = rows_rows(
                flat(left, part * step, step), flat(right, 0, features)
            ).astype(low)

    def block_rows(index):
        return pl.ds(pl.multiple_of(index * unit, 16), unit)

    def send_block(kind, place, index):
        push(
            grads.at[kind, block_rows(index), :],
            got_y.at[kind, place],
            send_m.at[kind, place],
            recv_m.at[kind, place],
            near,
        )

    def fold_block(kind, place, index):
        arrive(got_y.at[kind, place], recv_m.at[kind, place])
        rows = block_rows(index)
        grads[kind, rows, :] = (
            grads[kind, rows, :].astype(full) + got_y[kind, place].astype(full)
        ).astype(low)

    def send_wide(kind, index, mask):
        place = mask // 2 - 1
        return remote(
            grads.at[kind, block_rows(index), :],
            got_z.at[kind, place],
            send_m.at[kind, 4 + place],
            recv_m.at[kind, 4 + place],
            (d_at, index),
        )

    waves = (2, 4, 6, 0)

    def fold_wave(kind, place):
        fold_block(kind, place, f_at ^ waves[place])
        if waves[place]:
            copy = send_wide(kind, f_at ^ waves[place], waves[place])
            copy.start()
            sent.append(copy)

    def finish(kind):
        total = grads[kind, block_rows(f_at), :].astype(full)
        for place in range(3):
            arrive(got_z.at[kind, place], recv_m.at[kind, 4 + place])
            total = total + got_z[kind, place].astype(full)
        return total

    weight_grad(1, branch_all, act_ref)
    for place, wide in enumerate((2, 4, 6, 0)):
        send_block(1, place, f_at ^ wide ^ 1)
    loads[3].wait()
    lax.fori_loop(0, n_dp, back_step, 0)

    def part_step(left, right, dims):
        def step(image, carry):
            part_ref[image] = contract(left[image], right[...], (1,), dims).astype(low)
            return carry

        lax.fori_loop(0, n_dp, step, 0)

    def core_send(kind):
        return [
            push(
                part_ref.at[image],
                core_got.at[kind, place],
                send_d.at[kind, place],
                recv_d.at[kind, place],
                core,
            )
            for place, image in enumerate((3, 1))
        ]

    def cross_send(kind):
        arrive(core_got.at[kind, 0], recv_d.at[kind, 0])
        cross_put[kind] = (
            part_ref[2].astype(full) + core_got[kind, 0].astype(full)
        ).astype(low)
        push(
            cross_put.at[kind], cross_got.at[kind], send_d.at[kind, 2], recv_d.at[kind, 2], cross
        )
        arrive(core_got.at[kind, 1], recv_d.at[kind, 1])

    part_step(d_raised_ref, one_ref, (0,))
    leaving = core_send(0)
    cross_send(0)
    own_part = part_ref[0].astype(full) + core_got[0, 1].astype(full)
    weight_grad(0, d_raised_ref, hidden_all)
    for place, wide in enumerate((2, 4, 6, 0)):
        send_block(0, place, f_at ^ wide ^ 1)
    for copy in leaving:
        copy.wait_send()
    part_step(act_ref, two_ref, (1,))
    core_send(1)
    cross_send(1)
    fold_wave(1, 0)
    one_sum = jnp.zeros((1, features), full)
    for image in range(n_dp):
        one_sum = one_sum + column_sums(d_raised_ref[image].astype(full))
    branch_sum = column_sums(branch_all[0].astype(full))

    mods = [mod_ref[row : row + 1, :] for row in range(6)]
    kept = kept_ref[...]
    attended = attended_ref[...]
    middle = kept + mods[2] * attended
    normed_two, rstd_two = normed(middle)
    upstream = cot_ref[...].astype(full)
    fold_wave(1, 1)
    loads[4].wait()
    arrive(cross_got.at[0], recv_d.at[0, 2])
    d_hidden_two = own_part + cross_got[0].astype(full)
    d_mod_ref[3:4, :] = column_sums(d_hidden_two)
    d_mod_ref[4:5, :] = column_sums(d_hidden_two * normed_two)
    d_middle = upstream + norm_back(d_hidden_two * (1.0 + mods[4]), normed_two, rstd_two)
    d_mod_ref[2:3, :] = column_sums(d_middle * attended)
    d_attended = (mods[2] * d_middle).astype(low)
    d_att_all[0] = d_attended
    patch_out[:slots, :] = d_middle
    att_sum = column_sums(d_attended.astype(full))
    d_mixed_ref[...] = contract(d_attended, proj_ref[...], (1,), (1,)).astype(low)
    push(d_att_all.at[0], d_att_all.at[2], send_e.at[2], recv_e.at[2], cross)
    push(d_att_all.at[0], d_att_all.at[1], send_e.at[1], recv_e.at[1], core)

    fold_wave(1, 2)
    loads[5].wait()

    leaps = (3, 2, 1, 0)
    turn = [(f_at // 2) ^ leap for leap in leaps]

    def pass_pair(place):
        push(
            d_proj_all.at[0, turn[place]],
            d_proj_all.at[2, turn[place]],
            send_p.at[2 + place, 2],
            recv_p.at[2 + place, 2],
            cross,
        )
        push(
            d_proj_all.at[0, turn[place]],
            d_proj_all.at[1, turn[place]],
            send_p.at[2 + place, 1],
            recv_p.at[2 + place, 1],
            core,
        )

    def relay_pair(place):
        arrive(d_proj_all.at[2, turn[place]], recv_p.at[2 + place, 2])
        push(
            d_proj_all.at[2, turn[place]],
            d_proj_all.at[3, turn[place]],
            send_p.at[2 + place, 3],
            recv_p.at[2 + place, 3],
            core,
        )

    allowed = lax.broadcasted_iota(jnp.int32, (slots, slots), 1) < count_ref[0]
    factor = 1.0 / math.sqrt(size)
    for h in range(heads):
        places = [
            ((kind * heads + h) // heads_per, (kind * heads + h) % heads_per)
            for kind in range(3)
        ]
        q, k, v = [projected_ref[f, :, j * size : (j + 1) * size] for f, j in places]
        pair, side = h // 2, h % 2
        start = ((pair % 2) * n_dp + pair // 2) * half_rows + side * size
        d_mix = d_mixed_ref[:, start : start + size]
        scores = contract(q, k, (1,), (1,)) * factor
        scores = jnp.where(allowed, scores, negative)
        exponent = jnp.exp(scores - jnp.max(scores, axis=-1, keepdims=True))
        softmax = exponent / jnp.sum(exponent, axis=-1, keepdims=True)
        d_softmax = contract(d_mix, v, (1,), (1,))
        delta = jnp.sum(d_softmax * softmax, axis=-1, keepdims=True)
        d_scores = (softmax * (d_softmax - delta)).astype(low)
        results = [
            jnp.dot(d_scores, k, preferred_element_type=full) * factor,
            rows_rows(d_scores, q) * factor,
            rows_rows(softmax.astype(low), d_mix),
        ]
        for (f, j), result in zip(places, results):
            start = (f % 2) * cols + j * size
            d_proj_all[0, f // 2, :, start : start + size] = result.astype(low)
    for place in range(4):
        pass_pair(place)
    fold_wave(1, 3)


    odd = f_at % 2

    def grad_pair(place):
        for mask in (1, 3):
            arrive(d_proj_all.at[mask, turn[place]], recv_p.at[2 + place, mask])
        result = rows_rows(
            rows_got[0].reshape(n_dp * slots, row_width),
            d_proj_all[:, turn[place]].reshape(n_dp * slots, 2 * cols),
        ).astype(low)
        for side in range(2):
            rows = block_rows(2 * turn[place] + side)
            for part in range(2):
                grads[2, rows, part * cols : (part + 1) * cols] = result[
                    part * half_rows : (part + 1) * half_rows, side * cols : (side + 1) * cols
                ]
        send_block(2, place, 2 * turn[place] + 1 - odd)

    def fold_pair(place):
        fold_block(2, place, 2 * turn[place] + odd)
        if leaps[place]:
            copy = send_wide(2, 2 * turn[place] + odd, 2 * leaps[place])
            copy.start()
            sent.append(copy)

    arrive(cross_got.at[1], recv_d.at[1, 2])
    branch = (
        part_ref[0].astype(full)
        + core_got[1, 1].astype(full)
        + cross_got[1].astype(full)
        + bias_ref[9:10, :]
    )
    d_mod_ref[5:6, :] = column_sums(upstream * branch)

    tall = weight_ring.shape[1]
    weights = [
        pltpu.make_async_copy(
            qkv_hbm.at[place // 2, pl.ds((place % 2) * tall, tall), :],
            weight_ring.at[place % 2],
            local.at[2 + place % 2],
        )
        for place in range(2 * n_fs)
    ]
    weights[0].start()
    quarters = [[jnp.zeros((slots, tall), full) for side in range(2)] for part in range(2)]
    for f in range(n_fs):
        own = d_proj_all[0, f // 2, :, (f % 2) * cols : (f % 2 + 1) * cols]
        for side in range(2):
            place = 2 * f + side
            if place + 1 < 2 * n_fs:
                weights[place + 1].start()
            weights[place].wait()
            for part in range(2):
                quarters[part][side] = quarters[part][side] + contract(
                    own, weight_ring[side, :, part * cols : (part + 1) * cols], (1,), (1,)
                )
        line = jnp.concatenate(
            [
                column_sums(own.astype(full)),
                att_sum[:, f * unit : (f + 1) * unit],
                branch_sum[:, f * unit : (f + 1) * unit],
                one_sum[:, f * unit : (f + 1) * unit],
            ],
            axis=1,
        )
        store_tile(sum_put, f, line)
    d_hidden_one = jnp.concatenate(
        [
            quarters[part][d // 2][:, (d % 2) * half_rows : (d % 2 + 1) * half_rows]
            for d in range(n_dp)
            for part in range(2)
        ],
        axis=1,
    )
    normed_one, rstd_one = normed(kept)
    d_mod_ref[0:1, :] = column_sums(d_hidden_one)
    d_mod_ref[1:2, :] = column_sums(d_hidden_one * normed_one)

    third = ada_width // 3
    pieces = []
    for row in range(6):
        line = d_mod_ref[row : row + 1, :].astype(low).astype(full)
        pieces += [line[:, step * third : (step + 1) * third] for step in range(n_dp)]
    for f in range(n_fs):
        store_tile(note_put, f, jnp.concatenate(pieces[3 * f : 3 * f + 3], axis=1))
    for mask in range(1, n_fs):
        push(
            sum_put.at[f_at ^ mask],
            sum_got.at[mask],
            send_s.at[mask],
            recv_s.at[mask],
            (d_at, f_at ^ mask),
        )
    for place, (a, b) in enumerate(others):
        push(
            note_put.at[f_at ^ b],
            note_got.at[own_at],
            send_n.at[0, place],
            recv_n.at[0, place],
            (d_at ^ a, f_at ^ b),
        )
    keep_note = pltpu.make_async_copy(note_put.at[f_at], note_got.at[own_at], local.at[4])
    keep_note.start()
    keep_sum = pltpu.make_async_copy(sum_put.at[f_at], sum_got.at[0], local.at[5])
    keep_sum.start()
    arrive(d_att_all.at[2], recv_e.at[2])
    push(d_att_all.at[2], d_att_all.at[3], send_e.at[3], recv_e.at[3], core)
    d_kept = patch_out[:slots, :] + norm_back(
        d_hidden_one * (1.0 + mods[1]), normed_one, rstd_one
    )
    chosen = lax.broadcasted_iota(jnp.int32, (patch_out.shape[0], slots), 0) == index_ref[...]
    chosen = chosen.astype(full).astype(low)
    left = d_kept
    spread_out = jnp.zeros(patch_out.shape, full)
    for step in range(3):
        part = left.astype(low)
        spread_out = spread_out + jnp.dot(chosen, part, preferred_element_type=full)
        left = left - part.astype(full)
    patch_out[...] = spread_out
    block_ref[...] = (middle + mods[5] * branch).astype(low)
    fold_wave(0, 0)
    for stay in stays:
        stay.wait()
    for kind in range(2):
        for mask in (2, 3, 1):
            arrive(rows_got.at[kind, mask], recv_p.at[kind, mask])
    for mask in (1, 3):
        arrive(d_att_all.at[mask], recv_e.at[mask])
    grad_proj = rows_rows(
        rows_got[1].reshape(n_dp * slots, row_width),
        d_att_all[...].reshape(n_dp * slots, features),
    ).astype(low)
    for f in range(n_fs):
        for part in range(2):
            grads[
                2,
                f * unit : (f + 1) * unit,
                2 * cols + part * unit : 2 * cols + (part + 1) * unit,
            ] = grad_proj[part * half_rows : (part + 1) * half_rows, f * unit : (f + 1) * unit]

    relay_pair(0)
    grad_pair(0)
    fold_wave(0, 1)

    relay_pair(1)
    grad_pair(1)
    fold_wave(0, 2)
    relay_pair(2)
    grad_pair(2)
    fold_wave(0, 3)
    fold_pair(0)

    keep_mlp = []

    def give_back(kind):
        total = finish(kind).astype(low)
        for d in range(n_dp):
            mlp_put[kind, d] = total[:, d * row_width : (d + 1) * row_width]
        for mask in (2, 3, 1):
            push(
                mlp_put.at[kind, d_at ^ mask],
                mlp_out.at[kind, d_at],
                send_b.at[kind, mask],
                recv_b.at[kind, mask],
                (d_at ^ mask, f_at),
            )
        keep_mlp.append(
            pltpu.make_async_copy(
                mlp_put.at[kind, d_at], mlp_out.at[kind, d_at], local.at[2 + kind]
            )
        )
        keep_mlp[-1].start()

    keep_note.wait()
    keep_sum.wait()
    for mask in range(1, n_fs):
        arrive(sum_got.at[mask], recv_s.at[mask])
    for place, (a, b) in enumerate(others):
        at = (d_at ^ a) * n_fs + (f_at ^ b)
        arrive(note_got.at[at], recv_n.at[0, place])
    sums = sum_got[0]
    for mask in range(1, n_fs):
        sums = sums + sum_got[mask]
    notes = note_got[...]
    all_d = jnp.concatenate([notes[:, row, :] for row in range(7)], axis=1)
    totals = column_sums(all_d)
    all_d = all_d.astype(low)
    all_d = all_d[:, :ada_width]
    terms = contract(all_d, ada_ref[...], (1,), (1,))
    sum_line = jnp.concatenate([sums[row : row + 1, :] for row in range(7)], axis=1)
    common = jnp.concatenate(
        [sum_line[:, :ada_width], totals[:, :ada_width], jnp.zeros((1, 32), full)], axis=1
    )
    lines = jnp.concatenate(
        [terms, jnp.broadcast_to(common, (n_dp * n_fs, common.shape[1]))], axis=1
    )
    for row in range(16):
        last_put[:, row, :] = lines[:, row * 128 : (row + 1) * 128]
    for place, (a, b) in enumerate(others):
        push(
            last_put.at[(d_at ^ a) * n_fs + (f_at ^ b)],
            last_got.at[own_at],
            send_n.at[1, place],
            recv_n.at[1, place],
            (d_at ^ a, f_at ^ b),
        )
    keep_last = pltpu.make_async_copy(last_put.at[own_at], last_got.at[own_at], local.at[0])
    keep_last.start()
    relay_pair(3)
    grad_pair(3)
    fold_pair(1)
    give_back(1)
    fold_pair(2)
    give_back(0)
    ada_out[...] = rows_rows(signal_ref[...], all_d)
    fold_pair(3)
    for kind in (1, 0):
        keep_mlp[1 - kind].wait()
        for mask in (1, 2, 3):
            arrive(mlp_out.at[kind, d_at ^ mask], recv_b.at[kind, mask])
    for d in range(n_dp):
        one_out[:, d * unit : (d + 1) * unit] = mlp_out[0, d].astype(full).T
        for e in range(2):
            start = (e * n_dp + d) * unit
            two_out[:, start : start + unit] = mlp_out[1, d, :, e * unit : (e + 1) * unit].astype(
                full
            )
    total = finish(2)
    for part in range(2):
        rows = slice(part * half_rows, (part + 1) * half_rows)
        qkv_out[rows, :] = total[:, part * cols : (part + 1) * cols]
        start = 2 * cols + part * unit
        proj_out[:, rows] = total[:, start : start + unit].T
    keep_last.wait()
    for place, (a, b) in enumerate(others):
        at = (d_at ^ a) * n_fs + (f_at ^ b)
        arrive(last_got.at[at], recv_n.at[1, place])
    for copy in sent:
        if not any(copy is gone for gone in leaving):
            copy.wait_send()


def backward_kernel(forward, ada, index, patches, cot, count):
    (
        qkv_all,
        one_all,
        two_all,
        projected,
        hidden_all,
        branch_all,
        proj_dense,
        attended,
        hidden_rows,
        mixed_rows,
        mods,
        bias,
        signals,
        kept,
    ) = forward
    n_dp, n_fs = lax.axis_size("dp"), lax.axis_size("fsdp")
    n_all = n_dp * n_fs
    slots, features = kept.shape
    row_width = features // n_dp
    unit = features // n_fs
    ada_width = 6 * features // n_fs
    cols = projected.shape[2]
    low, full = jnp.bfloat16, jnp.float32
    vmem = pl.BlockSpec(memory_space=pltpu.VMEM)
    anywhere = pl.BlockSpec(memory_space=pl.ANY)
    image = (slots, features)
    shapes = [
        (image, low),
        (patches, full),
        ((row_width, cols), full),
        ((unit, row_width), full),
        ((row_width, n_dp * unit), full),
        ((unit, features), full),
        ((row_width, ada_width), full),
        ((n_all, 16, 128), full),
    ]
    scratch = [
        ((2, n_dp, unit, row_width), low),
        (one_all.shape, low),
        (two_all.shape, low),
        (projected.shape, low),
        ((n_dp,) + image, low),
        ((n_dp,) + image, low),
        (proj_dense.shape, low),
        ((n_dp,) + image, low),
        ((n_dp,) + image, low),
        ((n_dp,) + image, low),
        ((2, 2) + image, low),
        ((2,) + image, low),
        ((2,) + image, low),
        ((3, features, features), low),
        ((3, 4, unit, features), low),
        ((3, 3, unit, features), low),
        ((2, n_dp, slots, row_width), low),
        ((n_dp,) + image, low),
        (image, low),
        ((n_dp, n_fs // 2, slots, 2 * cols), low),
        ((2, qkv_all.shape[1] // 2, qkv_all.shape[2]), low),
        ((2, n_dp, unit, row_width), low),
        ((8, features), full),
        ((n_fs, 8, 128), full),
        ((n_fs, 8, 128), full),
        ((n_fs, 8, 128), full),
        ((n_all, 8, 128), full),
        ((n_all, 16, 128), full),
    ]
    dma = pltpu.SemaphoreType.DMA
    sems = [(3, 7), (2, 3), (4,), (2 + n_fs // 2, 4), (2, n_all - 1), (n_fs,), (2, 4)]
    return pl.pallas_call(
        functools.partial(backward_body, (HEADS, features // HEADS, ada_width)),
        out_shape=[jax.ShapeDtypeStruct(shape, kind) for shape, kind in shapes],
        in_specs=[anywhere] * 9
        + [vmem] * 8
        + [pl.BlockSpec(memory_space=pltpu.SMEM)],
        out_specs=[vmem] * len(shapes),
        scratch_shapes=[pltpu.VMEM(shape, kind) for shape, kind in scratch]
        + [dma(shape) for shape in sems for side in range(2)]
        + [dma((6,)), dma((6,))],
        compiler_params=pltpu.CompilerParams(
            collective_id=6, has_side_effects=True, vmem_limit_bytes=64 * 1024 * 1024 - 65536
        ),
        name="backward",
    )(
        qkv_all,
        one_all,
        two_all,
        projected,
        hidden_all,
        branch_all,
        proj_dense,
        hidden_rows,
        mixed_rows,
        ada,
        signals,
        attended,
        kept,
        mods,
        bias,
        index,
        cot,
        count,
    )


def shards(
    patches_in,
    condition,
    keep_count,
    keep_index,
    w_ada,
    b_ada,
    w_qkv,
    qv_bias,
    w_proj,
    w_fc1,
    fc1_bias,
    w_fc2,
    out_bias,
    cotangent,
):
    n_dp, n_fs = lax.axis_size("dp"), lax.axis_size("fsdp")
    n_all = n_dp * n_fs
    d_at, f_at = lax.axis_index("dp"), lax.axis_index("fsdp")
    features = patches_in.shape[2]
    row_width = features // n_dp
    half_rows = row_width // 2
    low = jnp.bfloat16
    full = jnp.float32

    cond_float = condition.astype(full)
    signal = swish(cond_float).astype(low).astype(full)
    shards_bias = [b_ada, qv_bias, fc1_bias, out_bias]
    biases = jnp.concatenate(shards_bias).astype(full)
    notes = jnp.concatenate(
        [
            jnp.pad(signal.reshape(n_dp, row_width), ((0, 0), (0, 384 - row_width))),
            jnp.broadcast_to(jnp.pad(biases, (0, 640 - biases.shape[0])), (n_dp, 640)),
        ],
        axis=1,
    ).reshape(n_dp, 8, 128)
    ada_width = w_ada.shape[1]
    unit_width = w_fc1.shape[1] // n_dp
    index = keep_index.reshape(1, -1)
    patches = patches_in.reshape(patches_in.shape[1:])
    upstream = cotangent.reshape(cotangent.shape[1:])
    forward = forward_kernel(
        notes,
        w_ada,
        w_fc1,
        w_fc2.T,
        w_qkv,
        w_proj.T,
        patches,
        index,
        upstream,
        keep_count,
        (ada_width, qv_bias.shape[0], fc1_bias.shape[0], out_bias.shape[0]),
    )
    block_out, grad_patches, qkv_out, proj_out, one_out, two_out, grad_ada, last = (
        backward_kernel(forward, w_ada, index, patches.shape, upstream, keep_count)
    )
    qkv_cols, proj_cols = w_qkv.shape[1], w_proj.shape[1]

    groups = last[:, :3, :].reshape(n_dp, n_fs, 3, 128).sum(axis=1)
    d_signal = groups.reshape(n_dp, 384)[:, :row_width].reshape(1, features)
    unused, swish_pull = jax.vjp(swish, cond_float)
    grad_condition = swish_pull(d_signal)[0]
    own = d_at * n_fs + f_at
    head_size = qv_bias.shape[0]
    heads_per = qkv_cols // head_size

    def line_of(kind, d, f):
        source = lax.dynamic_slice_in_dim(last, d * n_fs + f, 1, 0).reshape(-1)
        start = row_width + kind * ada_width
        return source[start : start + ada_width]

    def summed(f):
        return sum(line_of(0, d, f) for d in range(n_dp))

    ada_count = b_ada.shape[0]
    ada_bias = lax.dynamic_slice_in_dim(
        line_of(1, d_at, own // n_dp), (own % n_dp) * ada_count, ada_count
    )
    block = jnp.where(own < HEADS, own, own + HEADS)
    qv_out = lax.dynamic_slice_in_dim(
        summed(block // heads_per), (block % heads_per) * head_size, head_size
    )
    per = proj_cols // head_size
    place = own % HEADS
    start = jnp.where(own < HEADS, qkv_cols, qkv_cols + proj_cols) + (place % per) * head_size
    out_out = lax.dynamic_slice_in_dim(summed(place // per), start, head_size)
    bias_out = lax.dynamic_slice_in_dim(
        line_of(0, own % n_dp, own // n_dp), qkv_cols + 2 * proj_cols, unit_width
    )
    return (
        block_out[None],
        grad_patches[None],
        grad_condition,
        grad_ada,
        ada_bias,
        qkv_out,
        qv_out,
        proj_out.T,
        one_out,
        bias_out,
        two_out.T,
        out_out,
    )


def kernels_fit(*arrays):
    w_qkv, w_fc1 = arrays[6], arrays[9]
    features = arrays[0].shape[2]
    unit_width = w_fc1.shape[1] // lax.axis_size("dp")
    return (
        w_qkv.shape[1] % (features // HEADS) == 0
        and w_qkv.shape[0] % 16 == 0
        and unit_width % 16 == 0
        and unit_width == arrays[11].shape[1]
        and lax.axis_size("dp") == 4
        and lax.axis_size("fsdp") == 8
    )


def solution(mesh):
    both = ("dp", "fsdp")
    weight = P("dp", "fsdp")
    flat = P(both)
    placed = (
        P(both, None, None),
        P(both, None),
        flat,
        P(both, None),
        weight,
        flat,
        weight,
        flat,
        weight,
        weight,
        flat,
        weight,
        flat,
        P(both, None, None),
    )

    def chosen(*arrays):
        return (shards if kernels_fit(*arrays) else plain_shards)(*arrays)

    return jax.shard_map(
        chosen,
        mesh=mesh,
        in_specs=placed,
        out_specs=(
            P(both, None, None),
            P(both, None, None),
            P(both, None),
            weight,
            flat,
            weight,
            flat,
            weight,
            weight,
            flat,
            weight,
            flat,
        ),
        check_vma=False,
    )
```
